32 devices in a mesh: dp: 8 (over y, x, core), head: 4 (over z).
Axes of the slice: x: 2, y: 2, z: 4, core: 2. Of those that a mesh axis runs over, the one named last changes fastest.
Arguments:
- block_in: float32 [4096, 768], P(('dp', 'head')), may hold values from -6 to 6
- first_gain: float32 [768], replicated, may hold values from 0.25 to 1.75
- first_bias: float32 [768], replicated, may hold values from -1 to 1
- qkv_weight: bfloat16 [3, 768, 768], P(None, None, 'head'), may hold values from -0.21875 to 0.21875
- out_weight: bfloat16 [768, 768], P('head'), may hold values from -0.875 to 0.875
- second_gain: float32 [768], replicated, may hold values from 0.25 to 1.75
- second_bias: float32 [768], replicated, may hold values from -1 to 1
- router_weight: bfloat16 [768, 16], replicated, may hold values from -0.15625 to 0.15625
- frozen_in: bfloat16 [8, 768, 3072], P('dp', None, 'head'), may hold values from -0.21875 to 0.21875
- frozen_out: bfloat16 [8, 3072, 768], P('dp', 'head'), may hold values from -0.21875 to 0.21875
- train_in: bfloat16 [8, 768, 3072], P('dp', None, 'head'), may hold values from -0.21875 to 0.21875
- train_out: bfloat16 [8, 3072, 768], P('dp', 'head'), may hold values from -0.21875 to 0.21875
- routes: int32 [4096, 2], P(('dp', 'head')), may hold values from 0 to 15, all different within a row; in each aligned block of 128 rows (0 to 127, 128 to 255, ...) at most 40 rows name the same one
- seq_ids: int32 [4096], P('dp'), may hold values from 0 to 1, as said below
- cotangent: float32 [4096, 768], P(('dp', 'head')), may hold values from -6 to 6
Outputs:
- block_out: float32 [4096, 768], P(('dp', 'head'))
- input_grad: float32 [4096, 768], P(('dp', 'head'))
- grad_first_gain: float32 [768], replicated
- grad_first_bias: float32 [768], replicated
- grad_qkv: float32 [3, 768, 768], P(None, None, 'head')
- grad_out: float32 [768, 768], P('head')
- grad_second_gain: float32 [768], replicated
- grad_second_bias: float32 [768], replicated
- grad_router: float32 [768, 16], replicated
- grad_train_in: float32 [8, 768, 3072], P('dp', None, 'head')
- grad_train_out: float32 [8, 3072, 768], P('dp', 'head')
The draws below stay inside these ranges and needn't reach their ends.
Inputs may be any that keep to these rules, and one draw needn't show every extreme that they name: `routes`: each row names two different experts; among the rows of one device (aligned blocks of 128 tokens) no expert is named more than 2 * 20 times. `seq_ids`: each aligned block of 512 tokens holds either one sequence (all 0) or two of 256 tokens (0, then 1); exactly half of the blocks hold one sequence.
All inputs are finite; a program needn't handle non-finite values.
Results may differ from the reference program's by a relative error of at most 0.017.
Values may be sent and summed in bfloat16 or wider, within the bound.
A program may use at most 128 MiB of HBM per device.

```python
import math
from functools import partial
import jax
import jax.numpy as jnp
import numpy as np
from jax import lax

D = 768
HEADS = 12
HEAD_DIM = 64
FF = 3072
SEQ = 512
TOK_DEV = 512
ROWS = 128
TOKENS = 4096
EXPERTS = 16
FROZEN = 8
CAP = 20


def draw_seq_ids(key, part):
    row_total = TOKENS // TOK_DEV
    order = jax.random.permutation(key, row_total)
    single = order < row_total // 2
    positions = jnp.arange(TOK_DEV, dtype=jnp.int32)
    later_half = (positions >= SEQ // 2).astype(jnp.int32)
    group_ids = jnp.where(single[:, None], 0, later_half[None, :])
    return group_ids.reshape(TOKENS).astype(jnp.int32)


def shard_levels(own_key, extent, split, low, largest):
    level, own = 1.0, jax.random.fold_in(own_key, 6)
    for position, shards_of in split:
        draws = jnp.exp(jax.random.uniform(jax.random.fold_in(own, position), (shards_of,), jnp.float32, low / len(split), largest / len(split)))
        level = level * jnp.repeat(draws, extent[position] // shards_of).reshape([-1 if axis == position else 1 for axis in range(len(extent))])
    return level


def shared_out(rng, own, number, rows, count, top, reach, slope):
    ranking = jax.random.permutation(rng, count)
    crowded, usual = load_shares(count, rows * top, reach, slope, True), load_shares(count, rows * top, reach, slope, False)
    places = jnp.arange(count)

    def named(tallies, turn):
        used = int((tallies > 0).sum())
        fixed = max(1, used // 4)
        shifted = fixed + (places - fixed + turn * (used - fixed)) % max(1, count - fixed)
        return jnp.zeros((count,), jnp.int32).at[ranking[jnp.where(places < fixed, places, shifted)]].set(jnp.asarray(tallies, jnp.int32))

    tallies = jnp.where(number % 4 == 0, named(crowded, number // 4), named(usual, number - number // 4 - 1))
    mixed = jax.random.permutation(jax.random.fold_in(own, 3), count)
    source_of, sink = mixed[0:count // 2 * 2:2], mixed[1:count // 2 * 2:2]
    room = jnp.minimum(tallies[source_of] - 1, reach - tallies[sink]) // 2
    room = jnp.where((source_of == ranking[0]) | (sink == ranking[0]) | (tallies[sink] == 0), 0, jnp.maximum(room, 0))
    shifted = jax.random.randint(jax.random.fold_in(own, 4), (count // 2,), 0, 1 << 20) % (room + 1)
    tallies = tallies.at[source_of].add(-shifted).at[sink].add(shifted)
    items = jnp.searchsorted(jnp.cumsum(tallies), jnp.arange(rows * top), side="right").astype(jnp.int32)
    table = items.reshape(top, rows).T
    table = table[jax.random.permutation(jax.random.fold_in(own, 1), rows)]
    turn = jax.random.randint(jax.random.fold_in(own, 2), (rows, 1), 0, top)
    return jnp.take_along_axis(table, (jnp.arange(top)[None, :] + turn) % top, axis=1)


def load_shares(number_of, total, most, slope, full):
    weights = [(1 << 20) // math.isqrt(grade ** slope) + 1 for grade in range(1, number_of + 1)]
    largest = most if full else min(most, max(-(-total // number_of), total * weights[0] // sum(weights)))
    least = 1 if total - largest >= number_of - 1 else 0
    counts, rest = [largest] + [least] * (number_of - 1), total - largest - least * (number_of - 1)
    while rest > 0:
        candidates = [i for i in range(1, number_of) if counts[i] < largest] or [i for i in range(1, number_of) if counts[i] < most]
        mass, budget = sum([weights[i] for i in candidates]), rest
        for i in candidates:
            addition = min(most - counts[i], max(1, budget * weights[i] // mass), rest)
            counts[i] = counts[i] + addition
            rest = rest - addition
    return np.array(counts)


def scatter_about(key, extent, width, reach, cuts=(), kind=jnp.bfloat16):
    entries = width * jax.random.normal(key, extent, jnp.float32)
    if cuts:
        entries = entries * shard_levels(key, extent, cuts, -0.22, 0.18)
    return jnp.clip(entries, -reach, reach).astype(kind)


def setup_inputs(seed: int = 0) -> dict:
    splits = jax.random.split(jax.random.key(seed), 16)
    block_in = scatter_about(splits[0], (TOKENS, D), 1.0, 6.0, ((0, 32),), jnp.float32)
    first_gain = jnp.clip(1.0 + 0.15 * jax.random.normal(splits[1], (D,), jnp.float32), 0.25, 1.75)
    first_bias = scatter_about(splits[2], (D,), 0.2, 1.0, (), jnp.float32)
    qkv_weight = scatter_about(splits[3], (3, D, D), D ** -0.5, 0.21875, ((2, 4),))
    out_weight = scatter_about(splits[4], (D, D), (D // 16) ** -0.5, 0.875, ((0, 4),))
    second_gain = jnp.clip(1.0 + 0.15 * jax.random.normal(splits[5], (D,), jnp.float32), 0.25, 1.75)
    second_bias = scatter_about(splits[6], (D,), 0.2, 1.0, (), jnp.float32)
    router_weight = scatter_about(splits[7], (D, EXPERTS), (2 * D) ** -0.5, 0.15625)
    frozen_in = scatter_about(splits[8], (FROZEN, D, FF), D ** -0.5, 0.21875, ((0, 8), (2, 4)))
    frozen_out = scatter_about(splits[9], (FROZEN, FF, D), (FF // 4) ** -0.5, 0.21875, ((0, 8), (1, 4)))
    train_in = scatter_about(splits[10], (EXPERTS - FROZEN, D, FF), D ** -0.5, 0.21875, ((0, 8), (2, 4)))
    train_out = scatter_about(splits[11], (EXPERTS - FROZEN, FF, D), (FF // 4) ** -0.5, 0.21875, ((0, 8), (1, 4)))
    routes_keys = jax.random.split(jax.random.fold_in(splits[12], 1), TOKENS // ROWS)
    routes_turns = jax.random.permutation(jax.random.fold_in(splits[12], 3), TOKENS // ROWS)
    routes = jax.vmap(lambda own, number: shared_out(jax.random.fold_in(splits[12], 2), own, number, ROWS, EXPERTS, 2, 2 * CAP, 1))(routes_keys, routes_turns).reshape((TOKENS, 2))
    seq_ids = draw_seq_ids(jax.random.fold_in(splits[15], 71), 0)
    cotangent = scatter_about(splits[14], (TOKENS, D), 1.0, 6.0, ((0, 32),), jnp.float32)
    return {"block_in": block_in, "first_gain": first_gain, "first_bias": first_bias, "qkv_weight": qkv_weight, "out_weight": out_weight, "second_gain": second_gain, "second_bias": second_bias, "router_weight": router_weight, "frozen_in": frozen_in, "frozen_out": frozen_out, "train_in": train_in, "train_out": train_out, "routes": routes, "seq_ids": seq_ids, "cotangent": cotangent}


EPS = 1e-05
HIGH = lax.Precision.HIGHEST

@jax.custom_vjp
def low(v):
    return lax.optimization_barrier(v.astype(jnp.bfloat16)).astype(jnp.float32)

@jax.custom_vjp
def low_back(v):
    return v

def low_keep(v):
    return (low(v), None)

def low_pass(kept, grad):
    return (grad,)

def back_keep(v):
    return (v, None)

def back_low(kept, grad):
    return (low(grad),)
low.defvjp(low_keep, low_pass)
low_back.defvjp(back_keep, back_low)

def layer_norm(values, gain_vec, bias_vec):
    average = lax.optimization_barrier(jnp.mean(values, axis=-1, keepdims=True))
    centred = values - average
    variance = lax.optimization_barrier(jnp.mean(centred * centred, axis=-1, keepdims=True))
    return centred * lax.rsqrt(variance + EPS) * gain_vec + bias_vec

def row_attention(queries, keys_row, values_row, group_row):
    scores = jnp.einsum('qhd,khd->hqk', queries, keys_row, precision=HIGH) * HEAD_DIM ** (-0.5)
    scores = low_back(scores)
    positions = jnp.arange(TOK_DEV, dtype=jnp.int32)
    allowed = (group_row[:, None] == group_row[None, :]) & (positions[:, None] >= positions[None, :])
    masked = jnp.where(allowed[None, :, :], scores, -1e+30)
    weights = low(jax.nn.softmax(masked, axis=-1))
    mixed = jnp.einsum('hqk,khd->qhd', weights, values_row, precision=HIGH)
    return low(low_back(mixed))

def attention_step(packed):
    return jax.checkpoint(row_attention)(packed[0], packed[1], packed[2], packed[3])

def expert_apply(rows_in, weight_in, weight_out):
    hidden = low_back(jnp.dot(rows_in, weight_in, precision=HIGH))
    active = low(jax.nn.gelu(hidden, approximate=False))
    return jnp.dot(active, weight_out, precision=HIGH)

def frozen_step(packed):
    return jax.checkpoint(expert_apply)(packed[0], packed[1].astype(jnp.float32), packed[2].astype(jnp.float32))

def train_step(packed):
    return jax.checkpoint(expert_apply)(packed[0], packed[1], packed[2])

def pick_rows(block_rows, indices):
    return block_rows[indices]

def forward(routes, seq_ids, frozen_in, frozen_out, block_in, first_gain, first_bias, qkv_weight, out_weight, second_gain, second_bias, router_weight, train_in, train_out):
    row_total = TOKENS // TOK_DEV
    first_normed = low(layer_norm(block_in, first_gain, first_bias))
    projected = low(low_back(jnp.einsum('td,sdf->stf', first_normed, qkv_weight, precision=HIGH)))
    shaped = projected.reshape(3, row_total, TOK_DEV, HEADS, HEAD_DIM)
    mixed = lax.map(attention_step, (shaped[0], shaped[1], shaped[2], seq_ids.reshape(row_total, TOK_DEV)))
    mixed = mixed.reshape(TOKENS, D)
    branch = low_back(jnp.dot(mixed, out_weight, precision=HIGH))
    residual = block_in + branch
    second_normed = low(layer_norm(residual, second_gain, second_bias))
    logits = jnp.dot(second_normed, router_weight, precision=HIGH)
    gate_vals = jax.nn.softmax(jnp.take_along_axis(logits, routes, axis=1), axis=1)
    sources = TOKENS // ROWS
    pair_expert = routes.reshape(sources, 2 * ROWS)
    one_hot = (pair_expert[:, :, None] == jnp.arange(EXPERTS, dtype=jnp.int32)[None, None, :]).astype(jnp.int32)
    earlier = jnp.cumsum(one_hot, axis=1) - one_hot
    slot_pos = lax.optimization_barrier(jnp.sum(earlier * one_hot, axis=2))
    is_kept = slot_pos < CAP
    target = jnp.where(is_kept, pair_expert * CAP + slot_pos, EXPERTS * CAP).astype(jnp.int32)
    source_ids = jnp.broadcast_to(jnp.arange(sources, dtype=jnp.int32)[:, None], target.shape)
    pair_ids = jnp.broadcast_to(jnp.arange(2 * ROWS, dtype=jnp.int32)[None, :], target.shape)
    slot_table = jnp.full((sources, EXPERTS * CAP + 1), 2 * ROWS, jnp.int32).at[source_ids, target].set(pair_ids)[:, :EXPERTS * CAP]
    is_filled = slot_table < 2 * ROWS
    token_row = jnp.where(is_filled, slot_table // 2, 0).astype(jnp.int32)
    picked = jax.vmap(pick_rows)(second_normed.reshape(sources, ROWS, D), token_row)
    dispatched = low_back(jnp.where(is_filled[:, :, None], picked, 0.0))
    per_expert = dispatched.reshape(sources, EXPERTS, CAP, D).transpose(1, 0, 2, 3).reshape(EXPERTS, sources * CAP, D)
    frozen_rows = lax.map(frozen_step, (per_expert[:FROZEN], frozen_in, frozen_out))
    train_rows = lax.map(train_step, (per_expert[FROZEN:], train_in, train_out))
    expert_rows = low(low_back(jnp.concatenate([frozen_rows, train_rows], axis=0)))
    by_source = expert_rows.reshape(EXPERTS, sources, CAP, D).transpose(1, 0, 2, 3).reshape(sources, EXPERTS * CAP, D)
    returned = jax.vmap(pick_rows)(by_source, jnp.where(is_kept, target, 0).astype(jnp.int32))
    returned = jnp.where(is_kept[:, :, None], returned, 0.0).reshape(TOKENS, 2, D)
    return residual + lax.optimization_barrier(jnp.sum(gate_vals[:, :, None] * returned, axis=1))

def reference(block_in, first_gain, first_bias, qkv_weight, out_weight, second_gain, second_bias, router_weight, frozen_in, frozen_out, train_in, train_out, routes, seq_ids, cotangent):
    params = (block_in, first_gain, first_bias, qkv_weight.astype(jnp.float32), out_weight.astype(jnp.float32), second_gain, second_bias, router_weight.astype(jnp.float32), train_in.astype(jnp.float32), train_out.astype(jnp.float32))
    block_out, pullback = jax.vjp(partial(forward, routes, seq_ids, frozen_in, frozen_out), *params)
    gradients = pullback(cotangent)
    return (block_out, gradients[0], gradients[1], gradients[2], gradients[3], gradients[4], gradients[5], gradients[6], gradients[7], gradients[8], gradients[9])
```

```python
import functools

import jax
import jax.numpy as jnp
from jax import lax
from jax.experimental import pallas as pl
from jax.experimental.pallas import tpu as pltpu
from jax.sharding import PartitionSpec as P

HEAD_DIM = 64
EPS = 1e-05
NEG = -1e30
FW = 256
F32 = jnp.float32
BF = jnp.bfloat16
MESH = pl.DeviceIdType.MESH
VMEM = pltpu.VMEM


def contract(left, right, left_dim, right_dim, precision=None):
    return lax.dot_general(
        left,
        right,
        (((left_dim,), (right_dim,)), ((), ())),
        precision=precision,
        preferred_element_type=F32,
    )


def mm(left, right):
    return contract(left, right, 1, 0)


def mm_nt(left, right):
    return contract(left, right, 1, 1)


def mm_tn(left, right):
    return contract(left, right, 0, 0)


def normalize(values):
    average = jnp.mean(values, axis=-1, keepdims=True)
    centred = values - average
    variance = jnp.mean(centred * centred, axis=-1, keepdims=True)
    inverse = lax.rsqrt(variance + EPS)
    return centred * inverse, inverse


def norm_back(grad_norm, normal, inverse, gain_vec):
    scaled = grad_norm * gain_vec
    first_mean = jnp.mean(scaled, axis=-1, keepdims=True)
    second_mean = jnp.mean(scaled * normal, axis=-1, keepdims=True)
    return inverse * (scaled - first_mean - normal * second_mean)


def nearest(place, step, count):
    low, high = place, count - 1 - place
    both = jnp.minimum(low, high)
    near = jnp.where(step % 2 == 1, place - (step + 1) // 2, place + step // 2)
    far = jnp.where(low > high, place - (step - both), place + (step - both))
    return jnp.where(step <= 2 * both, near, far)


class Line:
    def __init__(self, ref_of, send, recv, place, count):
        self.ref_of, self.send, self.recv = ref_of, send, recv
        self.place, self.count = place, count

    def copy(self, block, up):
        step = 1 if up else -1
        return pltpu.make_async_remote_copy(
            src_ref=self.ref_of(block),
            dst_ref=self.ref_of(block),
            send_sem=self.send.at[0 if up else 1, block],
            recv_sem=self.recv.at[block],
            device_id={"head": self.place + step},
            device_id_type=MESH,
        )

    def pass_on(self, block):
        @pl.when((block <= self.place) & (self.place < self.count - 1))
        def _():
            self.copy(block, True).start()

        @pl.when((block >= self.place) & (self.place > 0))
        def _():
            self.copy(block, False).start()

    def arrive(self, block):
        self.copy(block, True).wait_recv()

    def finish(self):
        for block in range(self.count):

            @pl.when((block <= self.place) & (self.place < self.count - 1))
            def _():
                self.copy(block, True).wait_send()

            @pl.when((block >= self.place) & (self.place > 0))
            def _():
                self.copy(block, False).wait_send()


class Exchange:
    def __init__(self, axis, place, count, source, target, send, recv, device=None):
        self.axis, self.place, self.count = axis, place, count
        self.source, self.target, self.send, self.recv = source, target, send, recv
        self.device = device or (lambda peer: peer)

    def copy(self, peer, lands):
        return pltpu.make_async_remote_copy(
            src_ref=self.source(peer),
            dst_ref=self.target(lands),
            send_sem=self.send.at[peer],
            recv_sem=self.recv.at[lands],
            device_id={self.axis: self.device(peer)},
            device_id_type=MESH,
        )

    def loop(self, act):
        def body(step, carry):
            act(lax.rem(self.place + step, self.count))
            return carry

        lax.fori_loop(1, self.count, body, 0)

    def start_one(self, peer):
        self.copy(peer, self.place).start()

    def start(self):
        self.loop(self.start_one)

    def arrive(self):
        self.loop(lambda peer: self.copy(peer, peer).wait_recv())

    def finish(self):
        self.loop(lambda peer: self.copy(peer, self.place).wait_send())


def body(
    block_in,
    first_gain,
    first_bias,
    qkv_weight,
    out_weight,
    second_gain,
    second_bias,
    router,
    frozen_in,
    frozen_out,
    train_in,
    train_out,
    routes,
    seq,
    cotangent,
    block_out,
    input_grad,
    vec_out,
    weights_out,
    grad_in_out,
    grad_out_out,
    s,
    cfg,
):
    n, S, T, D, L = cfg["n"], cfg["S"], cfg["T"], cfg["D"], cfg["L"]
    E, R, W, HID, cap = cfg["E"], cfg["R"], cfg["W"], cfg["HID"], cfg["cap"]
    NF = D // FW
    M = E * R
    heads = W // HEAD_DIM
    SB = 4 if S % 4 == 0 else 1
    RB = SB * R
    half = L // 2
    chips = S // 2
    group = cfg["group"]
    part = W // group
    z = lax.axis_index("head")
    d = lax.axis_index("dp")

    loads = []
    for index, ref in enumerate((frozen_in, train_in, frozen_out, train_out)):
        loads.append(pltpu.make_async_copy(ref.at[0], s.experts.at[index], s.load_sem.at[index]))
        loads[-1].start()
    barrier = pltpu.get_barrier_semaphore()
    for step in range(1, n):
        pl.semaphore_signal(barrier, 1, device_id={"head": lax.rem(z + step, n)}, device_id_type=MESH)

    def greet(step, carry):
        pl.semaphore_signal(barrier, 1, device_id={"dp": lax.rem(d + step, S)}, device_id_type=MESH)
        return carry

    lax.fori_loop(1, S, greet, 0)

    normal_one, inverse_one = normalize(block_in[...])
    s.normal_one[...] = normal_one
    s.inverse_one[...] = jnp.broadcast_to(inverse_one, s.inverse_one.shape)
    s.normed[z] = (normal_one * first_gain[...] + first_bias[...]).astype(BF)
    for f in range(NF):
        s.cots[f, z] = cotangent[:, f * FW : (f + 1) * FW].astype(BF)
    s.routes[z] = routes[...]
    part_id = lax.rem(d, group)
    for q in range(group):
        s.outw[z, q] = out_weight[q * part : (q + 1) * part, :]
    pl.semaphore_wait(barrier, n - 1 + S - 1)

    def over_z(source, target, send, recv):
        return Exchange("head", z, n, source, target, send, recv)

    routes_x = over_z(lambda p: s.routes.at[z], lambda p: s.routes.at[p], s.routes_s, s.routes_r)
    routes_x.start()
    T2 = T // 2
    normed_lines = [
        Line(lambda b, h=h: s.normed.at[b, pl.ds(h * T2, T2), :], s.normed_s.at[h], s.normed_r.at[h], z, n)
        for h in range(2)
    ]
    cot_lines = [Line(lambda b, f=f: s.cots.at[f, b], s.cot_s.at[f], s.cot_r.at[f], z, n) for f in range(NF)]
    for line in normed_lines:
        line.pass_on(z)
    outw_x = over_z(
        lambda p: s.outw.at[z, part_id], lambda p: s.outw.at[p, part_id], s.outw_s, s.outw_r
    )
    outw_x.start()

    def project(block):
        rows = pl.ds(pl.multiple_of(block * T, T), T)
        normed = s.normed[block]
        for index in range(3):
            value = mm(normed, qkv_weight[index]).astype(BF)
            if index == 0:
                value = value * jnp.asarray(HEAD_DIM**-0.5, BF)
            s.qkv[index, rows, :] = value

    project(z)
    routes_x.arrive()

    expert_col = lax.broadcasted_iota(jnp.int32, (E, T), 0)
    earlier = (
        lax.broadcasted_iota(jnp.int32, (T, T), 0) < lax.broadcasted_iota(jnp.int32, (T, T), 1)
    ).astype(F32).astype(BF)
    row_ids = lax.broadcasted_iota(jnp.int32, (M, T), 0)
    for j in range(n):
        first, second = s.routes[j, 0:1, :], s.routes[j, 1:2, :]
        hot0, hot1 = expert_col == first, expert_col == second
        hot = jnp.where(hot0 | hot1, 1.0, 0.0)
        count = mm(hot.astype(BF), earlier)
        for k, (names, hit) in enumerate(((first, hot0), (second, hot1))):
            slot = jnp.sum(jnp.where(hit, count, 0.0), axis=0, keepdims=True).astype(jnp.int32)
            late = names >= S
            owner = jnp.where(late, names - S, names)
            row = (owner * 2 + jnp.where(late, 1, 0)) * R + j * cap + slot
            s.target[j, k : k + 1, :] = jnp.where(slot < cap, row, -1)
        s.place[:, j * T : (j + 1) * T] = jnp.where(
            (row_ids == s.target[j, 0:1, :]) | (row_ids == s.target[j, 1:2, :]), 1.0, 0.0
        ).astype(BF)

    def end_of_line(block):
        @pl.when((block == 0) & (z < n - 1))
        def _():
            for line in cot_lines:
                line.copy(z, True).start()

        @pl.when((block == n - 1) & (z > 0))
        def _():
            for line in cot_lines:
                line.copy(z, False).start()

    end_of_line(z)
    for step in range(1, n):
        block = nearest(z, step, n)
        for line in normed_lines:
            line.arrive(block)
            line.pass_on(block)
        end_of_line(block)
        project(block)

    base = d - part_id
    plane = []
    outw_x.arrive()
    for step in range(1, n):
        other = lax.rem(z + step, n)
        plane.append(
            Exchange(
                "dp",
                part_id,
                group,
                lambda p, other=other: s.outw.at[other, part_id],
                lambda p, other=other: s.outw.at[other, p],
                s.outw_ps.at[step],
                s.outw_pr.at[step],
                device=lambda p: base + p,
            )
        )
        plane[-1].start()

    def lanes_of(rows):
        return lax.broadcasted_iota(jnp.int32, (rows, W), 1) // HEAD_DIM

    two = seq[0:1, L - 1 : L] > 0
    lane_t = lanes_of(T)
    mixed_x = over_z(lambda p: s.mixed.at[p], lambda p: s.mixed_in.at[p], s.mixed_s, s.mixed_r)

    inner_place = (z > 0) & (z < n - 1)

    def cot_service(step):
        @pl.when(inner_place)
        def _():
            block = nearest(z, step, n)
            for line in cot_lines:
                line.arrive(block)
                line.pass_on(block)

    for qi in range(n):
        keys = (qi + 1) * T
        query_pos = lax.broadcasted_iota(jnp.int32, (T, keys), 0) + qi * T
        key_pos = lax.broadcasted_iota(jnp.int32, (T, keys), 1)
        allowed = query_pos >= key_pos
        if (qi * T) // half > 0:
            allowed = allowed & ((key_pos >= half) | jnp.logical_not(two))
        queries = s.qkv[0, qi * T : (qi + 1) * T, :].astype(F32)
        out = jnp.zeros((T, W), F32)
        for h in range(heads):
            masked_q = jnp.where(lane_t == h, queries, 0.0).astype(BF)
            scores = jnp.where(allowed, mm_nt(masked_q, s.qkv[1, :keys, :]), NEG)
            exp_vals = jnp.exp(scores - jnp.max(scores, axis=1, keepdims=True))
            weights = (exp_vals / jnp.sum(exp_vals, axis=1, keepdims=True)).astype(BF)
            s.probs[h, qi * T : (qi + 1) * T, :keys] = weights
            out = jnp.where(lane_t == h, mm(weights, s.qkv[2, :keys, :]), out)
        s.mixed[qi] = out.astype(BF)

        @pl.when(z != qi)
        def _():
            mixed_x.start_one(qi)

        if qi == 0 and n > 2:
            cot_service(1)
        if qi == 1 and n > 2:
            cot_service(2)

    for step in range(3, n):
        cot_service(step)

    @pl.when(jnp.logical_not(inner_place))
    def _():
        for step in range(1, n):
            block = nearest(z, step, n)
            for line in cot_lines:
                line.arrive(block)
                line.pass_on(block)

    def dispatch(rows_ref, out_ref, in_ref, send, recv, f):
        tokens = rows_ref[f].reshape(n * T, FW)
        for half_id in range(2):
            span = S // 2
            rows = slice(half_id * span * 2 * R, (half_id + 1) * span * 2 * R)
            value = mm(s.place[rows, :], tokens).astype(BF)
            out_ref[f, half_id * span : (half_id + 1) * span] = value.reshape(span, 2, R, FW)
        exchange = Exchange(
            "dp", d, S, lambda p: out_ref.at[f, p], lambda p: in_ref.at[f, :, p], send.at[f], recv.at[f]
        )
        exchange.start()
        in_ref[f, :, d] = out_ref[f, d]
        return exchange

    cot_x = [None] * NF
    for f in range(NF - 1):
        cot_x[f] = dispatch(s.cots, s.cot_out, s.cot_in, s.cotx_s, s.cotx_r, f)

    for exchange in plane:
        exchange.arrive()
    mixed_x.arrive()
    s.mixed_in[z] = s.mixed[z]
    branch = jnp.zeros((T, D), F32)
    for j in range(n):
        branch = branch + mm(s.mixed_in[j], s.outw[j].reshape(W, D))
    residual = block_in[...] + branch
    s.residual[...] = residual
    normal_two, inverse_two = normalize(residual)
    s.normal_two[...] = normal_two
    s.inverse_two[...] = jnp.broadcast_to(inverse_two, s.inverse_two.shape)
    second_b = (normal_two * second_gain[...] + second_bias[...]).astype(BF)
    for f in range(NF):
        s.second[f, z] = second_b[:, f * FW : (f + 1) * FW]
    second_lines = [
        Line(lambda b, f=f: s.second.at[f, b], s.second_s.at[f], s.second_r.at[f], z, n) for f in range(NF)
    ]
    for line in second_lines:
        line.pass_on(z)
    row_x = []
    for f in range(NF):
        for step in range(1, n):
            block = nearest(z, step, n)
            second_lines[f].arrive(block)
            second_lines[f].pass_on(block)
        row_x.append(dispatch(s.second, s.row_out, s.row_in, s.rowx_s, s.rowx_r, f))
    cot_x[NF - 1] = dispatch(s.cots, s.cot_out, s.cot_in, s.cotx_s, s.cotx_r, NF - 1)

    for j in range(n):
        logits = jnp.zeros((E, T), F32)
        for f in range(NF):
            logits = logits + mm_nt(router[:, f * FW : (f + 1) * FW], s.second[f, j])
        hot0, hot1 = expert_col == s.routes[j, 0:1, :], expert_col == s.routes[j, 1:2, :]
        pick0 = jnp.sum(jnp.where(hot0, logits, 0.0), axis=0, keepdims=True)
        pick1 = jnp.sum(jnp.where(hot1, logits, 0.0), axis=0, keepdims=True)
        top = jnp.maximum(pick0, pick1)
        exp0, exp1 = jnp.exp(pick0 - top), jnp.exp(pick1 - top)
        s.gates[j, 0:1, :] = exp0 / (exp0 + exp1)
        s.gates[j, 1:2, :] = exp1 / (exp0 + exp1)
        s.gates[j, 2:4, :] = s.target[j, 0:2, :].astype(F32)
        s.gates[j, 4:8, :] = jnp.zeros((4, T), F32)
        columns = jnp.transpose(s.gates[j])
        lane_ids = lax.broadcasted_iota(jnp.int32, (T, M), 1).astype(F32)
        s.combine[j * T : (j + 1) * T, :] = jnp.where(
            lane_ids == columns[:, 2:3],
            columns[:, 0:1],
            jnp.where(lane_ids == columns[:, 3:4], columns[:, 1:2], 0.0),
        ).astype(BF)
    slot_ids = lax.broadcasted_iota(jnp.int32, (R, T), 0)
    lane_128 = lax.broadcasted_iota(jnp.int32, (128, 128), 1)
    table = jnp.zeros((128, 128), F32)
    for owner in range(S):
        total = jnp.zeros((R, T), F32)
        ids = slot_ids + (owner * 2 + 1) * R
        for j in range(n):
            total = total + jnp.where(
                ids == s.target[j, 0:1, :],
                s.gates[j, 0:1, :],
                jnp.where(ids == s.target[j, 1:2, :], s.gates[j, 1:2, :], 0.0),
            )
        column = jnp.sum(total, axis=1, keepdims=True)
        if R < 128:
            column = jnp.concatenate([column, jnp.zeros((128 - R, 1), F32)], axis=0)
        table = jnp.where(lane_128 == owner, column, table)
    table = jnp.transpose(table)
    for owner in range(S):
        s.gate_out[owner] = jnp.broadcast_to(table[owner : owner + 1, :], (8, 128))
    gate_x = Exchange(
        "dp", d, S, lambda p: s.gate_out.at[p], lambda p: s.gate_in.at[p], s.gate_s, s.gate_r
    )
    gate_x.start()
    s.gate_in[d] = s.gate_out[d]

    for load in loads:
        load.wait()

    def row_blocks(act):
        def step(i, carry):
            act(i * SB, pl.multiple_of(i * RB, RB))
            return carry

        lax.fori_loop(0, S // SB, step, 0)

    def add_up(total_ref, rows_ref, f, transposed):
        for g in range(2):

            def act(block, row):
                value = rows_ref[f, g, pl.ds(block, SB)].reshape(RB, FW)
                if transposed:
                    piece = mm_nt(value, s.experts[2 + g, :, f * FW : (f + 1) * FW])
                else:
                    piece = mm(value, s.experts[g, f * FW : (f + 1) * FW, :])
                rows = pl.ds(g * S * R + row, RB)
                total_ref[rows, :] = piece if f == 0 else total_ref[rows, :] + piece

            row_blocks(act)

    for f in range(NF - 1):
        cot_x[f].arrive()
        add_up(s.grad_active, s.cot_in, f, True)
    for f in range(NF):
        row_x[f].arrive()
        add_up(s.hidden, s.row_in, f, False)
    EB = 16 if R % 16 == 0 else 8

    for g in range(2):

        def activate(i, carry):
            rows = pl.ds(pl.multiple_of(i * EB, EB), EB)
            flat = pl.ds(pl.multiple_of(g * S * R + i * EB, EB), EB)
            value = s.hidden[flat, :]
            normal_cdf = 0.5 * (1.0 + lax.erf(value * 0.7071067811865476))
            s.active[g, rows, :] = (value * normal_cdf).astype(BF)
            s.hidden[flat, :] = normal_cdf + value * jnp.exp(-0.5 * value * value) * 0.3989422804014327
            return carry

        lax.fori_loop(0, S * R // EB, activate, 0)

    cot_x[NF - 1].arrive()
    add_up(s.grad_active, s.cot_in, NF - 1, True)

    tables = []
    for g in range(2):
        table = jnp.zeros((128, 128), F32)
        for source in range(S):
            sums = []
            for i in range(R // EB):
                rows = slice(source * R + i * EB, source * R + (i + 1) * EB)
                flat = slice(g * S * R + rows.start, g * S * R + rows.stop)
                grad = s.grad_active[flat, :]
                s.grad_hidden[g, rows, :] = (grad * s.hidden[flat, :]).astype(BF)
                sums.append(
                    jnp.sum(grad * s.active[g, rows, :].astype(F32), axis=1, keepdims=True)
                )
            if R < 128:
                sums.append(jnp.zeros((128 - R, 1), F32))
            table = jnp.where(lane_128 == source, jnp.concatenate(sums, axis=0), table)
        tables.append(jnp.transpose(table))
    row_8 = lax.broadcasted_iota(jnp.int32, (8, 128), 0)
    for source in range(S):
        s.dot_out[source] = jnp.where(
            row_8 == 0, tables[0][source : source + 1, :], tables[1][source : source + 1, :]
        )
    dot_x = Exchange("dp", d, S, lambda p: s.dot_out.at[p], lambda p: s.dot_in.at[p], s.dot_s, s.dot_r)
    dot_x.start()
    s.dot_in[d] = s.dot_out[d]

    def give_back(rows_ref, first_weight, out_ref, in_ref, send, recv, transposed):
        exchanges = []
        for f in range(NF):
            for g in range(2):

                def act(block, row):
                    value = rows_ref[g, pl.ds(row, RB), :]
                    if transposed:
                        piece = mm_nt(value, s.experts[first_weight + g, f * FW : (f + 1) * FW, :])
                    else:
                        piece = mm(value, s.experts[first_weight + g, :, f * FW : (f + 1) * FW])
                    out_ref[f, pl.ds(block, SB), g] = piece.astype(BF).reshape(SB, R, FW)

                row_blocks(act)
            exchange = Exchange(
                "dp",
                d,
                S,
                lambda p, f=f: out_ref.at[f, p],
                lambda p, f=f: in_ref.at[f, p],
                send.at[f],
                recv.at[f],
            )
            exchange.start()
            in_ref[f, d] = out_ref[f, d]
            exchanges.append(exchange)
        return exchanges

    if cfg["tight"]:
        for exchange in cot_x + row_x:
            exchange.finish()
        down_out, fore_out = s.cot_out, s.row_out
    else:
        down_out, fore_out = s.down_out, s.fore_out
    down_x = give_back(s.grad_hidden, 0, down_out, s.down_in, s.down_s, s.down_r, True)
    fore_x = give_back(s.active, 2, fore_out, s.fore_in, s.fore_s, s.fore_r, False)

    gate_x.arrive()
    columns = jnp.transpose(s.gate_in[:, 0, :])
    for source in range(S):
        column = columns[:R, source : source + 1]
        rows = slice(source * R, (source + 1) * R)
        s.active[1, rows, :] = (s.active[1, rows, :].astype(F32) * column).astype(BF)
        s.grad_hidden[1, rows, :] = (s.grad_hidden[1, rows, :].astype(F32) * column).astype(BF)
    for f in range(NF):
        s.hidden[f * FW : (f + 1) * FW, :] = mm_tn(
            s.row_in[f, 1].reshape(S * R, FW), s.grad_hidden[1]
        )
        s.grad_active[0:HID, f * FW : (f + 1) * FW] = mm_tn(
            s.active[1], s.cot_in[f, 1].reshape(S * R, FW)
        )
    stores = [
        pltpu.make_async_copy(s.hidden.at[0:D, :], grad_in_out.at[0], s.store_sem.at[0]),
        pltpu.make_async_copy(s.grad_active.at[0:HID, :], grad_out_out.at[0], s.store_sem.at[1]),
    ]
    for store in stores:
        store.start()

    def gather_rows(in_ref, f):
        return mm(s.combine[...], in_ref[f].reshape(M, FW)).astype(BF).reshape(n, T, FW)

    def token_sums(exchanges, in_ref, part_ref, sum_ref, send, recv):
        result = []
        for f in range(NF):
            exchanges[f].arrive()
            part_ref[f] = gather_rows(in_ref, f)
            sums_x = over_z(
                lambda p, f=f: part_ref.at[f, p], lambda p, f=f: sum_ref.at[f, p], send.at[f], recv.at[f]
            )
            sums_x.start()
            sum_ref[f, z] = part_ref[f, z]
            result.append(sums_x)
        return result

    def add_sums(sums_x, sum_ref):
        parts = []
        for f in range(NF):
            sums_x[f].arrive()
            total = sum_ref[f, 0].astype(F32)
            for j in range(1, n):
                total = total + sum_ref[f, j].astype(F32)
            parts.append(total)
        return jnp.concatenate(parts, axis=1)

    down_sums = token_sums(down_x, s.down_in, s.down_part, s.down_sum, s.dsum_s, s.dsum_r)

    dot_x.arrive()
    turned = [jnp.transpose(s.dot_in[:, g, :]) for g in range(2)]
    for j in range(n):
        total = jnp.zeros((R, T), F32)
        for owner in range(S):
            for g in range(2):
                ids = slot_ids + (owner * 2 + g) * R
                sign = jnp.where(
                    ids == s.target[j, 0:1, :], 1.0, jnp.where(ids == s.target[j, 1:2, :], -1.0, 0.0)
                )
                total = total + sign * turned[g][:R, owner : owner + 1]
        s.delta_out[j] = jnp.broadcast_to(jnp.sum(total, axis=0, keepdims=True), (8, T))
    delta_x = over_z(
        lambda p: s.delta_out.at[p], lambda p: s.delta_in.at[p], s.delta_s, s.delta_r
    )
    delta_x.start()
    s.delta_in[z] = s.delta_out[z]
    delta_x.arrive()
    delta = s.delta_in[0, 0:1, :]
    for j in range(1, n):
        delta = delta + s.delta_in[j, 0:1, :]

    grad_chosen = s.gates[z, 0:1, :] * s.gates[z, 1:2, :] * delta
    hot0, hot1 = expert_col == s.routes[z, 0:1, :], expert_col == s.routes[z, 1:2, :]
    grad_logits = jnp.where(hot0, grad_chosen, jnp.where(hot1, -grad_chosen, 0.0))
    router_part = contract(grad_logits, router[...].astype(F32), 0, 0, lax.Precision.HIGHEST)
    for f in range(NF):
        s.early[0:E, f * FW : (f + 1) * FW] = contract(
            grad_logits, s.second[f, z].astype(F32), 1, 0, lax.Precision.HIGHEST
        )
    grad_second = add_sums(down_sums, s.down_sum) + router_part
    normal_two = s.normal_two[...]
    pair = jnp.concatenate(
        [
            jnp.sum(grad_second * normal_two, axis=0, keepdims=True),
            jnp.sum(grad_second, axis=0, keepdims=True),
            jnp.zeros((6, D), F32),
        ],
        axis=0,
    )
    s.early[E : E + 8, :] = pair
    grad_residual = cotangent[...] + norm_back(
        grad_second, normal_two, s.inverse_two[:, 0:1], second_gain[...]
    )
    s.grad_residual[...] = grad_residual
    s.branch[z] = grad_residual.astype(BF)
    branch_lines = [
        Line(lambda b, h=h: s.branch.at[b, pl.ds(h * T2, T2), :], s.branch_s.at[h], s.branch_r.at[h], z, n)
        for h in range(2)
    ]
    for line in branch_lines:
        line.pass_on(z)

    def mixed_back(block):
        s.grad_mixed[pl.ds(pl.multiple_of(block * T, T), T), :] = mm_nt(
            s.branch[block], out_weight[...]
        ).astype(BF)

    mixed_back(z)
    early_x = Exchange(
        "dp",
        part_id,
        group,
        lambda p: s.early,
        lambda p: s.early_dp.at[p],
        s.early_s,
        s.early_r,
        device=lambda p: base + p,
    )
    early_x.start()
    s.early_dp[part_id] = s.early[...]
    for step in range(1, n):
        block = nearest(z, step, n)
        for line in branch_lines:
            line.arrive(block)
            line.pass_on(block)
        mixed_back(block)

    if cfg["tight"]:
        for exchange in down_sums:
            exchange.finish()
        fore_part = s.down_part
    else:
        fore_part = s.fore_part
    fore_sums = token_sums(fore_x, s.fore_in, fore_part, s.fore_sum, s.fsum_s, s.fsum_r)

    for qi in range(n):
        keys = (qi + 1) * T
        rows = slice(qi * T, (qi + 1) * T)
        grads = s.grad_mixed[rows, :]
        grads_f = grads.astype(F32)
        lane_k = lanes_of(keys)
        grad_q = jnp.zeros((T, W), F32)
        grad_k = jnp.zeros((keys, W), F32)
        grad_v = jnp.zeros((keys, W), F32)
        for h in range(heads):
            masked = jnp.where(lane_t == h, grads_f, 0.0).astype(BF)
            grad_w = mm_nt(masked, s.qkv[2, :keys, :])
            weights = s.probs[h, rows, :keys]
            probs = weights.astype(F32)
            inner = jnp.sum(probs * grad_w, axis=1, keepdims=True)
            grad_s = (probs * (grad_w - inner)).astype(BF)
            grad_q = jnp.where(lane_t == h, mm(grad_s, s.qkv[1, :keys, :]), grad_q)
            grad_k = jnp.where(lane_k == h, mm_tn(grad_s, s.qkv[0, rows, :]), grad_k)
            grad_v = jnp.where(lane_k == h, mm_tn(weights, grads), grad_v)
        s.grad_proj[0, rows, :] = (grad_q * HEAD_DIM**-0.5).astype(BF)
        if qi == 0:
            s.grad_kv[...] = jnp.zeros(s.grad_kv.shape, F32)
        s.grad_kv[0, :keys, :] = s.grad_kv[0, :keys, :] + grad_k
        s.grad_kv[1, :keys, :] = s.grad_kv[1, :keys, :] + grad_v
    for index in range(2):
        s.grad_proj[1 + index] = s.grad_kv[index].astype(BF)

    def first_part(block):
        rows = pl.ds(pl.multiple_of(block * T, T), T)
        total = mm_nt(s.grad_proj[0, rows, :], qkv_weight[0])
        for index in range(1, 3):
            total = total + mm_nt(s.grad_proj[index, rows, :], qkv_weight[index])
        s.first_out[block] = total.astype(BF)

    first_x = over_z(lambda p: s.first_out.at[p], lambda p: s.first_in.at[p], s.first_s, s.first_r)
    for step in range(1, n):
        peer = nearest(z, n - step, n)
        first_part(peer)
        first_x.start_one(peer)
    first_part(z)
    s.first_in[z] = s.first_out[z]

    normed_all = s.normed[...].reshape(L, D)
    each = chips // 2
    size = D // each
    for index in range(4):
        if index < 3:
            value = mm_tn(normed_all, s.grad_proj[index])
        else:
            value = mm_tn(s.branch[...].reshape(L, D), s.mixed[...].reshape(L, W))
        s.wsum[index // 2, (index % 2) * each : (index % 2 + 1) * each] = value.astype(BF).reshape(
            each, size, W
        )
    core = lax.rem(d, 2)
    chip = d // 2
    mate = d + 1 - 2 * core
    swap = pltpu.make_async_remote_copy(
        src_ref=s.wsum.at[1 - core],
        dst_ref=s.wswap,
        send_sem=s.swap_sem.at[0],
        recv_sem=s.swap_sem.at[1],
        device_id={"dp": mate},
        device_id_type=MESH,
    )
    swap.start()
    swap.wait_recv()
    s.wswap[...] = (s.wsum[core].astype(F32) + s.wswap[...].astype(F32)).astype(BF)

    def over_chips(source, target, send, recv):
        return Exchange("dp", chip, chips, source, target, send, recv, device=lambda p: 2 * p + core)

    pair_x = over_chips(lambda p: s.wswap.at[p], lambda p: s.wparts.at[p], s.pair_s, s.pair_r)
    pair_x.start()
    s.wparts[chip] = s.wswap[chip]

    early_x.arrive()
    total = s.early_dp[0]
    for peer in range(1, group):
        total = total + s.early_dp[peer]
    crowds = S // group
    far_x = []
    if crowds > 1:
        crowd = d // group
        s.early_far[crowd] = total
        far_x.append(
            Exchange(
                "dp",
                crowd,
                crowds,
                lambda p: s.early_far.at[crowd],
                lambda p: s.early_far.at[p],
                s.earlyf_s,
                s.earlyf_r,
                device=lambda p: p * group + part_id,
            )
        )
        far_x[0].start()
        far_x[0].arrive()
        total = s.early_far[0]
        for peer in range(1, crowds):
            total = total + s.early_far[peer]
    s.early_z[z] = total
    early_zx = over_z(lambda p: s.early_z.at[z], lambda p: s.early_z.at[p], s.earlyz_s, s.earlyz_r)
    early_zx.start()

    pair_x.arrive()
    total = s.wparts[0].astype(F32)
    for peer in range(1, chips):
        total = total + s.wparts[peer].astype(F32)
    s.wfull[core, chip] = total.astype(BF)
    full_x = over_chips(
        lambda p: s.wfull.at[core, chip], lambda p: s.wfull.at[core, p], s.full_s, s.full_r
    )
    full_x.start()

    block_out[...] = s.residual[...] + add_sums(fore_sums, s.fore_sum)

    first_x.arrive()
    grad_first = s.first_in[0].astype(F32)
    for j in range(1, n):
        grad_first = grad_first + s.first_in[j].astype(F32)
    normal_one = s.normal_one[...]
    s.late[...] = jnp.concatenate(
        [
            jnp.sum(grad_first * normal_one, axis=0, keepdims=True),
            jnp.sum(grad_first, axis=0, keepdims=True),
            jnp.zeros((6, D), F32),
        ],
        axis=0,
    )
    late_x = Exchange("dp", d, S, lambda p: s.late, lambda p: s.late_dp.at[p], s.late_s, s.late_r)
    late_x.start()
    s.late_dp[d] = s.late[...]
    input_grad[...] = s.grad_residual[...] + norm_back(
        grad_first, normal_one, s.inverse_one[:, 0:1], first_gain[...]
    )
    full_x.arrive()
    back = pltpu.make_async_remote_copy(
        src_ref=s.wfull.at[core],
        dst_ref=s.wfull.at[core],
        send_sem=s.swap_sem.at[2],
        recv_sem=s.swap_sem.at[3],
        device_id={"dp": mate},
        device_id_type=MESH,
    )
    back.start()
    late_x.arrive()
    total = s.late_dp[0]
    for peer in range(1, S):
        total = total + s.late_dp[peer]
    s.late_z[z] = total
    late_zx = over_z(lambda p: s.late_z.at[z], lambda p: s.late_z.at[p], s.latez_s, s.latez_r)
    late_zx.start()
    early_zx.arrive()
    total = s.early_z[0]
    for j in range(1, n):
        total = total + s.early_z[j]
    vec_out[0 : E + 8, :] = total
    late_zx.arrive()
    total = s.late_z[0]
    for j in range(1, n):
        total = total + s.late_z[j]
    vec_out[E + 8 : E + 16, :] = total
    pltpu.make_async_remote_copy(
        src_ref=s.wfull.at[core],
        dst_ref=s.wfull.at[1 - core],
        send_sem=s.swap_sem.at[2],
        recv_sem=s.swap_sem.at[3],
        device_id={"dp": mate},
        device_id_type=MESH,
    ).wait_recv()
    sums_store = pltpu.make_async_copy(s.wfull, weights_out, s.store_sem.at[2])
    sums_store.start()
    stores.append(sums_store)

    for store in stores:
        store.wait()
    swap.wait_send()
    back.wait_send()
    for lines in (normed_lines, cot_lines, second_lines, branch_lines):
        for line in lines:
            line.finish()
    done = [routes_x, outw_x, gate_x, dot_x, delta_x, early_x, pair_x, early_zx, full_x, first_x, late_x]
    if not cfg["tight"]:
        done += cot_x + row_x + down_sums
    done += far_x + [late_zx, mixed_x] + plane + down_x + fore_x + fore_sums
    for exchange in done:
        exchange.finish()


class Names:
    pass


def shards(
    block_in,
    first_gain,
    first_bias,
    qkv_weight,
    out_weight,
    second_gain,
    second_bias,
    router_weight,
    frozen_in,
    frozen_out,
    train_in,
    train_out,
    routes,
    seq_ids,
    cotangent,
):
    T, D = block_in.shape
    L = seq_ids.shape[0]
    E = router_weight.shape[1]
    S, n = lax.axis_size("dp"), lax.axis_size("head")
    W = qkv_weight.shape[2]
    HID = frozen_in.shape[2]
    cap = max(2, 5 * T // (2 * E))
    R = -(-(n * cap) // 8) * 8
    M = E * R
    NF = D // FW
    chips = S // 2
    each = chips // 2
    group = 8
    tight = S > group
    cfg = dict(tight=tight, n=n, S=S, T=T, D=D, L=L, E=E, R=R, W=W, HID=HID, cap=cap, group=group)
    DMA = pltpu.SemaphoreType.DMA
    scratch = dict(
        experts=VMEM((4, D, HID), BF),
        normal_one=VMEM((T, D), F32),
        inverse_one=VMEM((T, 128), F32),
        normed=VMEM((n, T, D), BF),
        cots=VMEM((NF, n, T, FW), BF),
        routes=VMEM((n, 2, T), jnp.int32),
        outw=VMEM((n, group, W // group, D), BF),
        qkv=VMEM((3, L, W), BF),
        target=VMEM((n, 8, T), jnp.int32),
        gates=VMEM((n, 8, T), F32),
        place=VMEM((M, L), BF),
        combine=VMEM((L, M), BF),
        probs=VMEM((W // HEAD_DIM, L, L), BF),
        mixed=VMEM((n, T, W), BF),
        mixed_in=VMEM((n, T, W), BF),
        residual=VMEM((T, D), F32),
        normal_two=VMEM((T, D), F32),
        inverse_two=VMEM((T, 128), F32),
        second=VMEM((NF, n, T, FW), BF),
        cot_out=VMEM((NF, S, 2, R, FW), BF),
        cot_in=VMEM((NF, 2, S, R, FW), BF),
        row_out=VMEM((NF, S, 2, R, FW), BF),
        row_in=VMEM((NF, 2, S, R, FW), BF),
        gate_out=VMEM((S, 8, 128), F32),
        gate_in=VMEM((S, 8, 128), F32),
        hidden=VMEM((2 * S * R, HID), F32),
        grad_active=VMEM((2 * S * R, HID), F32),
        active=VMEM((2, S * R, HID), BF),
        grad_hidden=VMEM((2, S * R, HID), BF),
        dot_out=VMEM((S, 8, 128), F32),
        dot_in=VMEM((S, 8, 128), F32),
        down_out=VMEM((NF, S, 2, R, FW), BF),
        down_in=VMEM((NF, S, 2, R, FW), BF),
        fore_out=VMEM((NF, S, 2, R, FW), BF),
        fore_in=VMEM((NF, S, 2, R, FW), BF),
        down_part=VMEM((NF, n, T, FW), BF),
        down_sum=VMEM((NF, n, T, FW), BF),
        fore_part=VMEM((NF, n, T, FW), BF),
        fore_sum=VMEM((NF, n, T, FW), BF),
        delta_out=VMEM((n, 8, T), F32),
        delta_in=VMEM((n, 8, T), F32),
        early=VMEM((E + 8, D), F32),
        early_dp=VMEM((group, E + 8, D), F32),
        early_z=VMEM((n, E + 8, D), F32),
        late=VMEM((8, D), F32),
        late_dp=VMEM((S, 8, D), F32),
        late_z=VMEM((n, 8, D), F32),
        grad_residual=VMEM((T, D), F32),
        branch=VMEM((n, T, D), BF),
        grad_mixed=VMEM((L, W), BF),
        grad_proj=VMEM((3, L, W), BF),
        grad_kv=VMEM((2, L, W), F32),
        first_out=VMEM((n, T, D), BF),
        first_in=VMEM((n, T, D), BF),
        wsum=VMEM((2, chips, D // each, W), BF),
        wswap=VMEM((chips, D // each, W), BF),
        wparts=VMEM((chips, D // each, W), BF),
        wfull=VMEM((2, chips, D // each, W), BF),
        load_sem=DMA((4,)),
        store_sem=DMA((3,)),
        swap_sem=DMA((4,)),
        routes_s=DMA((n,)),
        routes_r=DMA((n,)),
        normed_s=DMA((2, 2, n)),
        normed_r=DMA((2, n)),
        cot_s=DMA((NF, 2, n)),
        cot_r=DMA((NF, n)),
        outw_s=DMA((n,)),
        outw_r=DMA((n,)),
        outw_ps=DMA((n, group)),
        outw_pr=DMA((n, group)),
        mixed_s=DMA((n,)),
        mixed_r=DMA((n,)),
        cotx_s=DMA((NF, S)),
        cotx_r=DMA((NF, S)),
        rowx_s=DMA((NF, S)),
        rowx_r=DMA((NF, S)),
        second_s=DMA((NF, 2, n)),
        second_r=DMA((NF, n)),
        gate_s=DMA((S,)),
        gate_r=DMA((S,)),
        dot_s=DMA((S,)),
        dot_r=DMA((S,)),
        down_s=DMA((NF, S)),
        down_r=DMA((NF, S)),
        fore_s=DMA((NF, S)),
        fore_r=DMA((NF, S)),
        dsum_s=DMA((NF, n)),
        dsum_r=DMA((NF, n)),
        fsum_s=DMA((NF, n)),
        fsum_r=DMA((NF, n)),
        delta_s=DMA((n,)),
        delta_r=DMA((n,)),
        branch_s=DMA((2, 2, n)),
        branch_r=DMA((2, n)),
        early_s=DMA((group,)),
        early_r=DMA((group,)),
        earlyz_s=DMA((n,)),
        earlyz_r=DMA((n,)),
        first_s=DMA((n,)),
        first_r=DMA((n,)),
        pair_s=DMA((chips,)),
        pair_r=DMA((chips,)),
        full_s=DMA((chips,)),
        full_r=DMA((chips,)),
        late_s=DMA((S,)),
        late_r=DMA((S,)),
        latez_s=DMA((n,)),
        latez_r=DMA((n,)),
    )
    if S > group:
        scratch.update(
            early_far=VMEM((S // group, E + 8, D), F32),
            earlyf_s=DMA((S // group,)),
            earlyf_r=DMA((S // group,)),
        )
    if tight:
        del scratch["down_out"], scratch["fore_out"], scratch["fore_part"]
    names = list(scratch)

    def kernel(*refs):
        space = Names()
        for name, ref in zip(names, refs[21:]):
            setattr(space, name, ref)
        body(*refs[:21], space, cfg)

    whole = pl.BlockSpec(memory_space=VMEM)
    left = pl.BlockSpec(memory_space=pl.ANY)
    outs = pl.pallas_call(
        kernel,
        out_shape=(
            jax.ShapeDtypeStruct((T, D), F32),
            jax.ShapeDtypeStruct((T, D), F32),
            jax.ShapeDtypeStruct((E + 16, D), F32),
            jax.ShapeDtypeStruct((2, chips, D // each, W), BF),
            jax.ShapeDtypeStruct((1, D, HID), F32),
            jax.ShapeDtypeStruct((1, HID, D), F32),
        ),
        in_specs=[whole] * 8 + [left] * 4 + [whole] * 3,
        out_specs=(whole, whole, whole, left, left, left),
        scratch_shapes=list(scratch.values()),
        compiler_params=pltpu.CompilerParams(
            collective_id=0, has_side_effects=True, vmem_limit_bytes=67043328
        ),
    )(
        block_in,
        first_gain.reshape(1, D),
        first_bias.reshape(1, D),
        qkv_weight,
        out_weight,
        second_gain.reshape(1, D),
        second_bias.reshape(1, D),
        router_weight.T,
        frozen_in,
        frozen_out,
        train_in,
        train_out,
        routes.T,
        seq_ids.reshape(1, L),
        cotangent,
    )
    block_out, input_grad, vecs, sums, grad_train_in, grad_train_out = outs
    sums = sums.reshape(4, D, W)
    return (
        block_out,
        input_grad,
        vecs[E + 8],
        vecs[E + 9],
        sums[:3].astype(F32),
        sums[3].T.astype(F32),
        vecs[E],
        vecs[E + 1],
        vecs[:E].T,
        grad_train_in,
        grad_train_out,
    )


def solution(mesh):
    return jax.shard_map(
        shards,
        mesh=mesh,
        in_specs=(
            P(("dp", "head"), None),
            P(),
            P(),
            P(None, None, "head"),
            P("head", None),
            P(),
            P(),
            P(),
            P("dp", None, "head"),
            P("dp", "head", None),
            P("dp", None, "head"),
            P("dp", "head", None),
            P(("dp", "head"), None),
            P("dp"),
            P(("dp", "head"), None),
        ),
        out_specs=(
            P(("dp", "head"), None),
            P(("dp", "head"), None),
            P(),
            P(),
            P(None, None, "head"),
            P("head", None),
            P(),
            P(),
            P(),
            P("dp", None, "head"),
            P("dp", "head", None),
        ),
        check_vma=False,
    )
```

```python
import functools

import jax
import jax.numpy as jnp
from jax import lax
from jax.experimental import pallas as pl
from jax.experimental.pallas import tpu as pltpu
from jax.sharding import PartitionSpec as P

HEAD_DIM = 64
EPS = 1e-05
NEG = -1e30
FW = 256
F32 = jnp.float32
BF = jnp.bfloat16
MESH = pl.DeviceIdType.MESH
VMEM = pltpu.VMEM


def contract(left, right, left_dim, right_dim, precision=None):
    return lax.dot_general(
        left,
        right,
        (((left_dim,), (right_dim,)), ((), ())),
        precision=precision,
        preferred_element_type=F32,
    )


def mm(left, right):
    return contract(left, right, 1, 0)


def mm_nt(left, right):
    return contract(left, right, 1, 1)


def mm_tn(left, right):
    return contract(left, right, 0, 0)


def normalize(values):
    average = jnp.mean(values, axis=-1, keepdims=True)
    centred = values - average
    variance = jnp.mean(centred * centred, axis=-1, keepdims=True)
    inverse = lax.rsqrt(variance + EPS)
    return centred * inverse, inverse


def norm_back(grad_norm, normal, inverse, gain_vec):
    scaled = grad_norm * gain_vec
    first_mean = jnp.mean(scaled, axis=-1, keepdims=True)
    second_mean = jnp.mean(scaled * normal, axis=-1, keepdims=True)
    return inverse * (scaled - first_mean - normal * second_mean)


def nearest(place, step, count):
    low, high = place, count - 1 - place
    both = jnp.minimum(low, high)
    near = jnp.where(step % 2 == 1, place - (step + 1) // 2, place + step // 2)
    far = jnp.where(low > high, place - (step - both), place + (step - both))
    return jnp.where(step <= 2 * both, near, far)


class Line:
    def __init__(self, ref_of, send, recv, place, count):
        self.ref_of, self.send, self.recv = ref_of, send, recv
        self.place, self.count = place, count

    def copy(self, block, up):
        step = 1 if up else -1
        return pltpu.make_async_remote_copy(
            src_ref=self.ref_of(block),
            dst_ref=self.ref_of(block),
            send_sem=self.send.at[0 if up else 1, block],
            recv_sem=self.recv.at[block],
            device_id={"head": self.place + step},
            device_id_type=MESH,
        )

    def pass_on(self, block):
        @pl.when((block <= self.place) & (self.place < self.count - 1))
        def _():
            self.copy(block, True).start()

        @pl.when((block >= self.place) & (self.place > 0))
        def _():
            self.copy(block, False).start()

    def arrive(self, block):
        self.copy(block, True).wait_recv()

    def finish(self):
        for block in range(self.count):

            @pl.when((block <= self.place) & (self.place < self.count - 1))
            def _():
                self.copy(block, True).wait_send()

            @pl.when((block >= self.place) & (self.place > 0))
            def _():
                self.copy(block, False).wait_send()


class Exchange:
    def __init__(self, axis, place, count, source, target, send, recv, device=None):
        self.axis, self.place, self.count = axis, place, count
        self.source, self.target, self.send, self.recv = source, target, send, recv
        self.device = device or (lambda peer: peer)

    def copy(self, peer, lands):
        return pltpu.make_async_remote_copy(
            src_ref=self.source(peer),
            dst_ref=self.target(lands),
            send_sem=self.send.at[peer],
            recv_sem=self.recv.at[lands],
            device_id={self.axis: self.device(peer)},
            device_id_type=MESH,
        )

    def loop(self, act):
        def body(step, carry):
            act(lax.rem(self.place + step, self.count))
            return carry

        lax.fori_loop(1, self.count, body, 0)

    def start_one(self, peer):
        self.copy(peer, self.place).start()

    def start(self):
        self.loop(self.start_one)

    def arrive(self):
        self.loop(lambda peer: self.copy(peer, peer).wait_recv())

    def finish(self):
        self.loop(lambda peer: self.copy(peer, self.place).wait_send())


def body(
    block_in,
    first_gain,
    first_bias,
    qkv_weight,
    out_weight,
    second_gain,
    second_bias,
    router,
    frozen_in,
    frozen_out,
    train_in,
    train_out,
    routes,
    seq,
    cotangent,
    block_out,
    input_grad,
    vec_out,
    weights_out,
    grad_in_out,
    grad_out_out,
    s,
    cfg,
):
    n, S, T, D, L = cfg["n"], cfg["S"], cfg["T"], cfg["D"], cfg["L"]
    E, R, W, HID, cap = cfg["E"], cfg["R"], cfg["W"], cfg["HID"], cfg["cap"]
    NF = D // FW
    M = E * R
    heads = W // HEAD_DIM
    SB = 4 if S % 4 == 0 else 1
    RB = SB * R
    half = L // 2
    chips = S // 2
    group = cfg["group"]
    part = W // group
    z = lax.axis_index("head")
    d = lax.axis_index("dp")

    loads = []
    for index, ref in enumerate((frozen_in, train_in, frozen_out, train_out)):
        loads.append(pltpu.make_async_copy(ref.at[0], s.experts.at[index], s.load_sem.at[index]))
        loads[-1].start()
    barrier = pltpu.get_barrier_semaphore()
    for step in range(1, n):
        pl.semaphore_signal(barrier, 1, device_id={"head": lax.rem(z + step, n)}, device_id_type=MESH)

    def greet(step, carry):
        pl.semaphore_signal(barrier, 1, device_id={"dp": lax.rem(d + step, S)}, device_id_type=MESH)
        return carry

    lax.fori_loop(1, S, greet, 0)

    normal_one, inverse_one = normalize(block_in[...])
    s.normal_one[...] = normal_one
    s.inverse_one[...] = jnp.broadcast_to(inverse_one, s.inverse_one.shape)
    s.normed[z] = (normal_one * first_gain[...].reshape(1, D) + first_bias[...].reshape(1, D)).astype(BF)
    for f in range(NF):
        s.cots[f, z] = cotangent[:, f * FW : (f + 1) * FW].astype(BF)
    s.routes[z] = routes[...]
    part_id = lax.rem(d, group)
    for q in range(group):
        s.outw[z, q] = out_weight[q * part : (q + 1) * part, :]
    pl.semaphore_wait(barrier, n - 1 + S - 1)

    def over_z(source, target, send, recv):
        return Exchange("head", z, n, source, target, send, recv)

    routes_x = over_z(lambda p: s.routes.at[z], lambda p: s.routes.at[p], s.routes_s, s.routes_r)
    routes_x.start()
    T2 = T // 2
    normed_lines = [
        Line(lambda b, h=h: s.normed.at[b, pl.ds(h * T2, T2), :], s.normed_s.at[h], s.normed_r.at[h], z, n)
        for h in range(2)
    ]
    cot_lines = [Line(lambda b, f=f: s.cots.at[f, b], s.cot_s.at[f], s.cot_r.at[f], z, n) for f in range(NF)]
    for line in normed_lines:
        line.pass_on(z)
    outw_x = over_z(
        lambda p: s.outw.at[z, part_id], lambda p: s.outw.at[p, part_id], s.outw_s, s.outw_r
    )
    outw_x.start()

    def project(block):
        rows = pl.ds(pl.multiple_of(block * T, T), T)
        normed = s.normed[block]
        for index in range(3):
            value = mm_nt(normed, qkv_weight[index]).astype(BF)
            if index == 0:
                value = value * jnp.asarray(HEAD_DIM**-0.5, BF)
            s.qkv[index, rows, :] = value

    project(z)
    routes_x.arrive()

    expert_col = lax.broadcasted_iota(jnp.int32, (E, T), 0)
    earlier = (
        lax.broadcasted_iota(jnp.int32, (T, T), 0) < lax.broadcasted_iota(jnp.int32, (T, T), 1)
    ).astype(F32).astype(BF)
    row_ids = lax.broadcasted_iota(jnp.int32, (M, T), 0)
    for j in range(n):
        first, second = s.routes[j, 0:1, :], s.routes[j, 1:2, :]
        hot0, hot1 = expert_col == first, expert_col == second
        hot = jnp.where(hot0 | hot1, 1.0, 0.0)
        count = mm(hot.astype(BF), earlier)
        for k, (names, hit) in enumerate(((first, hot0), (second, hot1))):
            slot = jnp.sum(jnp.where(hit, count, 0.0), axis=0, keepdims=True).astype(jnp.int32)
            late = names >= S
            owner = jnp.where(late, names - S, names)
            row = (owner * 2 + jnp.where(late, 1, 0)) * R + j * cap + slot
            s.target[j, k : k + 1, :] = jnp.where(slot < cap, row, -1)
        s.place[:, j * T : (j + 1) * T] = jnp.where(
            (row_ids == s.target[j, 0:1, :]) | (row_ids == s.target[j, 1:2, :]), 1.0, 0.0
        ).astype(BF)

    def end_of_line(block):
        @pl.when((block == 0) & (z < n - 1))
        def _():
            for line in cot_lines:
                line.copy(z, True).start()

        @pl.when((block == n - 1) & (z > 0))
        def _():
            for line in cot_lines:
                line.copy(z, False).start()

    end_of_line(z)
    for step in range(1, n):
        block = nearest(z, step, n)
        for line in normed_lines:
            line.arrive(block)
            line.pass_on(block)
        end_of_line(block)
        project(block)

    base = d - part_id
    plane = []
    outw_x.arrive()
    for step in range(1, n):
        other = lax.rem(z + step, n)
        plane.append(
            Exchange(
                "dp",
                part_id,
                group,
                lambda p, other=other: s.outw.at[other, part_id],
                lambda p, other=other: s.outw.at[other, p],
                s.outw_ps.at[step],
                s.outw_pr.at[step],
                device=lambda p: base + p,
            )
        )
        plane[-1].start()

    def lanes_of(rows):
        return lax.broadcasted_iota(jnp.int32, (rows, W), 1) // HEAD_DIM

    two = seq[0:1, L - 1 : L] > 0
    lane_t = lanes_of(T)
    mixed_x = over_z(lambda p: s.mixed.at[p], lambda p: s.mixed_in.at[p], s.mixed_s, s.mixed_r)

    inner_place = (z > 0) & (z < n - 1)

    def cot_service(step):
        @pl.when(inner_place)
        def _():
            block = nearest(z, step, n)
            for line in cot_lines:
                line.arrive(block)
                line.pass_on(block)

    for qi in range(n):
        keys = (qi + 1) * T
        query_pos = lax.broadcasted_iota(jnp.int32, (T, keys), 0) + qi * T
        key_pos = lax.broadcasted_iota(jnp.int32, (T, keys), 1)
        allowed = query_pos >= key_pos
        if (qi * T) // half > 0:
            allowed = allowed & ((key_pos >= half) | jnp.logical_not(two))
        queries = s.qkv[0, qi * T : (qi + 1) * T, :].astype(F32)
        out = jnp.zeros((T, W), F32)
        for h in range(heads):
            masked_q = jnp.where(lane_t == h, queries, 0.0).astype(BF)
            scores = jnp.where(allowed, mm_nt(masked_q, s.qkv[1, :keys, :]), NEG)
            exp_vals = jnp.exp(scores - jnp.max(scores, axis=1, keepdims=True))
            weights = (exp_vals / jnp.sum(exp_vals, axis=1, keepdims=True)).astype(BF)
            s.probs[h, qi * T : (qi + 1) * T, :keys] = weights
            out = jnp.where(lane_t == h, mm(weights, s.qkv[2, :keys, :]), out)
        s.mixed[qi] = out.astype(BF)

        @pl.when(z != qi)
        def _():
            mixed_x.start_one(qi)

        if qi == 0 and n > 2:
            cot_service(1)
        if qi == 1 and n > 2:
            cot_service(2)

    for step in range(3, n):
        cot_service(step)

    @pl.when(jnp.logical_not(inner_place))
    def _():
        for step in range(1, n):
            block = nearest(z, step, n)
            for line in cot_lines:
                line.arrive(block)
                line.pass_on(block)

    def dispatch(rows_ref, out_ref, in_ref, send, recv, f):
        tokens = rows_ref[f].reshape(n * T, FW)
        for half_id in range(2):
            span = S // 2
            rows = slice(half_id * span * 2 * R, (half_id + 1) * span * 2 * R)
            value = mm(s.place[rows, :], tokens).astype(BF)
            out_ref[f, half_id * span : (half_id + 1) * span] = value.reshape(span, 2, R, FW)
        exchange = Exchange(
            "dp", d, S, lambda p: out_ref.at[f, p], lambda p: in_ref.at[f, :, p], send.at[f], recv.at[f]
        )
        exchange.start()
        in_ref[f, :, d] = out_ref[f, d]
        return exchange

    cot_x = [None] * NF
    for f in range(NF - 1):
        cot_x[f] = dispatch(s.cots, s.cot_out, s.cot_in, s.cotx_s, s.cotx_r, f)

    for exchange in plane:
        exchange.arrive()
    mixed_x.arrive()
    s.mixed_in[z] = s.mixed[z]
    branch = jnp.zeros((T, D), F32)
    for j in range(n):
        branch = branch + mm(s.mixed_in[j], s.outw[j].reshape(W, D))
    residual = block_in[...] + branch
    s.residual[...] = residual
    normal_two, inverse_two = normalize(residual)
    s.normal_two[...] = normal_two
    s.inverse_two[...] = jnp.broadcast_to(inverse_two, s.inverse_two.shape)
    second_b = (normal_two * second_gain[...].reshape(1, D) + second_bias[...].reshape(1, D)).astype(BF)
    for f in range(NF):
        s.second[f, z] = second_b[:, f * FW : (f + 1) * FW]
    second_lines = [
        Line(lambda b, f=f: s.second.at[f, b], s.second_s.at[f], s.second_r.at[f], z, n) for f in range(NF)
    ]
    for line in second_lines:
        line.pass_on(z)
    row_x = []
    for f in range(NF):
        for step in range(1, n):
            block = nearest(z, step, n)
            second_lines[f].arrive(block)
            second_lines[f].pass_on(block)
        row_x.append(dispatch(s.second, s.row_out, s.row_in, s.rowx_s, s.rowx_r, f))
    cot_x[NF - 1] = dispatch(s.cots, s.cot_out, s.cot_in, s.cotx_s, s.cotx_r, NF - 1)

    for j in range(n):
        logits = jnp.zeros((E, T), F32)
        for f in range(NF):
            logits = logits + mm_nt(router[:, f * FW : (f + 1) * FW], s.second[f, j])
        hot0, hot1 = expert_col == s.routes[j, 0:1, :], expert_col == s.routes[j, 1:2, :]
        pick0 = jnp.sum(jnp.where(hot0, logits, 0.0), axis=0, keepdims=True)
        pick1 = jnp.sum(jnp.where(hot1, logits, 0.0), axis=0, keepdims=True)
        top = jnp.maximum(pick0, pick1)
        exp0, exp1 = jnp.exp(pick0 - top), jnp.exp(pick1 - top)
        s.gates[j, 0:1, :] = exp0 / (exp0 + exp1)
        s.gates[j, 1:2, :] = exp1 / (exp0 + exp1)
        s.gates[j, 2:4, :] = s.target[j, 0:2, :].astype(F32)
        s.gates[j, 4:8, :] = jnp.zeros((4, T), F32)
        columns = jnp.transpose(s.gates[j])
        lane_ids = lax.broadcasted_iota(jnp.int32, (T, M), 1).astype(F32)
        s.combine[j * T : (j + 1) * T, :] = jnp.where(
            lane_ids == columns[:, 2:3],
            columns[:, 0:1],
            jnp.where(lane_ids == columns[:, 3:4], columns[:, 1:2], 0.0),
        ).astype(BF)
    slot_ids = lax.broadcasted_iota(jnp.int32, (R, T), 0)
    lane_128 = lax.broadcasted_iota(jnp.int32, (128, 128), 1)
    table = jnp.zeros((128, 128), F32)
    for owner in range(S):
        total = jnp.zeros((R, T), F32)
        ids = slot_ids + (owner * 2 + 1) * R
        for j in range(n):
            total = total + jnp.where(
                ids == s.target[j, 0:1, :],
                s.gates[j, 0:1, :],
                jnp.where(ids == s.target[j, 1:2, :], s.gates[j, 1:2, :], 0.0),
            )
        column = jnp.sum(total, axis=1, keepdims=True)
        if R < 128:
            column = jnp.concatenate([column, jnp.zeros((128 - R, 1), F32)], axis=0)
        table = jnp.where(lane_128 == owner, column, table)
    table = jnp.transpose(table)
    for owner in range(S):
        s.gate_out[owner] = jnp.broadcast_to(table[owner : owner + 1, :], (8, 128))
    gate_x = Exchange(
        "dp", d, S, lambda p: s.gate_out.at[p], lambda p: s.gate_in.at[p], s.gate_s, s.gate_r
    )
    gate_x.start()
    s.gate_in[d] = s.gate_out[d]

    for load in loads:
        load.wait()

    def row_blocks(act):
        def step(i, carry):
            act(i * SB, pl.multiple_of(i * RB, RB))
            return carry

        lax.fori_loop(0, S // SB, step, 0)

    def add_up(total_ref, rows_ref, f, transposed):
        for g in range(2):

            def act(block, row):
                value = rows_ref[f, g, pl.ds(block, SB)].reshape(RB, FW)
                if transposed:
                    piece = mm_nt(value, s.experts[2 + g, :, f * FW : (f + 1) * FW])
                else:
                    piece = mm(value, s.experts[g, f * FW : (f + 1) * FW, :])
                rows = pl.ds(g * S * R + row, RB)
                total_ref[rows, :] = piece if f == 0 else total_ref[rows, :] + piece

            row_blocks(act)

    for f in range(NF - 1):
        cot_x[f].arrive()
        add_up(s.grad_active, s.cot_in, f, True)
    for f in range(NF):
        row_x[f].arrive()
        add_up(s.hidden, s.row_in, f, False)
    EB = 16 if R % 16 == 0 else 8

    for g in range(2):

        def activate(i, carry):
            rows = pl.ds(pl.multiple_of(i * EB, EB), EB)
            flat = pl.ds(pl.multiple_of(g * S * R + i * EB, EB), EB)
            value = s.hidden[flat, :]
            normal_cdf = 0.5 * (1.0 + lax.erf(value * 0.7071067811865476))
            s.active[g, rows, :] = (value * normal_cdf).astype(BF)
            s.hidden[flat, :] = normal_cdf + value * jnp.exp(-0.5 * value * value) * 0.3989422804014327
            return carry

        lax.fori_loop(0, S * R // EB, activate, 0)

    cot_x[NF - 1].arrive()
    add_up(s.grad_active, s.cot_in, NF - 1, True)

    tables = []
    for g in range(2):
        table = jnp.zeros((128, 128), F32)
        for source in range(S):
            sums = []
            for i in range(R // EB):
                rows = slice(source * R + i * EB, source * R + (i + 1) * EB)
                flat = slice(g * S * R + rows.start, g * S * R + rows.stop)
                grad = s.grad_active[flat, :]
                s.grad_hidden[g, rows, :] = (grad * s.hidden[flat, :]).astype(BF)
                sums.append(
                    jnp.sum(grad * s.active[g, rows, :].astype(F32), axis=1, keepdims=True)
                )
            if R < 128:
                sums.append(jnp.zeros((128 - R, 1), F32))
            table = jnp.where(lane_128 == source, jnp.concatenate(sums, axis=0), table)
        tables.append(jnp.transpose(table))
    row_8 = lax.broadcasted_iota(jnp.int32, (8, 128), 0)
    for source in range(S):
        s.dot_out[source] = jnp.where(
            row_8 == 0, tables[0][source : source + 1, :], tables[1][source : source + 1, :]
        )
    dot_x = Exchange("dp", d, S, lambda p: s.dot_out.at[p], lambda p: s.dot_in.at[p], s.dot_s, s.dot_r)
    dot_x.start()
    s.dot_in[d] = s.dot_out[d]

    def give_back(rows_ref, first_weight, out_ref, in_ref, send, recv, transposed):
        exchanges = []
        for f in range(NF):
            for g in range(2):

                def act(block, row):
                    value = rows_ref[g, pl.ds(row, RB), :]
                    if transposed:
                        piece = mm_nt(value, s.experts[first_weight + g, f * FW : (f + 1) * FW, :])
                    else:
                        piece = mm(value, s.experts[first_weight + g, :, f * FW : (f + 1) * FW])
                    out_ref[f, pl.ds(block, SB), g] = piece.astype(BF).reshape(SB, R, FW)

                row_blocks(act)
            exchange = Exchange(
                "dp",
                d,
                S,
                lambda p, f=f: out_ref.at[f, p],
                lambda p, f=f: in_ref.at[f, p],
                send.at[f],
                recv.at[f],
            )
            exchange.start()
            in_ref[f, d] = out_ref[f, d]
            exchanges.append(exchange)
        return exchanges

    if cfg["tight"]:
        for exchange in cot_x + row_x:
            exchange.finish()
        down_out, fore_out = s.cot_out, s.row_out
    else:
        down_out, fore_out = s.down_out, s.fore_out
    down_x = give_back(s.grad_hidden, 0, down_out, s.down_in, s.down_s, s.down_r, True)
    fore_x = give_back(s.active, 2, fore_out, s.fore_in, s.fore_s, s.fore_r, False)

    gate_x.arrive()
    columns = jnp.transpose(s.gate_in[:, 0, :])
    for source in range(S):
        column = columns[:R, source : source + 1]
        rows = slice(source * R, (source + 1) * R)
        s.active[1, rows, :] = (s.active[1, rows, :].astype(F32) * column).astype(BF)
        s.grad_hidden[1, rows, :] = (s.grad_hidden[1, rows, :].astype(F32) * column).astype(BF)
    for f in range(NF):
        s.hidden[f * FW : (f + 1) * FW, :] = mm_tn(
            s.row_in[f, 1].reshape(S * R, FW), s.grad_hidden[1]
        )
        s.grad_active[0:HID, f * FW : (f + 1) * FW] = mm_tn(
            s.active[1], s.cot_in[f, 1].reshape(S * R, FW)
        )
    stores = [
        pltpu.make_async_copy(s.hidden.at[0:D, :], grad_in_out.at[0], s.store_sem.at[0]),
        pltpu.make_async_copy(s.grad_active.at[0:HID, :], grad_out_out.at[0], s.store_sem.at[1]),
    ]
    for store in stores:
        store.start()

    def gather_rows(in_ref, f):
        return mm(s.combine[...], in_ref[f].reshape(M, FW)).astype(BF).reshape(n, T, FW)

    def token_sums(exchanges, in_ref, part_ref, sum_ref, send, recv):
        result = []
        for f in range(NF):
            exchanges[f].arrive()
            part_ref[f] = gather_rows(in_ref, f)
            sums_x = over_z(
                lambda p, f=f: part_ref.at[f, p], lambda p, f=f: sum_ref.at[f, p], send.at[f], recv.at[f]
            )
            sums_x.start()
            sum_ref[f, z] = part_ref[f, z]
            result.append(sums_x)
        return result

    def add_sums(sums_x, sum_ref):
        parts = []
        for f in range(NF):
            sums_x[f].arrive()
            total = sum_ref[f, 0].astype(F32)
            for j in range(1, n):
                total = total + sum_ref[f, j].astype(F32)
            parts.append(total)
        return jnp.concatenate(parts, axis=1)

    down_sums = token_sums(down_x, s.down_in, s.down_part, s.down_sum, s.dsum_s, s.dsum_r)

    dot_x.arrive()
    turned = [jnp.transpose(s.dot_in[:, g, :]) for g in range(2)]
    for j in range(n):
        total = jnp.zeros((R, T), F32)
        for owner in range(S):
            for g in range(2):
                ids = slot_ids + (owner * 2 + g) * R
                sign = jnp.where(
                    ids == s.target[j, 0:1, :], 1.0, jnp.where(ids == s.target[j, 1:2, :], -1.0, 0.0)
                )
                total = total + sign * turned[g][:R, owner : owner + 1]
        s.delta_out[j] = jnp.broadcast_to(jnp.sum(total, axis=0, keepdims=True), (8, T))
    delta_x = over_z(
        lambda p: s.delta_out.at[p], lambda p: s.delta_in.at[p], s.delta_s, s.delta_r
    )
    delta_x.start()
    s.delta_in[z] = s.delta_out[z]
    delta_x.arrive()
    delta = s.delta_in[0, 0:1, :]
    for j in range(1, n):
        delta = delta + s.delta_in[j, 0:1, :]

    grad_chosen = s.gates[z, 0:1, :] * s.gates[z, 1:2, :] * delta
    hot0, hot1 = expert_col == s.routes[z, 0:1, :], expert_col == s.routes[z, 1:2, :]
    grad_logits = jnp.where(hot0, grad_chosen, jnp.where(hot1, -grad_chosen, 0.0))
    router_part = contract(grad_logits, router[...].astype(F32), 0, 0, lax.Precision.HIGHEST)
    for f in range(NF):
        s.early[0:E, f * FW : (f + 1) * FW] = contract(
            grad_logits, s.second[f, z].astype(F32), 1, 0, lax.Precision.HIGHEST
        )
    grad_second = add_sums(down_sums, s.down_sum) + router_part
    normal_two = s.normal_two[...]
    pair = jnp.concatenate(
        [
            jnp.sum(grad_second * normal_two, axis=0, keepdims=True),
            jnp.sum(grad_second, axis=0, keepdims=True),
            jnp.zeros((6, D), F32),
        ],
        axis=0,
    )
    s.early[E : E + 8, :] = pair
    grad_residual = cotangent[...] + norm_back(
        grad_second, normal_two, s.inverse_two[:, 0:1], second_gain[...].reshape(1, D)
    )
    s.grad_residual[...] = grad_residual
    s.branch[z] = grad_residual.astype(BF)
    branch_lines = [
        Line(lambda b, h=h: s.branch.at[b, pl.ds(h * T2, T2), :], s.branch_s.at[h], s.branch_r.at[h], z, n)
        for h in range(2)
    ]
    for line in branch_lines:
        line.pass_on(z)

    def mixed_back(block):
        s.grad_mixed[pl.ds(pl.multiple_of(block * T, T), T), :] = mm_nt(
            s.branch[block], out_weight[...]
        ).astype(BF)

    mixed_back(z)
    early_x = Exchange(
        "dp",
        part_id,
        group,
        lambda p: s.early,
        lambda p: s.early_dp.at[p],
        s.early_s,
        s.early_r,
        device=lambda p: base + p,
    )
    early_x.start()
    s.early_dp[part_id] = s.early[...]
    for step in range(1, n):
        block = nearest(z, step, n)
        for line in branch_lines:
            line.arrive(block)
            line.pass_on(block)
        mixed_back(block)

    if cfg["tight"]:
        for exchange in down_sums:
            exchange.finish()
        fore_part = s.down_part
    else:
        fore_part = s.fore_part
    fore_sums = token_sums(fore_x, s.fore_in, fore_part, s.fore_sum, s.fsum_s, s.fsum_r)

    for qi in range(n):
        keys = (qi + 1) * T
        rows = slice(qi * T, (qi + 1) * T)
        grads = s.grad_mixed[rows, :]
        grads_f = grads.astype(F32)
        lane_k = lanes_of(keys)
        grad_q = jnp.zeros((T, W), F32)
        grad_k = jnp.zeros((keys, W), F32)
        grad_v = jnp.zeros((keys, W), F32)
        for h in range(heads):
            masked = jnp.where(lane_t == h, grads_f, 0.0).astype(BF)
            grad_w = mm_nt(masked, s.qkv[2, :keys, :])
            weights = s.probs[h, rows, :keys]
            probs = weights.astype(F32)
            inner = jnp.sum(probs * grad_w, axis=1, keepdims=True)
            grad_s = (probs * (grad_w - inner)).astype(BF)
            grad_q = jnp.where(lane_t == h, mm(grad_s, s.qkv[1, :keys, :]), grad_q)
            grad_k = jnp.where(lane_k == h, mm_tn(grad_s, s.qkv[0, rows, :]), grad_k)
            grad_v = jnp.where(lane_k == h, mm_tn(weights, grads), grad_v)
        s.grad_proj[0, rows, :] = (grad_q * HEAD_DIM**-0.5).astype(BF)
        if qi == 0:
            s.grad_kv[...] = jnp.zeros(s.grad_kv.shape, F32)
        s.grad_kv[0, :keys, :] = s.grad_kv[0, :keys, :] + grad_k
        s.grad_kv[1, :keys, :] = s.grad_kv[1, :keys, :] + grad_v
    for index in range(2):
        s.grad_proj[1 + index] = s.grad_kv[index].astype(BF)

    def first_part(block):
        rows = pl.ds(pl.multiple_of(block * T, T), T)
        total = mm(s.grad_proj[0, rows, :], qkv_weight[0])
        for index in range(1, 3):
            total = total + mm(s.grad_proj[index, rows, :], qkv_weight[index])
        s.first_out[block] = total.astype(BF)

    first_x = over_z(lambda p: s.first_out.at[p], lambda p: s.first_in.at[p], s.first_s, s.first_r)
    for step in range(1, n):
        peer = nearest(z, n - step, n)
        first_part(peer)
        first_x.start_one(peer)
    first_part(z)
    s.first_in[z] = s.first_out[z]

    normed_all = s.normed[...].reshape(L, D)
    each = chips // 2
    size = W // each
    for index in range(4):
        if index < 3:
            value = mm_tn(s.grad_proj[index], normed_all)
        else:
            value = mm_tn(s.mixed[...].reshape(L, W), s.branch[...].reshape(L, D))
        for piece in range(each):
            s.wsum[index // 2, (index % 2) * each + piece] = value[
                piece * size : (piece + 1) * size, :
            ].astype(BF)
    core = lax.rem(d, 2)
    chip = d // 2
    mate = d + 1 - 2 * core
    swap = pltpu.make_async_remote_copy(
        src_ref=s.wsum.at[1 - core],
        dst_ref=s.wswap,
        send_sem=s.swap_sem.at[0],
        recv_sem=s.swap_sem.at[1],
        device_id={"dp": mate},
        device_id_type=MESH,
    )
    swap.start()
    swap.wait_recv()
    s.wswap[...] = (s.wsum[core].astype(F32) + s.wswap[...].astype(F32)).astype(BF)

    def over_chips(source, target, send, recv):
        return Exchange("dp", chip, chips, source, target, send, recv, device=lambda p: 2 * p + core)

    pair_x = over_chips(lambda p: s.wswap.at[p], lambda p: s.wparts.at[p], s.pair_s, s.pair_r)
    pair_x.start()
    s.wparts[chip] = s.wswap[chip]

    early_x.arrive()
    total = s.early_dp[0]
    for peer in range(1, group):
        total = total + s.early_dp[peer]
    crowds = S // group
    far_x = []
    if crowds > 1:
        crowd = d // group
        s.early_far[crowd] = total
        far_x.append(
            Exchange(
                "dp",
                crowd,
                crowds,
                lambda p: s.early_far.at[crowd],
                lambda p: s.early_far.at[p],
                s.earlyf_s,
                s.earlyf_r,
                device=lambda p: p * group + part_id,
            )
        )
        far_x[0].start()
        far_x[0].arrive()
        total = s.early_far[0]
        for peer in range(1, crowds):
            total = total + s.early_far[peer]
    s.early_z[z] = total
    early_zx = over_z(lambda p: s.early_z.at[z], lambda p: s.early_z.at[p], s.earlyz_s, s.earlyz_r)
    early_zx.start()

    pair_x.arrive()
    total = s.wparts[0].astype(F32)
    for peer in range(1, chips):
        total = total + s.wparts[peer].astype(F32)
    s.wfull[core, chip] = total.astype(BF)
    full_x = over_chips(
        lambda p: s.wfull.at[core, chip], lambda p: s.wfull.at[core, p], s.full_s, s.full_r
    )
    full_x.start()

    block_out[...] = s.residual[...] + add_sums(fore_sums, s.fore_sum)

    first_x.arrive()
    grad_first = s.first_in[0].astype(F32)
    for j in range(1, n):
        grad_first = grad_first + s.first_in[j].astype(F32)
    normal_one = s.normal_one[...]
    s.late[...] = jnp.concatenate(
        [
            jnp.sum(grad_first * normal_one, axis=0, keepdims=True),
            jnp.sum(grad_first, axis=0, keepdims=True),
            jnp.zeros((6, D), F32),
        ],
        axis=0,
    )
    late_x = Exchange("dp", d, S, lambda p: s.late, lambda p: s.late_dp.at[p], s.late_s, s.late_r)
    late_x.start()
    s.late_dp[d] = s.late[...]
    input_grad[...] = s.grad_residual[...] + norm_back(
        grad_first, normal_one, s.inverse_one[:, 0:1], first_gain[...].reshape(1, D)
    )
    full_x.arrive()
    back = pltpu.make_async_remote_copy(
        src_ref=s.wfull.at[core],
        dst_ref=s.wfull.at[core],
        send_sem=s.swap_sem.at[2],
        recv_sem=s.swap_sem.at[3],
        device_id={"dp": mate},
        device_id_type=MESH,
    )
    back.start()
    late_x.arrive()
    total = s.late_dp[0]
    for peer in range(1, S):
        total = total + s.late_dp[peer]
    s.late_z[z] = total
    late_zx = over_z(lambda p: s.late_z.at[z], lambda p: s.late_z.at[p], s.latez_s, s.latez_r)
    late_zx.start()
    early_zx.arrive()
    total = s.early_z[0]
    for j in range(1, n):
        total = total + s.early_z[j]
    vec_out[0 : E + 8, :] = total
    late_zx.arrive()
    total = s.late_z[0]
    for j in range(1, n):
        total = total + s.late_z[j]
    vec_out[E + 8 : E + 16, :] = total
    pltpu.make_async_remote_copy(
        src_ref=s.wfull.at[core],
        dst_ref=s.wfull.at[1 - core],
        send_sem=s.swap_sem.at[2],
        recv_sem=s.swap_sem.at[3],
        device_id={"dp": mate},
        device_id_type=MESH,
    ).wait_recv()
    sums_store = pltpu.make_async_copy(s.wfull, weights_out, s.store_sem.at[2])
    sums_store.start()
    stores.append(sums_store)

    for store in stores:
        store.wait()
    swap.wait_send()
    back.wait_send()
    for lines in (normed_lines, cot_lines, second_lines, branch_lines):
        for line in lines:
            line.finish()
    done = [routes_x, outw_x, gate_x, dot_x, delta_x, early_x, pair_x, early_zx, full_x, first_x, late_x]
    if not cfg["tight"]:
        done += cot_x + row_x + down_sums
    done += far_x + [late_zx, mixed_x] + plane + down_x + fore_x + fore_sums
    for exchange in done:
        exchange.finish()


def hand_over(E, *refs):
    given, vecs = refs[:5], refs[5]
    large, small = refs[6:12], refs[12:17]
    held, narrow, wide, load_sem, store_sem = refs[17:21], refs[21], refs[22], refs[23], refs[24]
    loads = [
        pltpu.make_async_copy(given[index], (list(held) + [narrow])[index], load_sem.at[index])
        for index in range(5)
    ]
    for load in (loads[4], *loads[:4]):
        load.start()
    sources = [*held, wide.at[0:3], wide.at[3]]
    stores = [
        pltpu.make_async_copy(sources[index], large[index], store_sem.at[index]) for index in range(6)
    ]
    small[0][...] = vecs[0:E, :]
    D = vecs.shape[1]
    for index, row in enumerate((E + 8, E + 9, E, E + 1)):
        small[1 + index][...] = vecs[row : row + 1, :].reshape(D)
    loads[4].wait()
    wide[...] = narrow[...].astype(F32)
    stores[4].start()
    stores[5].start()
    for index in range(4):
        loads[index].wait()
        stores[index].start()
    for store in stores:
        store.wait()


class Names:
    pass


def shards(
    block_in,
    first_gain,
    first_bias,
    qkv_weight,
    out_weight,
    second_gain,
    second_bias,
    router_weight,
    frozen_in,
    frozen_out,
    train_in,
    train_out,
    routes,
    seq_ids,
    cotangent,
):
    T, D = block_in.shape
    L = seq_ids.shape[0]
    E = router_weight.shape[1]
    S, n = lax.axis_size("dp"), lax.axis_size("head")
    W = qkv_weight.shape[2]
    HID = frozen_in.shape[2]
    cap = max(2, 5 * T // (2 * E))
    R = -(-(n * cap) // 8) * 8
    M = E * R
    NF = D // FW
    chips = S // 2
    each = chips // 2
    group = 8
    tight = S > group
    cfg = dict(tight=tight, n=n, S=S, T=T, D=D, L=L, E=E, R=R, W=W, HID=HID, cap=cap, group=group)
    DMA = pltpu.SemaphoreType.DMA
    scratch = dict(
        experts=VMEM((4, D, HID), BF),
        normal_one=VMEM((T, D), F32),
        inverse_one=VMEM((T, 128), F32),
        normed=VMEM((n, T, D), BF),
        cots=VMEM((NF, n, T, FW), BF),
        routes=VMEM((n, 2, T), jnp.int32),
        outw=VMEM((n, group, W // group, D), BF),
        qkv=VMEM((3, L, W), BF),
        target=VMEM((n, 8, T), jnp.int32),
        gates=VMEM((n, 8, T), F32),
        place=VMEM((M, L), BF),
        combine=VMEM((L, M), BF),
        probs=VMEM((W // HEAD_DIM, L, L), BF),
        mixed=VMEM((n, T, W), BF),
        mixed_in=VMEM((n, T, W), BF),
        residual=VMEM((T, D), F32),
        normal_two=VMEM((T, D), F32),
        inverse_two=VMEM((T, 128), F32),
        second=VMEM((NF, n, T, FW), BF),
        cot_out=VMEM((NF, S, 2, R, FW), BF),
        cot_in=VMEM((NF, 2, S, R, FW), BF),
        row_out=VMEM((NF, S, 2, R, FW), BF),
        row_in=VMEM((NF, 2, S, R, FW), BF),
        gate_out=VMEM((S, 8, 128), F32),
        gate_in=VMEM((S, 8, 128), F32),
        hidden=VMEM((2 * S * R, HID), F32),
        grad_active=VMEM((2 * S * R, HID), F32),
        active=VMEM((2, S * R, HID), BF),
        grad_hidden=VMEM((2, S * R, HID), BF),
        dot_out=VMEM((S, 8, 128), F32),
        dot_in=VMEM((S, 8, 128), F32),
        down_out=VMEM((NF, S, 2, R, FW), BF),
        down_in=VMEM((NF, S, 2, R, FW), BF),
        fore_out=VMEM((NF, S, 2, R, FW), BF),
        fore_in=VMEM((NF, S, 2, R, FW), BF),
        down_part=VMEM((NF, n, T, FW), BF),
        down_sum=VMEM((NF, n, T, FW), BF),
        fore_part=VMEM((NF, n, T, FW), BF),
        fore_sum=VMEM((NF, n, T, FW), BF),
        delta_out=VMEM((n, 8, T), F32),
        delta_in=VMEM((n, 8, T), F32),
        early=VMEM((E + 8, D), F32),
        early_dp=VMEM((group, E + 8, D), F32),
        early_z=VMEM((n, E + 8, D), F32),
        late=VMEM((8, D), F32),
        late_dp=VMEM((S, 8, D), F32),
        late_z=VMEM((n, 8, D), F32),
        grad_residual=VMEM((T, D), F32),
        branch=VMEM((n, T, D), BF),
        grad_mixed=VMEM((L, W), BF),
        grad_proj=VMEM((3, L, W), BF),
        grad_kv=VMEM((2, L, W), F32),
        first_out=VMEM((n, T, D), BF),
        first_in=VMEM((n, T, D), BF),
        wsum=VMEM((2, chips, W // each, D), BF),
        wswap=VMEM((chips, W // each, D), BF),
        wparts=VMEM((chips, W // each, D), BF),
        wfull=VMEM((2, chips, W // each, D), BF),
        load_sem=DMA((4,)),
        store_sem=DMA((3,)),
        swap_sem=DMA((4,)),
        routes_s=DMA((n,)),
        routes_r=DMA((n,)),
        normed_s=DMA((2, 2, n)),
        normed_r=DMA((2, n)),
        cot_s=DMA((NF, 2, n)),
        cot_r=DMA((NF, n)),
        outw_s=DMA((n,)),
        outw_r=DMA((n,)),
        outw_ps=DMA((n, group)),
        outw_pr=DMA((n, group)),
        mixed_s=DMA((n,)),
        mixed_r=DMA((n,)),
        cotx_s=DMA((NF, S)),
        cotx_r=DMA((NF, S)),
        rowx_s=DMA((NF, S)),
        rowx_r=DMA((NF, S)),
        second_s=DMA((NF, 2, n)),
        second_r=DMA((NF, n)),
        gate_s=DMA((S,)),
        gate_r=DMA((S,)),
        dot_s=DMA((S,)),
        dot_r=DMA((S,)),
        down_s=DMA((NF, S)),
        down_r=DMA((NF, S)),
        fore_s=DMA((NF, S)),
        fore_r=DMA((NF, S)),
        dsum_s=DMA((NF, n)),
        dsum_r=DMA((NF, n)),
        fsum_s=DMA((NF, n)),
        fsum_r=DMA((NF, n)),
        delta_s=DMA((n,)),
        delta_r=DMA((n,)),
        branch_s=DMA((2, 2, n)),
        branch_r=DMA((2, n)),
        early_s=DMA((group,)),
        early_r=DMA((group,)),
        earlyz_s=DMA((n,)),
        earlyz_r=DMA((n,)),
        first_s=DMA((n,)),
        first_r=DMA((n,)),
        pair_s=DMA((chips,)),
        pair_r=DMA((chips,)),
        full_s=DMA((chips,)),
        full_r=DMA((chips,)),
        late_s=DMA((S,)),
        late_r=DMA((S,)),
        latez_s=DMA((n,)),
        latez_r=DMA((n,)),
    )
    if S > group:
        scratch.update(
            early_far=VMEM((S // group, E + 8, D), F32),
            earlyf_s=DMA((S // group,)),
            earlyf_r=DMA((S // group,)),
        )
    if tight:
        del scratch["down_out"], scratch["fore_out"], scratch["fore_part"]
    names = list(scratch)

    def kernel(*refs):
        space = Names()
        for name, ref in zip(names, refs[21:]):
            setattr(space, name, ref)
        body(*refs[:21], space, cfg)

    whole = pl.BlockSpec(memory_space=VMEM)
    left = pl.BlockSpec(memory_space=pl.ANY)
    outs = pl.pallas_call(
        kernel,
        out_shape=(
            jax.ShapeDtypeStruct((T, D), F32),
            jax.ShapeDtypeStruct((T, D), F32),
            jax.ShapeDtypeStruct((E + 16, D), F32),
            jax.ShapeDtypeStruct((2, chips, W // each, D), BF),
            jax.ShapeDtypeStruct((1, D, HID), F32),
            jax.ShapeDtypeStruct((1, HID, D), F32),
        ),
        in_specs=[whole] * 8 + [left] * 4 + [whole] * 3,
        out_specs=(whole, whole, whole, left, left, left),
        scratch_shapes=list(scratch.values()),
        compiler_params=pltpu.CompilerParams(
            collective_id=0, has_side_effects=True, vmem_limit_bytes=67043328
        ),
    )(
        block_in,
        first_gain,
        first_bias,
        jnp.swapaxes(qkv_weight, 1, 2),
        out_weight,
        second_gain,
        second_bias,
        router_weight.T,
        frozen_in,
        frozen_out,
        train_in,
        train_out,
        routes.T,
        seq_ids.reshape(1, L),
        cotangent,
    )
    block_out, input_grad, vecs, sums, grad_train_in, grad_train_out = outs
    sums = sums.reshape(4, W, D)
    big = [block_out, input_grad, grad_train_in, grad_train_out]
    vector = jax.ShapeDtypeStruct((D,), F32)
    done = pl.pallas_call(
        functools.partial(hand_over, E),
        out_shape=[jax.ShapeDtypeStruct(array.shape, F32) for array in big]
        + [
            jax.ShapeDtypeStruct((3, W, D), F32),
            jax.ShapeDtypeStruct((W, D), F32),
            jax.ShapeDtypeStruct((E, D), F32),
        ]
        + [vector] * 4,
        in_specs=[left] * 5 + [whole],
        out_specs=[left] * 6 + [whole] * 5,
        scratch_shapes=[VMEM(array.shape, F32) for array in big]
        + [VMEM((4, W, D), BF), VMEM((4, W, D), F32), DMA((5,)), DMA((6,))],
        compiler_params=pltpu.CompilerParams(vmem_limit_bytes=33554432),
    )(*big, sums, vecs)
    block_out, input_grad, grad_train_in, grad_train_out, grad_qkv, grad_out, grad_router = done[:7]
    return (
        block_out,
        input_grad,
        done[7],
        done[8],
        jnp.swapaxes(grad_qkv, 1, 2),
        grad_out,
        done[9],
        done[10],
        grad_router.T,
        grad_train_in,
        grad_train_out,
    )


def solution(mesh):
    return jax.shard_map(
        shards,
        mesh=mesh,
        in_specs=(
            P(("dp", "head"), None),
            P(),
            P(),
            P(None, None, "head"),
            P("head", None),
            P(),
            P(),
            P(),
            P("dp", None, "head"),
            P("dp", "head", None),
            P("dp", None, "head"),
            P("dp", "head", None),
            P(("dp", "head"), None),
            P("dp"),
            P(("dp", "head"), None),
        ),
        out_specs=(
            P(("dp", "head"), None),
            P(("dp", "head"), None),
            P(),
            P(),
            P(None, None, "head"),
            P("head", None),
            P(),
            P(),
            P(),
            P("dp", None, "head"),
            P("dp", "head", None),
        ),
        check_vma=False,
    )
```

```python
import functools

import jax
import jax.numpy as jnp
from jax import lax
from jax.experimental import pallas as pl
from jax.experimental.pallas import tpu as pltpu
from jax.sharding import PartitionSpec as P

HEAD_DIM = 64
EPS = 1e-05
NEG = -1e30
FW = 256
F32 = jnp.float32
BF = jnp.bfloat16
MESH = pl.DeviceIdType.MESH
VMEM = pltpu.VMEM


def contract(left, right, left_dim, right_dim, precision=None):
    return lax.dot_general(
        left,
        right,
        (((left_dim,), (right_dim,)), ((), ())),
        precision=precision,
        preferred_element_type=F32,
    )


def mm(left, right):
    return contract(left, right, 1, 0)


def mm_nt(left, right):
    return contract(left, right, 1, 1)


def mm_tn(left, right):
    return contract(left, right, 0, 0)


def normalize(values):
    average = jnp.mean(values, axis=-1, keepdims=True)
    centred = values - average
    variance = jnp.mean(centred * centred, axis=-1, keepdims=True)
    inverse = lax.rsqrt(variance + EPS)
    return centred * inverse, inverse


def norm_back(grad_norm, normal, inverse, gain_vec):
    scaled = grad_norm * gain_vec
    first_mean = jnp.mean(scaled, axis=-1, keepdims=True)
    second_mean = jnp.mean(scaled * normal, axis=-1, keepdims=True)
    return inverse * (scaled - first_mean - normal * second_mean)


def nearest(place, step, count):
    low, high = place, count - 1 - place
    both = jnp.minimum(low, high)
    near = jnp.where(step % 2 == 1, place - (step + 1) // 2, place + step // 2)
    far = jnp.where(low > high, place - (step - both), place + (step - both))
    return jnp.where(step <= 2 * both, near, far)


class Line:
    def __init__(self, ref_of, send, recv, place, count):
        self.ref_of, self.send, self.recv = ref_of, send, recv
        self.place, self.count = place, count

    def copy(self, block, up):
        step = 1 if up else -1
        return pltpu.make_async_remote_copy(
            src_ref=self.ref_of(block),
            dst_ref=self.ref_of(block),
            send_sem=self.send.at[0 if up else 1, block],
            recv_sem=self.recv.at[block],
            device_id={"head": self.place + step},
            device_id_type=MESH,
        )

    def pass_on(self, block):
        @pl.when((block <= self.place) & (self.place < self.count - 1))
        def _():
            self.copy(block, True).start()

        @pl.when((block >= self.place) & (self.place > 0))
        def _():
            self.copy(block, False).start()

    def arrive(self, block):
        self.copy(block, True).wait_recv()

    def finish(self):
        for block in range(self.count):

            @pl.when((block <= self.place) & (self.place < self.count - 1))
            def _():
                self.copy(block, True).wait_send()

            @pl.when((block >= self.place) & (self.place > 0))
            def _():
                self.copy(block, False).wait_send()


class Exchange:
    def __init__(self, axis, place, count, source, target, send, recv, device=None):
        self.axis, self.place, self.count = axis, place, count
        self.source, self.target, self.send, self.recv = source, target, send, recv
        self.device = device or (lambda peer: peer)

    def copy(self, peer, lands):
        return pltpu.make_async_remote_copy(
            src_ref=self.source(peer),
            dst_ref=self.target(lands),
            send_sem=self.send.at[peer],
            recv_sem=self.recv.at[lands],
            device_id={self.axis: self.device(peer)},
            device_id_type=MESH,
        )

    def loop(self, act):
        def body(step, carry):
            act(lax.rem(self.place + step, self.count))
            return carry

        lax.fori_loop(1, self.count, body, 0)

    def start_one(self, peer):
        self.copy(peer, self.place).start()

    def start(self):
        self.loop(self.start_one)

    def arrive(self):
        self.loop(lambda peer: self.copy(peer, peer).wait_recv())

    def finish(self):
        self.loop(lambda peer: self.copy(peer, self.place).wait_send())


def body(
    block_in,
    first_gain,
    first_bias,
    qkv_weight,
    out_weight,
    second_gain,
    second_bias,
    router,
    frozen_in,
    frozen_out,
    train_in,
    train_out,
    routes,
    seq,
    cotangent,
    block_out,
    input_grad,
    vec_out,
    weights_out,
    grad_in_out,
    grad_out_out,
    s,
    cfg,
):
    n, S, T, D, L = cfg["n"], cfg["S"], cfg["T"], cfg["D"], cfg["L"]
    E, R, W, HID, cap = cfg["E"], cfg["R"], cfg["W"], cfg["HID"], cfg["cap"]
    NF = D // FW
    M = E * R
    heads = W // HEAD_DIM
    SB = 4 if S % 4 == 0 else 1
    RB = SB * R
    half = L // 2
    group = cfg["group"]
    part = W // group
    quarters = group // 2
    crowds = S // group
    z = lax.axis_index("head")
    d = lax.axis_index("dp")

    loads = []
    for index, ref in enumerate((frozen_in, train_in, frozen_out, train_out)):
        loads.append(pltpu.make_async_copy(ref.at[0], s.experts.at[index], s.load_sem.at[index]))
        loads[-1].start()
    barrier = pltpu.get_barrier_semaphore()
    for step in range(1, n):
        pl.semaphore_signal(barrier, 1, device_id={"head": lax.rem(z + step, n)}, device_id_type=MESH)

    def greet(step, carry):
        pl.semaphore_signal(barrier, 1, device_id={"dp": lax.rem(d + step, S)}, device_id_type=MESH)
        return carry

    lax.fori_loop(1, S, greet, 0)

    normal_one, inverse_one = normalize(block_in[...])
    s.normal_one[...] = normal_one
    s.inverse_one[...] = jnp.broadcast_to(inverse_one, s.inverse_one.shape)
    s.normed[z] = (normal_one * first_gain[...].reshape(1, D) + first_bias[...].reshape(1, D)).astype(BF)
    for f in range(NF):
        s.cots[f, z] = cotangent[:, f * FW : (f + 1) * FW].astype(BF)
    s.routes[z] = routes[...]
    part_id = lax.rem(d, group)
    for q in range(group):
        s.outw[z, q] = out_weight[q * part : (q + 1) * part, :]
    pl.semaphore_wait(barrier, n - 1 + S - 1)

    def over_z(source, target, send, recv):
        return Exchange("head", z, n, source, target, send, recv)

    routes_x = over_z(lambda p: s.routes.at[z], lambda p: s.routes.at[p], s.routes_s, s.routes_r)
    routes_x.start()
    T2 = T // 2
    normed_lines = [
        Line(lambda b, h=h: s.normed.at[b, pl.ds(h * T2, T2), :], s.normed_s.at[h], s.normed_r.at[h], z, n)
        for h in range(2)
    ]
    cot_lines = [Line(lambda b, f=f: s.cots.at[f, b], s.cot_s.at[f], s.cot_r.at[f], z, n) for f in range(NF)]
    outw_x = over_z(
        lambda p: s.outw.at[z, part_id], lambda p: s.outw.at[p, part_id], s.outw_s, s.outw_r
    )
    outw_x.start()
    soon, later = cot_lines[: NF - 1], cot_lines[NF - 1]
    for line in soon + normed_lines:
        line.pass_on(z)

    def project(block):
        rows = pl.ds(pl.multiple_of(block * T, T), T)
        normed = s.normed[block]
        for index in range(3):
            value = mm_nt(normed, qkv_weight[index]).astype(BF)
            if index == 0:
                value = value * jnp.asarray(HEAD_DIM**-0.5, BF)
            s.qkv[index, rows, :] = value

    routes_x.arrive()

    expert_col = lax.broadcasted_iota(jnp.int32, (E, T), 0)
    earlier = (
        lax.broadcasted_iota(jnp.int32, (T, T), 0) < lax.broadcasted_iota(jnp.int32, (T, T), 1)
    ).astype(F32).astype(BF)
    row_ids = lax.broadcasted_iota(jnp.int32, (M, T), 0)
    for j in range(n):
        first, second = s.routes[j, 0:1, :], s.routes[j, 1:2, :]
        hot0, hot1 = expert_col == first, expert_col == second
        hot = jnp.where(hot0 | hot1, 1.0, 0.0)
        count = mm(hot.astype(BF), earlier)
        for k, (names, hit) in enumerate(((first, hot0), (second, hot1))):
            slot = jnp.sum(jnp.where(hit, count, 0.0), axis=0, keepdims=True).astype(jnp.int32)
            late = names >= S
            owner = jnp.where(late, names - S, names)
            row = (owner * 2 + jnp.where(late, 1, 0)) * R + j * cap + slot
            s.target[j, k : k + 1, :] = jnp.where(slot < cap, row, -1)
        s.place[:, j * T : (j + 1) * T] = jnp.where(
            (row_ids == s.target[j, 0:1, :]) | (row_ids == s.target[j, 1:2, :]), 1.0, 0.0
        ).astype(BF)

    base = d - part_id
    plane = []
    outw_x.arrive()
    for step in range(1, n):
        other = lax.rem(z + step, n)
        plane.append(
            Exchange(
                "dp",
                part_id,
                group,
                lambda p, other=other: s.outw.at[other, part_id],
                lambda p, other=other: s.outw.at[other, p],
                s.outw_ps.at[step],
                s.outw_pr.at[step],
                device=lambda p: base + p,
            )
        )
        plane[-1].start()

    def dispatch(rows_ref, out_ref, in_ref, send, recv, f):
        tokens = rows_ref[f].reshape(n * T, FW)
        for half_id in range(2):
            span = S // 2
            rows = slice(half_id * span * 2 * R, (half_id + 1) * span * 2 * R)
            value = mm(s.place[rows, :], tokens).astype(BF)
            out_ref[f, half_id * span : (half_id + 1) * span] = value.reshape(span, 2, R, FW)
        exchange = Exchange(
            "dp", d, S, lambda p: out_ref.at[f, p], lambda p: in_ref.at[f, :, p], send.at[f], recv.at[f]
        )
        exchange.start()
        in_ref[f, :, d] = out_ref[f, d]
        return exchange

    cot_x = []
    for step in range(1, n):
        block = nearest(z, step, n)
        for line in soon:
            line.arrive(block)
            line.pass_on(block)
        if step == 1:
            later.pass_on(z)
            project(z)
        if step == n - 1:
            for f in range(NF - 1):
                cot_x.append(dispatch(s.cots, s.cot_out, s.cot_in, s.cotx_s, s.cotx_r, f))
        for line in normed_lines:
            line.arrive(block)
            line.pass_on(block)
        project(block)

    def lanes_of(rows):
        return lax.broadcasted_iota(jnp.int32, (rows, W), 1) // HEAD_DIM

    two = seq[0:1, L - 1 : L] > 0
    lane_t = lanes_of(T)
    mixed_x = over_z(lambda p: s.mixed.at[p], lambda p: s.mixed_in.at[p], s.mixed_s, s.mixed_r)

    inner_place = (z > 0) & (z < n - 1)

    def cot_service(step):
        @pl.when(inner_place)
        def _():
            block = nearest(z, step, n)
            later.arrive(block)
            later.pass_on(block)

    for qi in range(n):
        keys = (qi + 1) * T
        query_pos = lax.broadcasted_iota(jnp.int32, (T, keys), 0) + qi * T
        key_pos = lax.broadcasted_iota(jnp.int32, (T, keys), 1)
        allowed = query_pos >= key_pos
        if (qi * T) // half > 0:
            allowed = allowed & ((key_pos >= half) | jnp.logical_not(two))
        queries = s.qkv[0, qi * T : (qi + 1) * T, :].astype(F32)
        out = jnp.zeros((T, W), F32)
        for h in range(heads):
            masked_q = jnp.where(lane_t == h, queries, 0.0).astype(BF)
            scores = jnp.where(allowed, mm_nt(masked_q, s.qkv[1, :keys, :]), NEG)
            exp_vals = jnp.exp(scores - jnp.max(scores, axis=1, keepdims=True))
            weights = (exp_vals / jnp.sum(exp_vals, axis=1, keepdims=True)).astype(BF)
            s.probs[h, qi * T : (qi + 1) * T, :keys] = weights
            out = jnp.where(lane_t == h, mm(weights, s.qkv[2, :keys, :]), out)
        s.mixed[qi] = out.astype(BF)

        @pl.when(z != qi)
        def _():
            mixed_x.start_one(qi)

        if qi == 0 and n > 2:
            cot_service(1)
        if qi == 1 and n > 2:
            cot_service(2)

    for step in range(3, n):
        cot_service(step)

    @pl.when(jnp.logical_not(inner_place))
    def _():
        for step in range(1, n):
            block = nearest(z, step, n)
            later.arrive(block)
            later.pass_on(block)

    cot_x.append(dispatch(s.cots, s.cot_out, s.cot_in, s.cotx_s, s.cotx_r, NF - 1))

    for exchange in plane:
        exchange.arrive()
    mixed_x.arrive()
    s.mixed_in[z] = s.mixed[z]
    branch = jnp.zeros((T, D), F32)
    for j in range(n):
        branch = branch + mm(s.mixed_in[j], s.outw[j].reshape(W, D))
    residual = block_in[...] + branch
    s.residual[...] = residual
    normal_two, inverse_two = normalize(residual)
    s.normal_two[...] = normal_two
    s.inverse_two[...] = jnp.broadcast_to(inverse_two, s.inverse_two.shape)
    second_b = (normal_two * second_gain[...].reshape(1, D) + second_bias[...].reshape(1, D)).astype(BF)
    for f in range(NF):
        s.second[f, z] = second_b[:, f * FW : (f + 1) * FW]
    second_lines = [
        Line(lambda b, f=f: s.second.at[f, b], s.second_s.at[f], s.second_r.at[f], z, n) for f in range(NF)
    ]
    for line in second_lines:
        line.pass_on(z)
    row_x = []
    for f in range(NF):
        for step in range(1, n):
            block = nearest(z, step, n)
            second_lines[f].arrive(block)
            second_lines[f].pass_on(block)
        row_x.append(dispatch(s.second, s.row_out, s.row_in, s.rowx_s, s.rowx_r, f))

    for j in range(n):
        logits = jnp.zeros((E, T), F32)
        for f in range(NF):
            logits = logits + mm_nt(router[:, f * FW : (f + 1) * FW], s.second[f, j])
        hot0, hot1 = expert_col == s.routes[j, 0:1, :], expert_col == s.routes[j, 1:2, :]
        pick0 = jnp.sum(jnp.where(hot0, logits, 0.0), axis=0, keepdims=True)
        pick1 = jnp.sum(jnp.where(hot1, logits, 0.0), axis=0, keepdims=True)
        top = jnp.maximum(pick0, pick1)
        exp0, exp1 = jnp.exp(pick0 - top), jnp.exp(pick1 - top)
        s.gates[j, 0:1, :] = exp0 / (exp0 + exp1)
        s.gates[j, 1:2, :] = exp1 / (exp0 + exp1)
        s.gates[j, 2:4, :] = s.target[j, 0:2, :].astype(F32)
        s.gates[j, 4:8, :] = jnp.zeros((4, T), F32)
        columns = jnp.transpose(s.gates[j])
        lane_ids = lax.broadcasted_iota(jnp.int32, (T, M), 1).astype(F32)
        s.combine[j * T : (j + 1) * T, :] = jnp.where(
            lane_ids == columns[:, 2:3],
            columns[:, 0:1],
            jnp.where(lane_ids == columns[:, 3:4], columns[:, 1:2], 0.0),
        ).astype(BF)
    slot_ids = lax.broadcasted_iota(jnp.int32, (R, T), 0)
    lane_128 = lax.broadcasted_iota(jnp.int32, (128, 128), 1)
    table = jnp.zeros((128, 128), F32)
    for owner in range(S):
        total = jnp.zeros((R, T), F32)
        ids = slot_ids + (owner * 2 + 1) * R
        for j in range(n):
            total = total + jnp.where(
                ids == s.target[j, 0:1, :],
                s.gates[j, 0:1, :],
                jnp.where(ids == s.target[j, 1:2, :], s.gates[j, 1:2, :], 0.0),
            )
        column = jnp.sum(total, axis=1, keepdims=True)
        if R < 128:
            column = jnp.concatenate([column, jnp.zeros((128 - R, 1), F32)], axis=0)
        table = jnp.where(lane_128 == owner, column, table)
    table = jnp.transpose(table)
    for owner in range(S):
        s.gate_out[owner] = jnp.broadcast_to(table[owner : owner + 1, :], (8, 128))
    gate_x = Exchange(
        "dp", d, S, lambda p: s.gate_out.at[p], lambda p: s.gate_in.at[p], s.gate_s, s.gate_r
    )
    gate_x.start()
    s.gate_in[d] = s.gate_out[d]

    for load in loads:
        load.wait()

    def row_blocks(act):
        def step(i, carry):
            act(i * SB, pl.multiple_of(i * RB, RB))
            return carry

        lax.fori_loop(0, S // SB, step, 0)

    def add_up(total_ref, rows_ref, f, transposed):
        for g in range(2):

            def act(block, row):
                value = rows_ref[f, g, pl.ds(block, SB)].reshape(RB, FW)
                if transposed:
                    piece = mm_nt(value, s.experts[2 + g, :, f * FW : (f + 1) * FW])
                else:
                    piece = mm(value, s.experts[g, f * FW : (f + 1) * FW, :])
                rows = pl.ds(g * S * R + row, RB)
                total_ref[rows, :] = piece if f == 0 else total_ref[rows, :] + piece

            row_blocks(act)

    for f in range(NF):
        cot_x[f].arrive()
        add_up(s.grad_active, s.cot_in, f, True)
    for f in range(NF):
        row_x[f].arrive()
        add_up(s.hidden, s.row_in, f, False)
    EB = 16 if R % 16 == 0 else 8

    for g in range(2):

        def activate(i, carry):
            rows = pl.ds(pl.multiple_of(i * EB, EB), EB)
            flat = pl.ds(pl.multiple_of(g * S * R + i * EB, EB), EB)
            value = s.hidden[flat, :]
            normal_cdf = 0.5 * (1.0 + lax.erf(value * 0.7071067811865476))
            s.active[g, rows, :] = (value * normal_cdf).astype(BF)
            s.hidden[flat, :] = normal_cdf + value * jnp.exp(-0.5 * value * value) * 0.3989422804014327
            return carry

        lax.fori_loop(0, S * R // EB, activate, 0)

    tables = []
    for g in range(2):
        table = jnp.zeros((128, 128), F32)
        for source in range(S):
            sums = []
            for i in range(R // EB):
                rows = slice(source * R + i * EB, source * R + (i + 1) * EB)
                flat = slice(g * S * R + rows.start, g * S * R + rows.stop)
                grad = s.grad_active[flat, :]
                s.grad_hidden[g, rows, :] = (grad * s.hidden[flat, :]).astype(BF)
                sums.append(
                    jnp.sum(grad * s.active[g, rows, :].astype(F32), axis=1, keepdims=True)
                )
            if R < 128:
                sums.append(jnp.zeros((128 - R, 1), F32))
            table = jnp.where(lane_128 == source, jnp.concatenate(sums, axis=0), table)
        tables.append(jnp.transpose(table))
    row_8 = lax.broadcasted_iota(jnp.int32, (8, 128), 0)
    for source in range(S):
        s.dot_out[source] = jnp.where(
            row_8 == 0, tables[0][source : source + 1, :], tables[1][source : source + 1, :]
        )
    dot_x = Exchange("dp", d, S, lambda p: s.dot_out.at[p], lambda p: s.dot_in.at[p], s.dot_s, s.dot_r)
    dot_x.start()
    s.dot_in[d] = s.dot_out[d]

    def give_back(f, rows_ref, first_weight, out_ref, in_ref, send, recv, transposed, go=True):
        for g in range(2):

            def act(block, row):
                value = rows_ref[g, pl.ds(row, RB), :]
                if transposed:
                    piece = mm_nt(value, s.experts[first_weight + g, f * FW : (f + 1) * FW, :])
                else:
                    piece = mm(value, s.experts[first_weight + g, :, f * FW : (f + 1) * FW])
                out_ref[f, pl.ds(block, SB), g] = piece.astype(BF).reshape(SB, R, FW)

            row_blocks(act)
        exchange = Exchange(
            "dp", d, S, lambda p: out_ref.at[f, p], lambda p: in_ref.at[f, p], send.at[f], recv.at[f]
        )
        if go:
            exchange.start()
        in_ref[f, d] = out_ref[f, d]
        return exchange

    if cfg["tight"]:
        for exchange in cot_x + row_x:
            exchange.finish()
        down_out, fore_out = s.cot_out, s.row_out
    else:
        down_out, fore_out = s.down_out, s.fore_out
    down_x = [
        give_back(f, s.grad_hidden, 0, down_out, s.down_in, s.down_s, s.down_r, True) for f in range(NF)
    ]
    fore_x = [
        give_back(f, s.active, 2, fore_out, s.fore_in, s.fore_s, s.fore_r, False, f < NF - 1)
        for f in range(NF)
    ]

    gate_x.arrive()
    columns = jnp.transpose(s.gate_in[:, 0, :])
    for source in range(S):
        column = columns[:R, source : source + 1]
        rows = slice(source * R, (source + 1) * R)
        s.active[1, rows, :] = (s.active[1, rows, :].astype(F32) * column).astype(BF)
        s.grad_hidden[1, rows, :] = (s.grad_hidden[1, rows, :].astype(F32) * column).astype(BF)
    for f in range(NF):
        s.hidden[f * FW : (f + 1) * FW, :] = mm_tn(
            s.row_in[f, 1].reshape(S * R, FW), s.grad_hidden[1]
        )
        s.grad_active[0:HID, f * FW : (f + 1) * FW] = mm_tn(
            s.active[1], s.cot_in[f, 1].reshape(S * R, FW)
        )
    stores = [
        pltpu.make_async_copy(s.hidden.at[0:D, :], grad_in_out.at[0], s.store_sem.at[0]),
        pltpu.make_async_copy(s.grad_active.at[0:HID, :], grad_out_out.at[0], s.store_sem.at[1]),
    ]
    for store in stores:
        store.start()

    def gather_rows(in_ref, f):
        return mm(s.combine[...], in_ref[f].reshape(M, FW)).astype(BF).reshape(n, T, FW)

    def token_sum(f, exchanges, in_ref, part_ref, sum_ref, send, recv):
        exchanges[f].arrive()
        part_ref[f] = gather_rows(in_ref, f)
        sums_x = over_z(
            lambda p: part_ref.at[f, p], lambda p: sum_ref.at[f, p], send.at[f], recv.at[f]
        )
        sums_x.start()
        sum_ref[f, z] = part_ref[f, z]
        return sums_x

    def add_sums(sums_x, sum_ref):
        parts = []
        for f in range(NF):
            sums_x[f].arrive()
            total = sum_ref[f, 0].astype(F32)
            for j in range(1, n):
                total = total + sum_ref[f, j].astype(F32)
            parts.append(total)
        return jnp.concatenate(parts, axis=1)

    if cfg["tight"]:
        for line in cot_lines:
            line.finish()
        down_part = s.cots
    else:
        down_part = s.down_part
    down_sums = [
        token_sum(f, down_x, s.down_in, down_part, s.down_sum, s.dsum_s, s.dsum_r) for f in range(NF)
    ]

    dot_x.arrive()
    turned = [jnp.transpose(s.dot_in[:, g, :]) for g in range(2)]
    for j in range(n):
        total = jnp.zeros((R, T), F32)
        for owner in range(S):
            for g in range(2):
                ids = slot_ids + (owner * 2 + g) * R
                sign = jnp.where(
                    ids == s.target[j, 0:1, :], 1.0, jnp.where(ids == s.target[j, 1:2, :], -1.0, 0.0)
                )
                total = total + sign * turned[g][:R, owner : owner + 1]
        s.delta_out[j] = jnp.broadcast_to(jnp.sum(total, axis=0, keepdims=True), (8, T))
    delta_x = over_z(
        lambda p: s.delta_out.at[p], lambda p: s.delta_in.at[p], s.delta_s, s.delta_r
    )
    delta_x.start()
    s.delta_in[z] = s.delta_out[z]
    delta_x.arrive()
    delta = s.delta_in[0, 0:1, :]
    for j in range(1, n):
        delta = delta + s.delta_in[j, 0:1, :]

    grad_chosen = s.gates[z, 0:1, :] * s.gates[z, 1:2, :] * delta
    hot0, hot1 = expert_col == s.routes[z, 0:1, :], expert_col == s.routes[z, 1:2, :]
    grad_logits = jnp.where(hot0, grad_chosen, jnp.where(hot1, -grad_chosen, 0.0))
    router_part = contract(grad_logits, router[...].astype(F32), 0, 0, lax.Precision.HIGHEST)
    router_grads = [
        contract(grad_logits, s.second[f, z].astype(F32), 1, 0, lax.Precision.HIGHEST)
        for f in range(NF)
    ]
    grad_second = add_sums(down_sums, s.down_sum) + router_part
    normal_two = s.normal_two[...]
    pair = jnp.concatenate(
        [
            jnp.sum(grad_second * normal_two, axis=0, keepdims=True),
            jnp.sum(grad_second, axis=0, keepdims=True),
            jnp.zeros((6, D), F32),
        ],
        axis=0,
    )
    sums_now = jnp.concatenate([jnp.concatenate(router_grads, axis=1), pair], axis=0)
    H = D // 2
    for side in range(2):
        s.early[side] = sums_now[:, side * H : (side + 1) * H]
    grad_residual = cotangent[...] + norm_back(
        grad_second, normal_two, s.inverse_two[:, 0:1], second_gain[...].reshape(1, D)
    )
    s.grad_residual[...] = grad_residual
    s.branch[...] = grad_residual.astype(BF)

    def mixed_back(heads_of):
        return mm_nt(s.branch[...], s.outw[heads_of].reshape(W, D)).astype(BF)

    mixed_x.finish()
    back_x = over_z(lambda p: s.mixed.at[p], lambda p: s.grad_mixed.at[p], s.back_s, s.back_r)
    for step in range(1, n):
        peer = nearest(z, n - step, n)
        s.mixed[peer] = mixed_back(peer)
        back_x.start_one(peer)
    s.grad_mixed[z] = mixed_back(z)
    core = lax.rem(d, 2)
    quarter = part_id // 2
    mate = d + 1 - 2 * core
    for j in range(n):
        value = mm_tn(s.mixed_in[j], s.branch[...])
        for piece in range(group):
            s.gsum[piece // quarters, piece % quarters, j] = value[piece * part : (piece + 1) * part, :].astype(BF)

    def to_mate(source, target, index):
        return pltpu.make_async_remote_copy(
            src_ref=source,
            dst_ref=target,
            send_sem=s.swap_s.at[index],
            recv_sem=s.swap_r.at[index],
            device_id={"dp": mate},
            device_id_type=MESH,
        )

    def over_chips(source, target, send, recv):
        return Exchange(
            "dp", quarter, quarters, source, target, send, recv, device=lambda p: base + 2 * p + core
        )

    early_swap = to_mate(s.early.at[1 - core], s.early_mate, 3)
    early_swap.start()
    out_swap = to_mate(s.gsum.at[1 - core], s.gswap, 0)
    out_swap.start()

    if cfg["tight"]:
        for exchange in down_sums:
            exchange.finish()
        fore_part = s.cots
    else:
        fore_part = s.fore_part
    fore_sums = []

    def fore_step(f):
        fore_sums.append(
            token_sum(f, fore_x, s.fore_in, fore_part, s.fore_sum, s.fsum_s, s.fsum_r)
        )

    fore_step(0)
    early_swap.wait_recv()
    s.early_mate[...] = s.early[core] + s.early_mate[...]
    early_x = over_chips(lambda p: s.early_mate, lambda p: s.early_dp.at[p], s.early_s, s.early_r)
    early_x.start()
    s.early_dp[quarter] = s.early_mate[...]
    out_swap.wait_recv()
    s.gswap[...] = (s.gsum[core].astype(F32) + s.gswap[...].astype(F32)).astype(BF)
    out_x = over_chips(lambda p: s.gswap.at[p], lambda p: s.gparts.at[p], s.outp_s, s.outp_r)
    out_x.start()
    s.gparts[quarter] = s.gswap[quarter]
    fore_x[NF - 1].start()
    back_x.arrive()

    for qi in range(n):
        keys = (qi + 1) * T
        rows = slice(qi * T, (qi + 1) * T)
        grads = s.grad_mixed[qi]
        grads_f = grads.astype(F32)
        lane_k = lanes_of(keys)
        grad_q = jnp.zeros((T, W), F32)
        grad_k = jnp.zeros((keys, W), F32)
        grad_v = jnp.zeros((keys, W), F32)
        for h in range(heads):
            masked = jnp.where(lane_t == h, grads_f, 0.0).astype(BF)
            grad_w = mm_nt(masked, s.qkv[2, :keys, :])
            weights = s.probs[h, rows, :keys]
            probs = weights.astype(F32)
            inner = jnp.sum(probs * grad_w, axis=1, keepdims=True)
            grad_s = (probs * (grad_w - inner)).astype(BF)
            grad_q = jnp.where(lane_t == h, mm(grad_s, s.qkv[1, :keys, :]), grad_q)
            grad_k = jnp.where(lane_k == h, mm_tn(grad_s, s.qkv[0, rows, :]), grad_k)
            grad_v = jnp.where(lane_k == h, mm_tn(weights, grads), grad_v)
        s.grad_proj[0, rows, :] = (grad_q * HEAD_DIM**-0.5).astype(BF)
        if qi == 0:
            s.grad_kv[...] = jnp.zeros(s.grad_kv.shape, F32)
        s.grad_kv[0, :keys, :] = s.grad_kv[0, :keys, :] + grad_k
        s.grad_kv[1, :keys, :] = s.grad_kv[1, :keys, :] + grad_v
    for index in range(2):
        s.grad_proj[1 + index] = s.grad_kv[index].astype(BF)

    def first_part(block):
        rows = pl.ds(pl.multiple_of(block * T, T), T)
        total = mm(s.grad_proj[0, rows, :], qkv_weight[0])
        for index in range(1, 3):
            total = total + mm(s.grad_proj[index, rows, :], qkv_weight[index])
        s.first_out[block] = total.astype(BF)

    first_x = over_z(lambda p: s.first_out.at[p], lambda p: s.first_in.at[p], s.first_s, s.first_r)
    for step in range(1, n):
        peer = nearest(z, n - step, n)
        first_part(peer)
        first_x.start_one(peer)
    first_part(z)
    s.first_in[z] = s.first_out[z]

    def add_chips(exchange, parts_ref):
        exchange.arrive()
        total = parts_ref[0].astype(F32)
        for peer in range(1, quarters):
            total = total + parts_ref[peer].astype(F32)
        return total

    crowd = d // group
    far_x = []

    def add_crowds(total, ref, send, recv):
        if crowds == 1:
            return total
        ref[crowd] = total.astype(ref.dtype)
        exchange = Exchange(
            "dp",
            crowd,
            crowds,
            lambda p: ref.at[crowd],
            lambda p: ref.at[p],
            send,
            recv,
            device=lambda p: p * group + part_id,
        )
        exchange.start()
        exchange.arrive()
        far_x.append(exchange)
        total = ref[0].astype(F32)
        for peer in range(1, crowds):
            total = total + ref[peer].astype(F32)
        return total

    out_swap.wait_send()
    normed_all = s.normed[...].reshape(L, D)
    for index in range(3):
        value = mm_tn(s.grad_proj[index], normed_all)
        for piece in range(group):
            s.gsum[piece // quarters, piece % quarters, index] = value[
                piece * part : (piece + 1) * part, :
            ].astype(BF)
    swap = to_mate(s.gsum.at[1 - core, :, 0:3], s.wswap, 1)
    swap.start()
    total = add_chips(out_x, s.gparts)
    if crowds > 1:
        total = add_crowds(total, s.out_far, s.outf_s, s.outf_r)
    s.out_piece[...] = total.astype(BF)
    out_zx = over_z(lambda p: s.out_piece.at[p], lambda p: s.out_pieces.at[p], s.outz_s, s.outz_r)
    out_zx.start()
    s.out_pieces[z] = s.out_piece[z]
    swap.wait_recv()
    s.wswap[...] = (s.gsum[core, :, 0:3].astype(F32) + s.wswap[...].astype(F32)).astype(BF)
    pair_x = over_chips(lambda p: s.wswap.at[p], lambda p: s.wparts.at[p], s.pair_s, s.pair_r)
    pair_x.start()
    s.wparts[quarter] = s.wswap[quarter]
    total = add_chips(early_x, s.early_dp)
    if crowds > 1:
        total = add_crowds(total, s.early_far, s.earlyf_s, s.earlyf_r)
    s.early_z[z] = total
    early_zx = over_z(lambda p: s.early_z.at[z], lambda p: s.early_z.at[p], s.earlyz_s, s.earlyz_r)
    early_zx.start()
    for f in range(1, NF):
        fore_step(f)

    first_x.arrive()
    grad_first = s.first_in[0].astype(F32)
    for j in range(1, n):
        grad_first = grad_first + s.first_in[j].astype(F32)
    normal_one = s.normal_one[...]
    s.late[...] = jnp.concatenate(
        [
            jnp.sum(grad_first * normal_one, axis=0, keepdims=True),
            jnp.sum(grad_first, axis=0, keepdims=True),
            jnp.zeros((6, D), F32),
        ],
        axis=0,
    )
    late_x = Exchange("dp", d, S, lambda p: s.late, lambda p: s.late_dp.at[p], s.late_s, s.late_r)
    late_x.start()
    s.late_dp[d] = s.late[...]
    input_grad[...] = s.grad_residual[...] + norm_back(
        grad_first, normal_one, s.inverse_one[:, 0:1], first_gain[...].reshape(1, D)
    )
    total = add_chips(pair_x, s.wparts)
    if crowds > 1:
        total = add_crowds(total, s.w_far, s.wf_s, s.wf_r)
    s.wfull[core, quarter, 0:3] = total.astype(BF)
    out_zx.arrive()
    total = s.out_pieces[0].astype(F32)
    for j in range(1, n):
        total = total + s.out_pieces[j].astype(F32)
    s.wfull[core, quarter, 3] = total.astype(BF)
    full_x = over_chips(
        lambda p: s.wfull.at[core, quarter], lambda p: s.wfull.at[core, p], s.full_s, s.full_r
    )
    full_x.start()
    early_zx.arrive()
    total = s.early_z[0]
    for j in range(1, n):
        total = total + s.early_z[j]
    s.early_all[core] = total
    early_back = to_mate(s.early_all.at[core], s.early_all.at[core], 4)
    early_back.start()
    late_x.arrive()
    total = s.late_dp[0]
    for peer in range(1, S):
        total = total + s.late_dp[peer]
    s.late_z[z] = total
    late_zx = over_z(lambda p: s.late_z.at[z], lambda p: s.late_z.at[p], s.latez_s, s.latez_r)
    late_zx.start()

    block_out[...] = s.residual[...] + add_sums(fore_sums, s.fore_sum)
    full_x.arrive()
    back = to_mate(s.wfull.at[core], s.wfull.at[core], 2)
    back.start()
    to_mate(s.early_all.at[core], s.early_all.at[1 - core], 4).wait_recv()
    for side in range(2):
        vec_out[0 : E + 8, side * H : (side + 1) * H] = s.early_all[side]
    late_zx.arrive()
    total = s.late_z[0]
    for j in range(1, n):
        total = total + s.late_z[j]
    vec_out[E + 8 : E + 16, :] = total
    to_mate(s.wfull.at[core], s.wfull.at[1 - core], 2).wait_recv()
    sums_store = pltpu.make_async_copy(s.wfull, weights_out, s.store_sem.at[2])
    sums_store.start()
    stores.append(sums_store)

    for store in stores:
        store.wait()
    for copy in (swap, back, early_swap, early_back):
        copy.wait_send()
    for lines in (normed_lines, second_lines) if cfg["tight"] else (normed_lines, cot_lines, second_lines):
        for line in lines:
            line.finish()
    done = [routes_x, outw_x, gate_x, dot_x, delta_x, early_x, pair_x, early_zx, full_x, first_x, late_x]
    if not cfg["tight"]:
        done += cot_x + row_x + down_sums
    done += far_x + [late_zx, back_x, out_x, out_zx] + plane + down_x + fore_x + fore_sums
    for exchange in done:
        exchange.finish()


def hand_over(E, *refs):
    given, vecs = refs[:5], refs[5]
    large, small = refs[6:12], refs[12:17]
    held, narrow, wide, load_sem, store_sem = refs[17:21], refs[21], refs[22], refs[23], refs[24]
    loads = [
        pltpu.make_async_copy(given[index], (list(held) + [narrow])[index], load_sem.at[index])
        for index in range(5)
    ]
    for load in (loads[4], *loads[:4]):
        load.start()
    sources = [*held, wide.at[0:3], wide.at[3]]
    stores = [
        pltpu.make_async_copy(sources[index], large[index], store_sem.at[index]) for index in range(6)
    ]
    small[0][...] = vecs[0:E, :]
    D = vecs.shape[1]
    for index, row in enumerate((E + 8, E + 9, E, E + 1)):
        small[1 + index][...] = vecs[row : row + 1, :].reshape(D)
    loads[4].wait()
    part = narrow.shape[2]
    for piece in range(narrow.shape[0]):
        wide[:, piece * part : (piece + 1) * part, :] = narrow[piece].astype(F32)
    stores[4].start()
    stores[5].start()
    for index in range(4):
        loads[index].wait()
        stores[index].start()
    for store in stores:
        store.wait()


class Names:
    pass


def shards(
    block_in,
    first_gain,
    first_bias,
    qkv_weight,
    out_weight,
    second_gain,
    second_bias,
    router_weight,
    frozen_in,
    frozen_out,
    train_in,
    train_out,
    routes,
    seq_ids,
    cotangent,
):
    T, D = block_in.shape
    L = seq_ids.shape[0]
    E = router_weight.shape[1]
    S, n = lax.axis_size("dp"), lax.axis_size("head")
    W = qkv_weight.shape[2]
    HID = frozen_in.shape[2]
    cap = max(2, 5 * T // (2 * E))
    R = -(-(n * cap) // 8) * 8
    M = E * R
    NF = D // FW
    group = 8
    quarters = group // 2
    part = W // group
    crowds = S // group
    tight = S > group
    cfg = dict(tight=tight, n=n, S=S, T=T, D=D, L=L, E=E, R=R, W=W, HID=HID, cap=cap, group=group)
    DMA = pltpu.SemaphoreType.DMA
    scratch = dict(
        experts=VMEM((4, D, HID), BF),
        normal_one=VMEM((T, D), F32),
        inverse_one=VMEM((T, 128), F32),
        normed=VMEM((n, T, D), BF),
        cots=VMEM((NF, n, T, FW), BF),
        routes=VMEM((n, 2, T), jnp.int32),
        outw=VMEM((n, group, W // group, D), BF),
        qkv=VMEM((3, L, W), BF),
        target=VMEM((n, 8, T), jnp.int32),
        gates=VMEM((n, 8, T), F32),
        place=VMEM((M, L), BF),
        combine=VMEM((L, M), BF),
        probs=VMEM((W // HEAD_DIM, L, L), BF),
        mixed=VMEM((n, T, W), BF),
        mixed_in=VMEM((n, T, W), BF),
        residual=VMEM((T, D), F32),
        normal_two=VMEM((T, D), F32),
        inverse_two=VMEM((T, 128), F32),
        second=VMEM((NF, n, T, FW), BF),
        cot_out=VMEM((NF, S, 2, R, FW), BF),
        cot_in=VMEM((NF, 2, S, R, FW), BF),
        row_out=VMEM((NF, S, 2, R, FW), BF),
        row_in=VMEM((NF, 2, S, R, FW), BF),
        gate_out=VMEM((S, 8, 128), F32),
        gate_in=VMEM((S, 8, 128), F32),
        hidden=VMEM((2 * S * R, HID), F32),
        grad_active=VMEM((2 * S * R, HID), F32),
        active=VMEM((2, S * R, HID), BF),
        grad_hidden=VMEM((2, S * R, HID), BF),
        dot_out=VMEM((S, 8, 128), F32),
        dot_in=VMEM((S, 8, 128), F32),
        down_out=VMEM((NF, S, 2, R, FW), BF),
        down_in=VMEM((NF, S, 2, R, FW), BF),
        fore_out=VMEM((NF, S, 2, R, FW), BF),
        fore_in=VMEM((NF, S, 2, R, FW), BF),
        down_part=VMEM((NF, n, T, FW), BF),
        down_sum=VMEM((NF, n, T, FW), BF),
        fore_part=VMEM((NF, n, T, FW), BF),
        fore_sum=VMEM((NF, n, T, FW), BF),
        delta_out=VMEM((n, 8, T), F32),
        delta_in=VMEM((n, 8, T), F32),
        early=VMEM((2, E + 8, D // 2), F32),
        early_mate=VMEM((E + 8, D // 2), F32),
        early_dp=VMEM((quarters, E + 8, D // 2), F32),
        early_z=VMEM((n, E + 8, D // 2), F32),
        early_all=VMEM((2, E + 8, D // 2), F32),
        late=VMEM((8, D), F32),
        late_dp=VMEM((S, 8, D), F32),
        late_z=VMEM((n, 8, D), F32),
        grad_residual=VMEM((T, D), F32),
        branch=VMEM((T, D), BF),
        grad_mixed=VMEM((n, T, W), BF),
        grad_proj=VMEM((3, L, W), BF),
        grad_kv=VMEM((2, L, W), F32),
        first_out=VMEM((n, T, D), BF),
        first_in=VMEM((n, T, D), BF),
        gsum=VMEM((2, quarters, n, part, D), BF),
        gswap=VMEM((quarters, n, part, D), BF),
        gparts=VMEM((quarters, n, part, D), BF),
        out_piece=VMEM((n, part, D), BF),
        out_pieces=VMEM((n, part, D), BF),
        wswap=VMEM((quarters, 3, part, D), BF),
        wparts=VMEM((quarters, 3, part, D), BF),
        wfull=VMEM((2, quarters, 4, part, D), BF),
        load_sem=DMA((4,)),
        store_sem=DMA((3,)),
        swap_s=DMA((5,)),
        swap_r=DMA((5,)),
        routes_s=DMA((n,)),
        routes_r=DMA((n,)),
        normed_s=DMA((2, 2, n)),
        normed_r=DMA((2, n)),
        cot_s=DMA((NF, 2, n)),
        cot_r=DMA((NF, n)),
        outw_s=DMA((n,)),
        outw_r=DMA((n,)),
        outw_ps=DMA((n, group)),
        outw_pr=DMA((n, group)),
        mixed_s=DMA((n,)),
        mixed_r=DMA((n,)),
        cotx_s=DMA((NF, S)),
        cotx_r=DMA((NF, S)),
        rowx_s=DMA((NF, S)),
        rowx_r=DMA((NF, S)),
        second_s=DMA((NF, 2, n)),
        second_r=DMA((NF, n)),
        gate_s=DMA((S,)),
        gate_r=DMA((S,)),
        dot_s=DMA((S,)),
        dot_r=DMA((S,)),
        down_s=DMA((NF, S)),
        down_r=DMA((NF, S)),
        fore_s=DMA((NF, S)),
        fore_r=DMA((NF, S)),
        dsum_s=DMA((NF, n)),
        dsum_r=DMA((NF, n)),
        fsum_s=DMA((NF, n)),
        fsum_r=DMA((NF, n)),
        delta_s=DMA((n,)),
        delta_r=DMA((n,)),
        back_s=DMA((n,)),
        back_r=DMA((n,)),
        outp_s=DMA((quarters,)),
        outp_r=DMA((quarters,)),
        outz_s=DMA((n,)),
        outz_r=DMA((n,)),
        early_s=DMA((quarters,)),
        early_r=DMA((quarters,)),
        earlyz_s=DMA((n,)),
        earlyz_r=DMA((n,)),
        first_s=DMA((n,)),
        first_r=DMA((n,)),
        pair_s=DMA((quarters,)),
        pair_r=DMA((quarters,)),
        full_s=DMA((quarters,)),
        full_r=DMA((quarters,)),
        late_s=DMA((S,)),
        late_r=DMA((S,)),
        latez_s=DMA((n,)),
        latez_r=DMA((n,)),
    )
    if crowds > 1:
        scratch.update(
            early_far=VMEM((crowds, E + 8, D // 2), F32),
            earlyf_s=DMA((crowds,)),
            earlyf_r=DMA((crowds,)),
            out_far=VMEM((crowds, n, part, D), BF),
            outf_s=DMA((crowds,)),
            outf_r=DMA((crowds,)),
            w_far=VMEM((crowds, 3, part, D), BF),
            wf_s=DMA((crowds,)),
            wf_r=DMA((crowds,)),
        )
    if tight:
        del scratch["down_out"], scratch["fore_out"], scratch["fore_part"], scratch["down_part"]
    names = list(scratch)

    def kernel(*refs):
        space = Names()
        for name, ref in zip(names, refs[21:]):
            setattr(space, name, ref)
        body(*refs[:21], space, cfg)

    whole = pl.BlockSpec(memory_space=VMEM)
    left = pl.BlockSpec(memory_space=pl.ANY)
    outs = pl.pallas_call(
        kernel,
        out_shape=(
            jax.ShapeDtypeStruct((T, D), F32),
            jax.ShapeDtypeStruct((T, D), F32),
            jax.ShapeDtypeStruct((E + 16, D), F32),
            jax.ShapeDtypeStruct((2, quarters, 4, part, D), BF),
            jax.ShapeDtypeStruct((1, D, HID), F32),
            jax.ShapeDtypeStruct((1, HID, D), F32),
        ),
        in_specs=[whole] * 8 + [left] * 4 + [whole] * 3,
        out_specs=(whole, whole, whole, left, left, left),
        scratch_shapes=list(scratch.values()),
        compiler_params=pltpu.CompilerParams(
            collective_id=0, has_side_effects=True, vmem_limit_bytes=67043328
        ),
    )(
        block_in,
        first_gain,
        first_bias,
        jnp.swapaxes(qkv_weight, 1, 2),
        out_weight,
        second_gain,
        second_bias,
        router_weight.T,
        frozen_in,
        frozen_out,
        train_in,
        train_out,
        routes.T,
        seq_ids.reshape(1, L),
        cotangent,
    )
    block_out, input_grad, vecs, sums, grad_train_in, grad_train_out = outs
    sums = sums.reshape(group, 4, part, D)
    big = [block_out, input_grad, grad_train_in, grad_train_out]
    vector = jax.ShapeDtypeStruct((D,), F32)
    done = pl.pallas_call(
        functools.partial(hand_over, E),
        out_shape=[jax.ShapeDtypeStruct(array.shape, F32) for array in big]
        + [
            jax.ShapeDtypeStruct((3, W, D), F32),
            jax.ShapeDtypeStruct((W, D), F32),
            jax.ShapeDtypeStruct((E, D), F32),
        ]
        + [vector] * 4,
        in_specs=[left] * 5 + [whole],
        out_specs=[left] * 6 + [whole] * 5,
        scratch_shapes=[VMEM(array.shape, F32) for array in big]
        + [VMEM((group, 4, part, D), BF), VMEM((4, W, D), F32), DMA((5,)), DMA((6,))],
        compiler_params=pltpu.CompilerParams(vmem_limit_bytes=67043328),
    )(*big, sums, vecs)
    block_out, input_grad, grad_train_in, grad_train_out, grad_qkv, grad_out, grad_router = done[:7]
    return (
        block_out,
        input_grad,
        done[7],
        done[8],
        jnp.swapaxes(grad_qkv, 1, 2),
        grad_out,
        done[9],
        done[10],
        grad_router.T,
        grad_train_in,
        grad_train_out,
    )


def solution(mesh):
    return jax.shard_map(
        shards,
        mesh=mesh,
        in_specs=(
            P(("dp", "head"), None),
            P(),
            P(),
            P(None, None, "head"),
            P("head", None),
            P(),
            P(),
            P(),
            P("dp", None, "head"),
            P("dp", "head", None),
            P("dp", None, "head"),
            P("dp", "head", None),
            P(("dp", "head"), None),
            P("dp"),
            P(("dp", "head"), None),
        ),
        out_specs=(
            P(("dp", "head"), None),
            P(("dp", "head"), None),
            P(),
            P(),
            P(None, None, "head"),
            P("head", None),
            P(),
            P(),
            P(),
            P("dp", None, "head"),
            P("dp", "head", None),
        ),
        check_vma=False,
    )
```

```python
import functools

import jax
import jax.numpy as jnp
from jax import lax
from jax.experimental import pallas as pl
from jax.experimental.pallas import tpu as pltpu
from jax.sharding import PartitionSpec as P

HEAD_DIM = 64
EPS = 1e-05
NEG = -1e30
FW = 256
F32 = jnp.float32
BF = jnp.bfloat16
MESH = pl.DeviceIdType.MESH
VMEM = pltpu.VMEM


def contract(left, right, left_dim, right_dim, precision=None):
    return lax.dot_general(
        left,
        right,
        (((left_dim,), (right_dim,)), ((), ())),
        precision=precision,
        preferred_element_type=F32,
    )


def mm(left, right):
    return contract(left, right, 1, 0)


def mm_nt(left, right):
    return contract(left, right, 1, 1)


def mm_tn(left, right):
    return contract(left, right, 0, 0)


def normalize(values):
    average = jnp.mean(values, axis=-1, keepdims=True)
    centred = values - average
    variance = jnp.mean(centred * centred, axis=-1, keepdims=True)
    inverse = lax.rsqrt(variance + EPS)
    return centred * inverse, inverse


def norm_back(grad_norm, normal, inverse, gain_vec):
    scaled = grad_norm * gain_vec
    first_mean = jnp.mean(scaled, axis=-1, keepdims=True)
    second_mean = jnp.mean(scaled * normal, axis=-1, keepdims=True)
    return inverse * (scaled - first_mean - normal * second_mean)


def nearest(place, step, count):
    low, high = place, count - 1 - place
    both = jnp.minimum(low, high)
    near = jnp.where(step % 2 == 1, place - (step + 1) // 2, place + step // 2)
    far = jnp.where(low > high, place - (step - both), place + (step - both))
    return jnp.where(step <= 2 * both, near, far)


class Line:
    def __init__(self, ref_of, send, recv, place, count):
        self.ref_of, self.send, self.recv = ref_of, send, recv
        self.place, self.count = place, count

    def copy(self, block, up):
        step = 1 if up else -1
        return pltpu.make_async_remote_copy(
            src_ref=self.ref_of(block),
            dst_ref=self.ref_of(block),
            send_sem=self.send.at[0 if up else 1, block],
            recv_sem=self.recv.at[block],
            device_id={"head": self.place + step},
            device_id_type=MESH,
        )

    def pass_on(self, block):
        @pl.when((block <= self.place) & (self.place < self.count - 1))
        def _():
            self.copy(block, True).start()

        @pl.when((block >= self.place) & (self.place > 0))
        def _():
            self.copy(block, False).start()

    def arrive(self, block):
        self.copy(block, True).wait_recv()

    def finish(self):
        for block in range(self.count):

            @pl.when((block <= self.place) & (self.place < self.count - 1))
            def _():
                self.copy(block, True).wait_send()

            @pl.when((block >= self.place) & (self.place > 0))
            def _():
                self.copy(block, False).wait_send()


class Exchange:
    def __init__(self, axis, place, count, source, target, send, recv, device=None):
        self.axis, self.place, self.count = axis, place, count
        self.source, self.target, self.send, self.recv = source, target, send, recv
        self.device = device or (lambda peer: peer)

    def copy(self, peer, lands):
        return pltpu.make_async_remote_copy(
            src_ref=self.source(peer),
            dst_ref=self.target(lands),
            send_sem=self.send.at[peer],
            recv_sem=self.recv.at[lands],
            device_id={self.axis: self.device(peer)},
            device_id_type=MESH,
        )

    def loop(self, act):
        def body(step, carry):
            act(lax.rem(self.place + step, self.count))
            return carry

        lax.fori_loop(1, self.count, body, 0)

    def start_one(self, peer):
        self.copy(peer, self.place).start()

    def start(self):
        self.loop(self.start_one)

    def arrive(self):
        self.loop(lambda peer: self.copy(peer, peer).wait_recv())

    def finish(self):
        self.loop(lambda peer: self.copy(peer, self.place).wait_send())


class Sums(Exchange):
    def __init__(self, place, count, source, target, relay, send, recv, relay_sem):
        super().__init__("head", place, count, source, target, send, recv)
        self.relay, self.relay_sem, self.joined = relay, relay_sem, count == 4
        self.end = (place == 0) | (place == 3)
        self.low = place < 2
        self.goal = jnp.where(self.low, 3, 0)

    def relayed(self):
        return pltpu.make_async_remote_copy(
            src_ref=self.source(self.goal),
            dst_ref=self.relay,
            send_sem=self.relay_sem.at[0],
            recv_sem=self.relay_sem.at[1],
            device_id={"head": jnp.where(self.low, 1, 2)},
            device_id_type=MESH,
        )

    def send_to(self, peer):
        if not self.joined:
            self.start_one(peer)
            return
        to_goal = peer == self.goal

        @pl.when(to_goal & self.end)
        def _():
            self.relayed().start()

        @pl.when(jnp.logical_not(to_goal))
        def _():
            self.start_one(peer)

    def loop(self, act):
        if not self.joined:
            super().loop(act)
            return
        for step in range(1, self.count):
            peer = lax.rem(self.place + step, self.count)

            @pl.when(jnp.logical_not(self.end & (peer == self.goal)))
            def _():
                act(peer)

    def start(self):
        for step in range(1, self.count):
            self.send_to(nearest(self.place, self.count - step, self.count))

    def pass_on(self):
        if self.joined:

            @pl.when(jnp.logical_not(self.end))
            def _():
                self.relayed().wait_recv()
                own = self.source(self.goal)
                own[...] = (own[...].astype(F32) + self.relay[...].astype(F32)).astype(BF)
                self.start_one(self.goal)

    def finish(self):
        super().finish()
        if self.joined:

            @pl.when(self.end)
            def _():
                self.relayed().wait_send()

    def total(self):
        self.arrive()
        if self.joined:

            @pl.when(self.end)
            def _():
                ref = self.target(self.goal)
                ref[...] = jnp.zeros(ref.shape, BF)

        total = self.target(0)[...].astype(F32)
        for j in range(1, self.count):
            total = total + self.target(j)[...].astype(F32)
        return total


def body(
    block_in,
    first_gain,
    first_bias,
    qkv_weight,
    out_weight,
    second_gain,
    second_bias,
    router,
    frozen_in,
    frozen_out,
    train_in,
    train_out,
    routes,
    seq,
    cotangent,
    block_out,
    input_grad,
    vec_out,
    weights_out,
    grad_in_out,
    grad_out_out,
    s,
    cfg,
):
    n, S, T, D, L = cfg["n"], cfg["S"], cfg["T"], cfg["D"], cfg["L"]
    E, R, W, HID, cap = cfg["E"], cfg["R"], cfg["W"], cfg["HID"], cfg["cap"]
    NF = D // FW
    M = E * R
    heads = W // HEAD_DIM
    SB = 4 if S % 4 == 0 else 1
    RB = SB * R
    half = L // 2
    group = cfg["group"]
    part = W // group
    quarters = group // 2
    crowds = S // group
    z = lax.axis_index("head")
    d = lax.axis_index("dp")

    loads = []
    for index, ref in enumerate((frozen_in, train_in, frozen_out, train_out)):
        loads.append(pltpu.make_async_copy(ref.at[0], s.experts.at[index], s.load_sem.at[index]))
        loads[-1].start()
    barrier = pltpu.get_barrier_semaphore()
    for step in range(1, n):
        pl.semaphore_signal(barrier, 1, device_id={"head": lax.rem(z + step, n)}, device_id_type=MESH)

    def greet(step, carry):
        pl.semaphore_signal(barrier, 1, device_id={"dp": lax.rem(d + step, S)}, device_id_type=MESH)
        return carry

    lax.fori_loop(1, S, greet, 0)

    normal_one, inverse_one = normalize(block_in[...])
    s.normal_one[...] = normal_one
    s.inverse_one[...] = jnp.broadcast_to(inverse_one, s.inverse_one.shape)
    s.normed[z] = (normal_one * first_gain[...].reshape(1, D) + first_bias[...].reshape(1, D)).astype(BF)
    for f in range(NF):
        s.cots[f, z] = cotangent[:, f * FW : (f + 1) * FW].astype(BF)
    s.routes[z] = routes[...]
    part_id = lax.rem(d, group)
    for q in range(group):
        s.outw[z, q] = out_weight[q * part : (q + 1) * part, :]
    pl.semaphore_wait(barrier, n - 1 + S - 1)

    def over_z(source, target, send, recv):
        return Exchange("head", z, n, source, target, send, recv)

    routes_x = over_z(lambda p: s.routes.at[z], lambda p: s.routes.at[p], s.routes_s, s.routes_r)
    routes_x.start()
    T2 = T // 2
    normed_lines = [
        Line(lambda b, h=h: s.normed.at[b, pl.ds(h * T2, T2), :], s.normed_s.at[h], s.normed_r.at[h], z, n)
        for h in range(2)
    ]
    cot_lines = [Line(lambda b, f=f: s.cots.at[f, b], s.cot_s.at[f], s.cot_r.at[f], z, n) for f in range(NF)]
    outw_x = over_z(
        lambda p: s.outw.at[z, part_id], lambda p: s.outw.at[p, part_id], s.outw_s, s.outw_r
    )
    outw_x.start()
    soon, later = cot_lines[: NF - 1], cot_lines[NF - 1]
    for line in soon + normed_lines:
        line.pass_on(z)

    def project(block):
        rows = pl.ds(pl.multiple_of(block * T, T), T)
        normed = s.normed[block]
        for index in range(3):
            value = mm_nt(normed, qkv_weight[index]).astype(BF)
            if index == 0:
                value = value * jnp.asarray(HEAD_DIM**-0.5, BF)
            s.qkv[index, rows, :] = value

    routes_x.arrive()

    expert_col = lax.broadcasted_iota(jnp.int32, (E, T), 0)
    earlier = (
        lax.broadcasted_iota(jnp.int32, (T, T), 0) < lax.broadcasted_iota(jnp.int32, (T, T), 1)
    ).astype(F32).astype(BF)
    row_ids = lax.broadcasted_iota(jnp.int32, (M, T), 0)
    for j in range(n):
        first, second = s.routes[j, 0:1, :], s.routes[j, 1:2, :]
        hot0, hot1 = expert_col == first, expert_col == second
        hot = jnp.where(hot0 | hot1, 1.0, 0.0)
        count = mm(hot.astype(BF), earlier)
        for k, (names, hit) in enumerate(((first, hot0), (second, hot1))):
            slot = jnp.sum(jnp.where(hit, count, 0.0), axis=0, keepdims=True).astype(jnp.int32)
            late = names >= S
            owner = jnp.where(late, names - S, names)
            row = (owner * 2 + jnp.where(late, 1, 0)) * R + j * cap + slot
            s.target[j, k : k + 1, :] = jnp.where(slot < cap, row, -1)
        s.place[:, j * T : (j + 1) * T] = jnp.where(
            (row_ids == s.target[j, 0:1, :]) | (row_ids == s.target[j, 1:2, :]), 1.0, 0.0
        ).astype(BF)

    base = d - part_id
    plane = []
    outw_x.arrive()
    for step in range(1, n):
        other = lax.rem(z + step, n)
        plane.append(
            Exchange(
                "dp",
                part_id,
                group,
                lambda p, other=other: s.outw.at[other, part_id],
                lambda p, other=other: s.outw.at[other, p],
                s.outw_ps.at[step],
                s.outw_pr.at[step],
                device=lambda p: base + p,
            )
        )
        plane[-1].start()

    def dispatch(rows_ref, out_ref, in_ref, send, recv, f):
        tokens = rows_ref[f].reshape(n * T, FW)
        for half_id in range(2):
            span = S // 2
            rows = slice(half_id * span * 2 * R, (half_id + 1) * span * 2 * R)
            value = mm(s.place[rows, :], tokens).astype(BF)
            out_ref[f, half_id * span : (half_id + 1) * span] = value.reshape(span, 2, R, FW)
        exchange = Exchange(
            "dp", d, S, lambda p: out_ref.at[f, p], lambda p: in_ref.at[f, :, p], send.at[f], recv.at[f]
        )
        exchange.start()
        in_ref[f, :, d] = out_ref[f, d]
        return exchange

    cot_x = []
    for step in range(1, n):
        block = nearest(z, step, n)
        for line in soon:
            line.arrive(block)
            line.pass_on(block)
        if step == 1:
            later.pass_on(z)
            project(z)
        if step == n - 1:
            for f in range(NF - 1):
                cot_x.append(dispatch(s.cots, s.cot_out, s.cot_in, s.cotx_s, s.cotx_r, f))
        for line in normed_lines:
            line.arrive(block)
            line.pass_on(block)
        project(block)

    def lanes_of(rows):
        return lax.broadcasted_iota(jnp.int32, (rows, W), 1) // HEAD_DIM

    two = seq[0:1, L - 1 : L] > 0
    lane_t = lanes_of(T)
    mixed_x = over_z(lambda p: s.mixed.at[p], lambda p: s.mixed_in.at[p], s.mixed_s, s.mixed_r)

    inner_place = (z > 0) & (z < n - 1)

    def cot_service(step):
        @pl.when(inner_place)
        def _():
            block = nearest(z, step, n)
            later.arrive(block)
            later.pass_on(block)

    for qi in range(n):
        keys = (qi + 1) * T
        query_pos = lax.broadcasted_iota(jnp.int32, (T, keys), 0) + qi * T
        key_pos = lax.broadcasted_iota(jnp.int32, (T, keys), 1)
        allowed = query_pos >= key_pos
        if (qi * T) // half > 0:
            allowed = allowed & ((key_pos >= half) | jnp.logical_not(two))
        queries = s.qkv[0, qi * T : (qi + 1) * T, :].astype(F32)
        out = jnp.zeros((T, W), F32)
        for h in range(heads):
            masked_q = jnp.where(lane_t == h, queries, 0.0).astype(BF)
            scores = jnp.where(allowed, mm_nt(masked_q, s.qkv[1, :keys, :]), NEG)
            exp_vals = jnp.exp(scores - jnp.max(scores, axis=1, keepdims=True))
            weights = (exp_vals / jnp.sum(exp_vals, axis=1, keepdims=True)).astype(BF)
            s.probs[h, qi * T : (qi + 1) * T, :keys] = weights
            out = jnp.where(lane_t == h, mm(weights, s.qkv[2, :keys, :]), out)
        s.mixed[qi] = out.astype(BF)

        @pl.when(z != qi)
        def _():
            mixed_x.start_one(qi)

        if qi == 0 and n > 2:
            cot_service(1)
        if qi == 1 and n > 2:
            cot_service(2)

    for step in range(3, n):
        cot_service(step)

    @pl.when(jnp.logical_not(inner_place))
    def _():
        for step in range(1, n):
            block = nearest(z, step, n)
            later.arrive(block)
            later.pass_on(block)

    cot_x.append(dispatch(s.cots, s.cot_out, s.cot_in, s.cotx_s, s.cotx_r, NF - 1))

    for exchange in plane:
        exchange.arrive()
    mixed_x.arrive()
    s.mixed_in[z] = s.mixed[z]
    branch = jnp.zeros((T, D), F32)
    for j in range(n):
        branch = branch + mm(s.mixed_in[j], s.outw[j].reshape(W, D))
    residual = block_in[...] + branch
    s.residual[...] = residual
    normal_two, inverse_two = normalize(residual)
    s.normal_two[...] = normal_two
    s.inverse_two[...] = jnp.broadcast_to(inverse_two, s.inverse_two.shape)
    second_b = (normal_two * second_gain[...].reshape(1, D) + second_bias[...].reshape(1, D)).astype(BF)
    for f in range(NF):
        s.second[f, z] = second_b[:, f * FW : (f + 1) * FW]
    second_lines = [
        Line(lambda b, f=f: s.second.at[f, b], s.second_s.at[f], s.second_r.at[f], z, n) for f in range(NF)
    ]
    for line in second_lines:
        line.pass_on(z)
    row_x = []
    for f in range(NF):
        for step in range(1, n):
            block = nearest(z, step, n)
            second_lines[f].arrive(block)
            second_lines[f].pass_on(block)
        row_x.append(dispatch(s.second, s.row_out, s.row_in, s.rowx_s, s.rowx_r, f))

    for j in range(n):
        logits = jnp.zeros((E, T), F32)
        for f in range(NF):
            logits = logits + mm_nt(router[:, f * FW : (f + 1) * FW], s.second[f, j])
        hot0, hot1 = expert_col == s.routes[j, 0:1, :], expert_col == s.routes[j, 1:2, :]
        pick0 = jnp.sum(jnp.where(hot0, logits, 0.0), axis=0, keepdims=True)
        pick1 = jnp.sum(jnp.where(hot1, logits, 0.0), axis=0, keepdims=True)
        top = jnp.maximum(pick0, pick1)
        exp0, exp1 = jnp.exp(pick0 - top), jnp.exp(pick1 - top)
        s.gates[j, 0:1, :] = exp0 / (exp0 + exp1)
        s.gates[j, 1:2, :] = exp1 / (exp0 + exp1)
        s.gates[j, 2:4, :] = s.target[j, 0:2, :].astype(F32)
        s.gates[j, 4:8, :] = jnp.zeros((4, T), F32)
        columns = jnp.transpose(s.gates[j])
        lane_ids = lax.broadcasted_iota(jnp.int32, (T, M), 1).astype(F32)
        s.combine[j * T : (j + 1) * T, :] = jnp.where(
            lane_ids == columns[:, 2:3],
            columns[:, 0:1],
            jnp.where(lane_ids == columns[:, 3:4], columns[:, 1:2], 0.0),
        ).astype(BF)
    slot_ids = lax.broadcasted_iota(jnp.int32, (R, T), 0)
    lane_128 = lax.broadcasted_iota(jnp.int32, (128, 128), 1)
    table = jnp.zeros((128, 128), F32)
    for owner in range(S):
        total = jnp.zeros((R, T), F32)
        ids = slot_ids + (owner * 2 + 1) * R
        for j in range(n):
            total = total + jnp.where(
                ids == s.target[j, 0:1, :],
                s.gates[j, 0:1, :],
                jnp.where(ids == s.target[j, 1:2, :], s.gates[j, 1:2, :], 0.0),
            )
        column = jnp.sum(total, axis=1, keepdims=True)
        if R < 128:
            column = jnp.concatenate([column, jnp.zeros((128 - R, 1), F32)], axis=0)
        table = jnp.where(lane_128 == owner, column, table)
    table = jnp.transpose(table)
    for owner in range(S):
        s.gate_out[owner] = jnp.broadcast_to(table[owner : owner + 1, :], (8, 128))
    gate_x = Exchange(
        "dp", d, S, lambda p: s.gate_out.at[p], lambda p: s.gate_in.at[p], s.gate_s, s.gate_r
    )
    gate_x.start()
    s.gate_in[d] = s.gate_out[d]

    for load in loads:
        load.wait()

    def row_blocks(act):
        def step(i, carry):
            act(i * SB, pl.multiple_of(i * RB, RB))
            return carry

        lax.fori_loop(0, S // SB, step, 0)

    def add_up(total_ref, rows_ref, f, transposed):
        for g in range(2):

            def act(block, row):
                value = rows_ref[f, g, pl.ds(block, SB)].reshape(RB, FW)
                if transposed:
                    piece = mm_nt(value, s.experts[2 + g, :, f * FW : (f + 1) * FW])
                else:
                    piece = mm(value, s.experts[g, f * FW : (f + 1) * FW, :])
                rows = pl.ds(g * S * R + row, RB)
                total_ref[rows, :] = piece if f == 0 else total_ref[rows, :] + piece

            row_blocks(act)

    for f in range(NF):
        cot_x[f].arrive()
        add_up(s.grad_active, s.cot_in, f, True)
    for f in range(NF):
        row_x[f].arrive()
        add_up(s.hidden, s.row_in, f, False)
    EB = 16 if R % 16 == 0 else 8

    for g in range(2):

        def activate(i, carry):
            rows = pl.ds(pl.multiple_of(i * EB, EB), EB)
            flat = pl.ds(pl.multiple_of(g * S * R + i * EB, EB), EB)
            value = s.hidden[flat, :]
            normal_cdf = 0.5 * (1.0 + lax.erf(value * 0.7071067811865476))
            s.active[g, rows, :] = (value * normal_cdf).astype(BF)
            s.hidden[flat, :] = normal_cdf + value * jnp.exp(-0.5 * value * value) * 0.3989422804014327
            return carry

        lax.fori_loop(0, S * R // EB, activate, 0)

    tables = []
    for g in range(2):
        table = jnp.zeros((128, 128), F32)
        for source in range(S):
            sums = []
            for i in range(R // EB):
                rows = slice(source * R + i * EB, source * R + (i + 1) * EB)
                flat = slice(g * S * R + rows.start, g * S * R + rows.stop)
                grad = s.grad_active[flat, :]
                s.grad_hidden[g, rows, :] = (grad * s.hidden[flat, :]).astype(BF)
                sums.append(
                    jnp.sum(grad * s.active[g, rows, :].astype(F32), axis=1, keepdims=True)
                )
            if R < 128:
                sums.append(jnp.zeros((128 - R, 1), F32))
            table = jnp.where(lane_128 == source, jnp.concatenate(sums, axis=0), table)
        tables.append(jnp.transpose(table))
    row_8 = lax.broadcasted_iota(jnp.int32, (8, 128), 0)
    for source in range(S):
        s.dot_out[source] = jnp.where(
            row_8 == 0, tables[0][source : source + 1, :], tables[1][source : source + 1, :]
        )
    dot_x = Exchange("dp", d, S, lambda p: s.dot_out.at[p], lambda p: s.dot_in.at[p], s.dot_s, s.dot_r)
    dot_x.start()
    s.dot_in[d] = s.dot_out[d]

    def give_back(f, rows_ref, first_weight, out_ref, in_ref, send, recv, transposed, go=True):
        for g in range(2):

            def act(block, row):
                value = rows_ref[g, pl.ds(row, RB), :]
                if transposed:
                    piece = mm_nt(value, s.experts[first_weight + g, f * FW : (f + 1) * FW, :])
                else:
                    piece = mm(value, s.experts[first_weight + g, :, f * FW : (f + 1) * FW])
                out_ref[f, pl.ds(block, SB), g] = piece.astype(BF).reshape(SB, R, FW)

            row_blocks(act)
        exchange = Exchange(
            "dp", d, S, lambda p: out_ref.at[f, p], lambda p: in_ref.at[f, p], send.at[f], recv.at[f]
        )
        if go:
            exchange.start()
        in_ref[f, d] = out_ref[f, d]
        return exchange

    if cfg["tight"]:
        for exchange in cot_x + row_x:
            exchange.finish()
        down_out, fore_out = s.cot_out, s.row_out
    else:
        down_out, fore_out = s.down_out, s.fore_out
    down_x = [
        give_back(f, s.grad_hidden, 0, down_out, s.down_in, s.down_s, s.down_r, True) for f in range(NF)
    ]
    fore_x = [
        give_back(f, s.active, 2, fore_out, s.fore_in, s.fore_s, s.fore_r, False, f < NF - 1)
        for f in range(NF)
    ]

    gate_x.arrive()
    columns = jnp.transpose(s.gate_in[:, 0, :])
    for source in range(S):
        column = columns[:R, source : source + 1]
        rows = slice(source * R, (source + 1) * R)
        s.active[1, rows, :] = (s.active[1, rows, :].astype(F32) * column).astype(BF)
        s.grad_hidden[1, rows, :] = (s.grad_hidden[1, rows, :].astype(F32) * column).astype(BF)
    for f in range(NF):
        s.hidden[f * FW : (f + 1) * FW, :] = mm_tn(
            s.row_in[f, 1].reshape(S * R, FW), s.grad_hidden[1]
        )
        s.grad_active[0:HID, f * FW : (f + 1) * FW] = mm_tn(
            s.active[1], s.cot_in[f, 1].reshape(S * R, FW)
        )
    stores = [
        pltpu.make_async_copy(s.hidden.at[0:D, :], grad_in_out.at[0], s.store_sem.at[0]),
        pltpu.make_async_copy(s.grad_active.at[0:HID, :], grad_out_out.at[0], s.store_sem.at[1]),
    ]
    for store in stores:
        store.start()

    def gather_rows(in_ref, f):
        return mm(s.combine[...], in_ref[f].reshape(M, FW)).astype(BF).reshape(n, T, FW)

    def token_sum(f, exchanges, in_ref, part_ref, sum_ref, send, recv, relay, relay_sem):
        exchanges[f].arrive()
        part_ref[f] = gather_rows(in_ref, f)
        sums_x = Sums(
            z,
            n,
            lambda p: part_ref.at[f, p],
            lambda p: sum_ref.at[f, p],
            relay.at[f],
            send.at[f],
            recv.at[f],
            relay_sem.at[f],
        )
        sums_x.start()
        sum_ref[f, z] = part_ref[f, z]
        return sums_x

    def add_sums(sums_x):
        return jnp.concatenate([exchange.total() for exchange in sums_x], axis=1)

    if cfg["tight"]:
        for line in cot_lines:
            line.finish()
        down_part = s.cots
    else:
        down_part = s.down_part
    down_sums = []
    for f in range(NF):
        down_sums.append(
            token_sum(
                f, down_x, s.down_in, down_part, s.down_sum, s.dsum_s, s.dsum_r, s.drelay, s.drelay_sem
            )
        )
        if f > 0:
            down_sums[f - 1].pass_on()

    dot_x.arrive()
    turned = [jnp.transpose(s.dot_in[:, g, :]) for g in range(2)]
    for j in range(n):
        total = jnp.zeros((R, T), F32)
        for owner in range(S):
            for g in range(2):
                ids = slot_ids + (owner * 2 + g) * R
                sign = jnp.where(
                    ids == s.target[j, 0:1, :], 1.0, jnp.where(ids == s.target[j, 1:2, :], -1.0, 0.0)
                )
                total = total + sign * turned[g][:R, owner : owner + 1]
        s.delta_out[j] = jnp.broadcast_to(jnp.sum(total, axis=0, keepdims=True), (8, T))
    delta_x = over_z(
        lambda p: s.delta_out.at[p], lambda p: s.delta_in.at[p], s.delta_s, s.delta_r
    )
    delta_x.start()
    down_sums[NF - 1].pass_on()
    s.delta_in[z] = s.delta_out[z]
    delta_x.arrive()
    delta = s.delta_in[0, 0:1, :]
    for j in range(1, n):
        delta = delta + s.delta_in[j, 0:1, :]

    grad_chosen = s.gates[z, 0:1, :] * s.gates[z, 1:2, :] * delta
    hot0, hot1 = expert_col == s.routes[z, 0:1, :], expert_col == s.routes[z, 1:2, :]
    grad_logits = jnp.where(hot0, grad_chosen, jnp.where(hot1, -grad_chosen, 0.0))
    router_part = contract(grad_logits, router[...].astype(F32), 0, 0, lax.Precision.HIGHEST)
    router_grads = [
        contract(grad_logits, s.second[f, z].astype(F32), 1, 0, lax.Precision.HIGHEST)
        for f in range(NF)
    ]
    grad_second = add_sums(down_sums) + router_part
    normal_two = s.normal_two[...]
    pair = jnp.concatenate(
        [
            jnp.sum(grad_second * normal_two, axis=0, keepdims=True),
            jnp.sum(grad_second, axis=0, keepdims=True),
            jnp.zeros((6, D), F32),
        ],
        axis=0,
    )
    sums_now = jnp.concatenate([jnp.concatenate(router_grads, axis=1), pair], axis=0)
    H = D // 2
    for side in range(2):
        s.early[side] = sums_now[:, side * H : (side + 1) * H]
    grad_residual = cotangent[...] + norm_back(
        grad_second, normal_two, s.inverse_two[:, 0:1], second_gain[...].reshape(1, D)
    )
    s.grad_residual[...] = grad_residual
    s.branch[...] = grad_residual.astype(BF)

    def mixed_back(heads_of):
        return mm_nt(s.branch[...], s.outw[heads_of].reshape(W, D)).astype(BF)

    mixed_x.finish()
    back_x = over_z(lambda p: s.mixed.at[p], lambda p: s.grad_mixed.at[p], s.back_s, s.back_r)
    for step in range(1, n):
        peer = nearest(z, n - step, n)
        s.mixed[peer] = mixed_back(peer)
        back_x.start_one(peer)
    s.grad_mixed[z] = mixed_back(z)
    core = lax.rem(d, 2)
    quarter = part_id // 2
    mate = d + 1 - 2 * core
    for j in range(n):
        value = mm_tn(s.mixed_in[j], s.branch[...])
        for piece in range(group):
            s.gsum[piece // quarters, piece % quarters, j] = value[piece * part : (piece + 1) * part, :].astype(BF)

    def to_mate(source, target, index):
        return pltpu.make_async_remote_copy(
            src_ref=source,
            dst_ref=target,
            send_sem=s.swap_s.at[index],
            recv_sem=s.swap_r.at[index],
            device_id={"dp": mate},
            device_id_type=MESH,
        )

    def over_chips(source, target, send, recv):
        return Exchange(
            "dp", quarter, quarters, source, target, send, recv, device=lambda p: base + 2 * p + core
        )

    early_swap = to_mate(s.early.at[1 - core], s.early_mate, 3)
    early_swap.start()
    out_swap = to_mate(s.gsum.at[1 - core], s.gswap, 0)
    out_swap.start()

    if cfg["tight"]:
        for exchange in down_sums:
            exchange.finish()
        fore_part = s.cots
    else:
        fore_part = s.fore_part
    fore_sums = []

    def fore_step(f):
        fore_sums.append(
            token_sum(
                f, fore_x, s.fore_in, fore_part, s.fore_sum, s.fsum_s, s.fsum_r, s.frelay, s.frelay_sem
            )
        )

    fore_step(0)
    early_swap.wait_recv()
    s.early_mate[...] = s.early[core] + s.early_mate[...]
    early_x = over_chips(lambda p: s.early_mate, lambda p: s.early_dp.at[p], s.early_s, s.early_r)
    early_x.start()
    s.early_dp[quarter] = s.early_mate[...]
    out_swap.wait_recv()
    s.gswap[...] = (s.gsum[core].astype(F32) + s.gswap[...].astype(F32)).astype(BF)
    out_x = over_chips(lambda p: s.gswap.at[p], lambda p: s.gparts.at[p], s.outp_s, s.outp_r)
    out_x.start()
    s.gparts[quarter] = s.gswap[quarter]
    fore_x[NF - 1].start()
    fore_sums[0].pass_on()
    back_x.arrive()
    fore_step(1)

    for qi in range(n):
        keys = (qi + 1) * T
        rows = slice(qi * T, (qi + 1) * T)
        grads = s.grad_mixed[qi]
        grads_f = grads.astype(F32)
        lane_k = lanes_of(keys)
        grad_q = jnp.zeros((T, W), F32)
        grad_k = jnp.zeros((keys, W), F32)
        grad_v = jnp.zeros((keys, W), F32)
        for h in range(heads):
            masked = jnp.where(lane_t == h, grads_f, 0.0).astype(BF)
            grad_w = mm_nt(masked, s.qkv[2, :keys, :])
            weights = s.probs[h, rows, :keys]
            probs = weights.astype(F32)
            inner = jnp.sum(probs * grad_w, axis=1, keepdims=True)
            grad_s = (probs * (grad_w - inner)).astype(BF)
            grad_q = jnp.where(lane_t == h, mm(grad_s, s.qkv[1, :keys, :]), grad_q)
            grad_k = jnp.where(lane_k == h, mm_tn(grad_s, s.qkv[0, rows, :]), grad_k)
            grad_v = jnp.where(lane_k == h, mm_tn(weights, grads), grad_v)
        s.grad_proj[0, rows, :] = (grad_q * HEAD_DIM**-0.5).astype(BF)
        if qi == 0:
            s.grad_kv[...] = jnp.zeros(s.grad_kv.shape, F32)
        s.grad_kv[0, :keys, :] = s.grad_kv[0, :keys, :] + grad_k
        s.grad_kv[1, :keys, :] = s.grad_kv[1, :keys, :] + grad_v
    for index in range(2):
        s.grad_proj[1 + index] = s.grad_kv[index].astype(BF)

    def first_part(block):
        rows = pl.ds(pl.multiple_of(block * T, T), T)
        total = mm(s.grad_proj[0, rows, :], qkv_weight[0])
        for index in range(1, 3):
            total = total + mm(s.grad_proj[index, rows, :], qkv_weight[index])
        s.first_out[block] = total.astype(BF)

    first_x = Sums(
        z,
        n,
        lambda p: s.first_out.at[p],
        lambda p: s.first_in.at[p],
        s.first_relay,
        s.first_s,
        s.first_r,
        s.first_relay_sem,
    )
    for step in range(1, n):
        peer = nearest(z, n - step, n)
        first_part(peer)
        first_x.send_to(peer)
    fore_sums[1].pass_on()
    first_part(z)
    s.first_in[z] = s.first_out[z]

    def add_chips(exchange, parts_ref):
        exchange.arrive()
        total = parts_ref[0].astype(F32)
        for peer in range(1, quarters):
            total = total + parts_ref[peer].astype(F32)
        return total

    crowd = d // group
    far_x = []

    def add_crowds(total, ref, send, recv):
        if crowds == 1:
            return total
        ref[crowd] = total.astype(ref.dtype)
        exchange = Exchange(
            "dp",
            crowd,
            crowds,
            lambda p: ref.at[crowd],
            lambda p: ref.at[p],
            send,
            recv,
            device=lambda p: p * group + part_id,
        )
        exchange.start()
        exchange.arrive()
        far_x.append(exchange)
        total = ref[0].astype(F32)
        for peer in range(1, crowds):
            total = total + ref[peer].astype(F32)
        return total

    out_swap.wait_send()
    normed_all = s.normed[...].reshape(L, D)
    for index in range(3):
        value = mm_tn(s.grad_proj[index], normed_all)
        for piece in range(group):
            s.gsum[piece // quarters, piece % quarters, index] = value[
                piece * part : (piece + 1) * part, :
            ].astype(BF)
    swap = to_mate(s.gsum.at[1 - core, :, 0:3], s.wswap, 1)
    swap.start()
    first_x.pass_on()
    total = add_chips(out_x, s.gparts)
    if crowds > 1:
        total = add_crowds(total, s.out_far, s.outf_s, s.outf_r)
    s.out_piece[...] = total.astype(BF)
    out_zx = over_z(lambda p: s.out_piece.at[p], lambda p: s.out_pieces.at[p], s.outz_s, s.outz_r)
    out_zx.start()
    s.out_pieces[z] = s.out_piece[z]
    swap.wait_recv()
    s.wswap[...] = (s.gsum[core, :, 0:3].astype(F32) + s.wswap[...].astype(F32)).astype(BF)
    pair_x = over_chips(lambda p: s.wswap.at[p], lambda p: s.wparts.at[p], s.pair_s, s.pair_r)
    pair_x.start()
    s.wparts[quarter] = s.wswap[quarter]
    total = add_chips(early_x, s.early_dp)
    if crowds > 1:
        total = add_crowds(total, s.early_far, s.earlyf_s, s.earlyf_r)
    s.early_z[z] = total
    early_zx = over_z(lambda p: s.early_z.at[z], lambda p: s.early_z.at[p], s.earlyz_s, s.earlyz_r)
    early_zx.start()
    for f in range(2, NF):
        fore_step(f)

    grad_first = first_x.total()
    normal_one = s.normal_one[...]
    s.late[...] = jnp.concatenate(
        [
            jnp.sum(grad_first * normal_one, axis=0, keepdims=True),
            jnp.sum(grad_first, axis=0, keepdims=True),
            jnp.zeros((6, D), F32),
        ],
        axis=0,
    )
    late_x = Exchange("dp", d, S, lambda p: s.late, lambda p: s.late_dp.at[p], s.late_s, s.late_r)
    late_x.start()
    s.late_dp[d] = s.late[...]
    total = add_chips(pair_x, s.wparts)
    if crowds > 1:
        total = add_crowds(total, s.w_far, s.wf_s, s.wf_r)
    s.wfull[core, quarter, 0:3] = total.astype(BF)
    out_zx.arrive()
    total = s.out_pieces[0].astype(F32)
    for j in range(1, n):
        total = total + s.out_pieces[j].astype(F32)
    s.wfull[core, quarter, 3] = total.astype(BF)
    full_x = over_chips(
        lambda p: s.wfull.at[core, quarter], lambda p: s.wfull.at[core, p], s.full_s, s.full_r
    )
    full_x.start()
    own_back = to_mate(s.wfull.at[core, quarter], s.wfull.at[core, quarter], 5)
    own_back.start()
    late_x.arrive()
    total = s.late_dp[0]
    for peer in range(1, S):
        total = total + s.late_dp[peer]
    s.late_z[z] = total
    late_zx = over_z(lambda p: s.late_z.at[z], lambda p: s.late_z.at[p], s.latez_s, s.latez_r)
    late_zx.start()
    for f in range(2, NF):
        fore_sums[f].pass_on()
    input_grad[...] = s.grad_residual[...] + norm_back(
        grad_first, normal_one, s.inverse_one[:, 0:1], first_gain[...].reshape(1, D)
    )
    early_zx.arrive()
    total = s.early_z[0]
    for j in range(1, n):
        total = total + s.early_z[j]
    s.early_all[core] = total
    early_back = to_mate(s.early_all.at[core], s.early_all.at[core], 4)
    early_back.start()
    backs = [own_back]
    for turn in range(1, quarters):
        peer = lax.rem(quarter + turn, quarters)
        full_x.copy(peer, peer).wait_recv()
        backs.append(to_mate(s.wfull.at[core, peer], s.wfull.at[core, peer], 5 + turn))
        backs[-1].start()

    block_out[...] = s.residual[...] + add_sums(fore_sums)
    to_mate(s.early_all.at[core], s.early_all.at[1 - core], 4).wait_recv()
    for side in range(2):
        vec_out[0 : E + 8, side * H : (side + 1) * H] = s.early_all[side]
    late_zx.arrive()
    total = s.late_z[0]
    for j in range(1, n):
        total = total + s.late_z[j]
    vec_out[E + 8 : E + 16, :] = total
    for turn in range(quarters):
        peer = lax.rem(quarter + turn, quarters)
        to_mate(s.wfull.at[core, peer], s.wfull.at[1 - core, peer], 5 + turn).wait_recv()
    sums_store = pltpu.make_async_copy(s.wfull, weights_out, s.store_sem.at[2])
    sums_store.start()
    stores.append(sums_store)

    for store in stores:
        store.wait()
    for copy in [swap, early_swap, early_back] + backs:
        copy.wait_send()
    for lines in (normed_lines, second_lines) if cfg["tight"] else (normed_lines, cot_lines, second_lines):
        for line in lines:
            line.finish()
    done = [routes_x, outw_x, gate_x, dot_x, delta_x, early_x, pair_x, early_zx, full_x, first_x, late_x]
    if not cfg["tight"]:
        done += cot_x + row_x + down_sums
    done += far_x + [late_zx, back_x, out_x, out_zx] + plane + down_x + fore_x + fore_sums
    for exchange in done:
        exchange.finish()


def hand_over(E, *refs):
    given, vecs = refs[:5], refs[5]
    large, small = refs[6:12], refs[12:17]
    held, narrow, wide, load_sem, store_sem = refs[17:21], refs[21], refs[22], refs[23], refs[24]
    loads = [
        pltpu.make_async_copy(given[index], (list(held) + [narrow])[index], load_sem.at[index])
        for index in range(5)
    ]
    for load in (loads[4], *loads[:4]):
        load.start()
    sources = [*held, wide.at[0:3], wide.at[3]]
    stores = [
        pltpu.make_async_copy(sources[index], large[index], store_sem.at[index]) for index in range(6)
    ]
    small[0][...] = vecs[0:E, :]
    D = vecs.shape[1]
    for index, row in enumerate((E + 8, E + 9, E, E + 1)):
        small[1 + index][...] = vecs[row : row + 1, :].reshape(D)
    loads[4].wait()
    part = narrow.shape[2]
    for piece in range(narrow.shape[0]):
        wide[:, piece * part : (piece + 1) * part, :] = narrow[piece].astype(F32)
    stores[4].start()
    stores[5].start()
    for index in range(4):
        loads[index].wait()
        stores[index].start()
    for store in stores:
        store.wait()


class Names:
    pass


def shards(
    block_in,
    first_gain,
    first_bias,
    qkv_weight,
    out_weight,
    second_gain,
    second_bias,
    router_weight,
    frozen_in,
    frozen_out,
    train_in,
    train_out,
    routes,
    seq_ids,
    cotangent,
):
    T, D = block_in.shape
    L = seq_ids.shape[0]
    E = router_weight.shape[1]
    S, n = lax.axis_size("dp"), lax.axis_size("head")
    W = qkv_weight.shape[2]
    HID = frozen_in.shape[2]
    cap = max(2, 5 * T // (2 * E))
    R = -(-(n * cap) // 8) * 8
    M = E * R
    NF = D // FW
    group = 8
    quarters = group // 2
    part = W // group
    crowds = S // group
    tight = S > group
    cfg = dict(tight=tight, n=n, S=S, T=T, D=D, L=L, E=E, R=R, W=W, HID=HID, cap=cap, group=group)
    DMA = pltpu.SemaphoreType.DMA
    scratch = dict(
        experts=VMEM((4, D, HID), BF),
        normal_one=VMEM((T, D), F32),
        inverse_one=VMEM((T, 128), F32),
        normed=VMEM((n, T, D), BF),
        cots=VMEM((NF, n, T, FW), BF),
        routes=VMEM((n, 2, T), jnp.int32),
        outw=VMEM((n, group, W // group, D), BF),
        qkv=VMEM((3, L, W), BF),
        target=VMEM((n, 8, T), jnp.int32),
        gates=VMEM((n, 8, T), F32),
        place=VMEM((M, L), BF),
        combine=VMEM((L, M), BF),
        probs=VMEM((W // HEAD_DIM, L, L), BF),
        mixed=VMEM((n, T, W), BF),
        mixed_in=VMEM((n, T, W), BF),
        residual=VMEM((T, D), F32),
        normal_two=VMEM((T, D), F32),
        inverse_two=VMEM((T, 128), F32),
        second=VMEM((NF, n, T, FW), BF),
        cot_out=VMEM((NF, S, 2, R, FW), BF),
        cot_in=VMEM((NF, 2, S, R, FW), BF),
        row_out=VMEM((NF, S, 2, R, FW), BF),
        row_in=VMEM((NF, 2, S, R, FW), BF),
        gate_out=VMEM((S, 8, 128), F32),
        gate_in=VMEM((S, 8, 128), F32),
        hidden=VMEM((2 * S * R, HID), F32),
        grad_active=VMEM((2 * S * R, HID), F32),
        active=VMEM((2, S * R, HID), BF),
        grad_hidden=VMEM((2, S * R, HID), BF),
        dot_out=VMEM((S, 8, 128), F32),
        dot_in=VMEM((S, 8, 128), F32),
        down_out=VMEM((NF, S, 2, R, FW), BF),
        down_in=VMEM((NF, S, 2, R, FW), BF),
        fore_out=VMEM((NF, S, 2, R, FW), BF),
        fore_in=VMEM((NF, S, 2, R, FW), BF),
        down_part=VMEM((NF, n, T, FW), BF),
        down_sum=VMEM((NF, n, T, FW), BF),
        fore_part=VMEM((NF, n, T, FW), BF),
        fore_sum=VMEM((NF, n, T, FW), BF),
        delta_out=VMEM((n, 8, T), F32),
        delta_in=VMEM((n, 8, T), F32),
        early=VMEM((2, E + 8, D // 2), F32),
        early_mate=VMEM((E + 8, D // 2), F32),
        early_dp=VMEM((quarters, E + 8, D // 2), F32),
        early_z=VMEM((n, E + 8, D // 2), F32),
        early_all=VMEM((2, E + 8, D // 2), F32),
        late=VMEM((8, D), F32),
        late_dp=VMEM((S, 8, D), F32),
        late_z=VMEM((n, 8, D), F32),
        grad_residual=VMEM((T, D), F32),
        branch=VMEM((T, D), BF),
        grad_mixed=VMEM((n, T, W), BF),
        grad_proj=VMEM((3, L, W), BF),
        grad_kv=VMEM((2, L, W), F32),
        first_out=VMEM((n, T, D), BF),
        first_relay=VMEM((T, D), BF),
        drelay=VMEM((NF, T, FW), BF),
        frelay=VMEM((NF, T, FW), BF),
        first_in=VMEM((n, T, D), BF),
        gsum=VMEM((2, quarters, n, part, D), BF),
        gswap=VMEM((quarters, n, part, D), BF),
        gparts=VMEM((quarters, n, part, D), BF),
        out_piece=VMEM((n, part, D), BF),
        out_pieces=VMEM((n, part, D), BF),
        wswap=VMEM((quarters, 3, part, D), BF),
        wparts=VMEM((quarters, 3, part, D), BF),
        wfull=VMEM((2, quarters, 4, part, D), BF),
        load_sem=DMA((4,)),
        store_sem=DMA((3,)),
        swap_s=DMA((5 + quarters,)),
        swap_r=DMA((5 + quarters,)),
        routes_s=DMA((n,)),
        routes_r=DMA((n,)),
        normed_s=DMA((2, 2, n)),
        normed_r=DMA((2, n)),
        cot_s=DMA((NF, 2, n)),
        cot_r=DMA((NF, n)),
        outw_s=DMA((n,)),
        outw_r=DMA((n,)),
        outw_ps=DMA((n, group)),
        outw_pr=DMA((n, group)),
        mixed_s=DMA((n,)),
        mixed_r=DMA((n,)),
        cotx_s=DMA((NF, S)),
        cotx_r=DMA((NF, S)),
        rowx_s=DMA((NF, S)),
        rowx_r=DMA((NF, S)),
        second_s=DMA((NF, 2, n)),
        second_r=DMA((NF, n)),
        gate_s=DMA((S,)),
        gate_r=DMA((S,)),
        dot_s=DMA((S,)),
        dot_r=DMA((S,)),
        down_s=DMA((NF, S)),
        down_r=DMA((NF, S)),
        fore_s=DMA((NF, S)),
        fore_r=DMA((NF, S)),
        dsum_s=DMA((NF, n)),
        dsum_r=DMA((NF, n)),
        fsum_s=DMA((NF, n)),
        fsum_r=DMA((NF, n)),
        delta_s=DMA((n,)),
        delta_r=DMA((n,)),
        back_s=DMA((n,)),
        back_r=DMA((n,)),
        outp_s=DMA((quarters,)),
        outp_r=DMA((quarters,)),
        outz_s=DMA((n,)),
        outz_r=DMA((n,)),
        early_s=DMA((quarters,)),
        early_r=DMA((quarters,)),
        earlyz_s=DMA((n,)),
        earlyz_r=DMA((n,)),
        first_relay_sem=DMA((2,)),
        drelay_sem=DMA((NF, 2)),
        frelay_sem=DMA((NF, 2)),
        first_s=DMA((n,)),
        first_r=DMA((n,)),
        pair_s=DMA((quarters,)),
        pair_r=DMA((quarters,)),
        full_s=DMA((quarters,)),
        full_r=DMA((quarters,)),
        late_s=DMA((S,)),
        late_r=DMA((S,)),
        latez_s=DMA((n,)),
        latez_r=DMA((n,)),
    )
    if crowds > 1:
        scratch.update(
            early_far=VMEM((crowds, E + 8, D // 2), F32),
            earlyf_s=DMA((crowds,)),
            earlyf_r=DMA((crowds,)),
            out_far=VMEM((crowds, n, part, D), BF),
            outf_s=DMA((crowds,)),
            outf_r=DMA((crowds,)),
            w_far=VMEM((crowds, 3, part, D), BF),
            wf_s=DMA((crowds,)),
            wf_r=DMA((crowds,)),
        )
    if tight:
        del scratch["down_out"], scratch["fore_out"], scratch["fore_part"], scratch["down_part"]
    names = list(scratch)

    def kernel(*refs):
        space = Names()
        for name, ref in zip(names, refs[21:]):
            setattr(space, name, ref)
        body(*refs[:21], space, cfg)

    whole = pl.BlockSpec(memory_space=VMEM)
    left = pl.BlockSpec(memory_space=pl.ANY)
    outs = pl.pallas_call(
        kernel,
        out_shape=(
            jax.ShapeDtypeStruct((T, D), F32),
            jax.ShapeDtypeStruct((T, D), F32),
            jax.ShapeDtypeStruct((E + 16, D), F32),
            jax.ShapeDtypeStruct((2, quarters, 4, part, D), BF),
            jax.ShapeDtypeStruct((1, D, HID), F32),
            jax.ShapeDtypeStruct((1, HID, D), F32),
        ),
        in_specs=[whole] * 8 + [left] * 4 + [whole] * 3,
        out_specs=(whole, whole, whole, left, left, left),
        scratch_shapes=list(scratch.values()),
        compiler_params=pltpu.CompilerParams(
            collective_id=0, has_side_effects=True, vmem_limit_bytes=67043328
        ),
    )(
        block_in,
        first_gain,
        first_bias,
        jnp.swapaxes(qkv_weight, 1, 2),
        out_weight,
        second_gain,
        second_bias,
        router_weight.T,
        frozen_in,
        frozen_out,
        train_in,
        train_out,
        routes.T,
        seq_ids.reshape(1, L),
        cotangent,
    )
    block_out, input_grad, vecs, sums, grad_train_in, grad_train_out = outs
    sums = sums.reshape(group, 4, part, D)
    big = [block_out, input_grad, grad_train_in, grad_train_out]
    vector = jax.ShapeDtypeStruct((D,), F32)
    done = pl.pallas_call(
        functools.partial(hand_over, E),
        out_shape=[jax.ShapeDtypeStruct(array.shape, F32) for array in big]
        + [
            jax.ShapeDtypeStruct((3, W, D), F32),
            jax.ShapeDtypeStruct((W, D), F32),
            jax.ShapeDtypeStruct((E, D), F32),
        ]
        + [vector] * 4,
        in_specs=[left] * 5 + [whole],
        out_specs=[left] * 6 + [whole] * 5,
        scratch_shapes=[VMEM(array.shape, F32) for array in big]
        + [VMEM((group, 4, part, D), BF), VMEM((4, W, D), F32), DMA((5,)), DMA((6,))],
        compiler_params=pltpu.CompilerParams(vmem_limit_bytes=67043328),
    )(*big, sums, vecs)
    block_out, input_grad, grad_train_in, grad_train_out, grad_qkv, grad_out, grad_router = done[:7]
    return (
        block_out,
        input_grad,
        done[7],
        done[8],
        jnp.swapaxes(grad_qkv, 1, 2),
        grad_out,
        done[9],
        done[10],
        grad_router.T,
        grad_train_in,
        grad_train_out,
    )


def solution(mesh):
    return jax.shard_map(
        shards,
        mesh=mesh,
        in_specs=(
            P(("dp", "head"), None),
            P(),
            P(),
            P(None, None, "head"),
            P("head", None),
            P(),
            P(),
            P(),
            P("dp", None, "head"),
            P("dp", "head", None),
            P("dp", None, "head"),
            P("dp", "head", None),
            P(("dp", "head"), None),
            P("dp"),
            P(("dp", "head"), None),
        ),
        out_specs=(
            P(("dp", "head"), None),
            P(("dp", "head"), None),
            P(),
            P(),
            P(None, None, "head"),
            P("head", None),
            P(),
            P(),
            P(),
            P("dp", None, "head"),
            P("dp", "head", None),
        ),
        check_vma=False,
    )
```

```python
import functools

import jax
import jax.numpy as jnp
from jax import lax
from jax.experimental import pallas as pl
from jax.experimental.pallas import tpu as pltpu
from jax.sharding import PartitionSpec as P

HEAD_DIM = 64
EPS = 1e-05
NEG = -1e30
FW = 256
F32 = jnp.float32
BF = jnp.bfloat16
MESH = pl.DeviceIdType.MESH
VMEM = pltpu.VMEM


def contract(left, right, left_dim, right_dim, precision=None):
    return lax.dot_general(
        left,
        right,
        (((left_dim,), (right_dim,)), ((), ())),
        precision=precision,
        preferred_element_type=F32,
    )


def mm(left, right):
    return contract(left, right, 1, 0)


def mm_nt(left, right):
    return contract(left, right, 1, 1)


def mm_tn(left, right):
    return contract(left, right, 0, 0)


def normalize(values):
    average = jnp.mean(values, axis=-1, keepdims=True)
    centred = values - average
    variance = jnp.mean(centred * centred, axis=-1, keepdims=True)
    inverse = lax.rsqrt(variance + EPS)
    return centred * inverse, inverse


def norm_back(grad_norm, normal, inverse, gain_vec):
    scaled = grad_norm * gain_vec
    first_mean = jnp.mean(scaled, axis=-1, keepdims=True)
    second_mean = jnp.mean(scaled * normal, axis=-1, keepdims=True)
    return inverse * (scaled - first_mean - normal * second_mean)


def nearest(place, step, count):
    low, high = place, count - 1 - place
    both = jnp.minimum(low, high)
    near = jnp.where(step % 2 == 1, place - (step + 1) // 2, place + step // 2)
    far = jnp.where(low > high, place - (step - both), place + (step - both))
    return jnp.where(step <= 2 * both, near, far)


class Line:
    def __init__(self, ref_of, send, recv, place, count):
        self.ref_of, self.send, self.recv = ref_of, send, recv
        self.place, self.count = place, count

    def copy(self, block, up):
        step = 1 if up else -1
        return pltpu.make_async_remote_copy(
            src_ref=self.ref_of(block),
            dst_ref=self.ref_of(block),
            send_sem=self.send.at[0 if up else 1, block],
            recv_sem=self.recv.at[block],
            device_id={"head": self.place + step},
            device_id_type=MESH,
        )

    def pass_on(self, block):
        @pl.when((block <= self.place) & (self.place < self.count - 1))
        def _():
            self.copy(block, True).start()

        @pl.when((block >= self.place) & (self.place > 0))
        def _():
            self.copy(block, False).start()

    def arrive(self, block):
        self.copy(block, True).wait_recv()

    def finish(self):
        for block in range(self.count):

            @pl.when((block <= self.place) & (self.place < self.count - 1))
            def _():
                self.copy(block, True).wait_send()

            @pl.when((block >= self.place) & (self.place > 0))
            def _():
                self.copy(block, False).wait_send()


class Exchange:
    def __init__(self, axis, place, count, source, target, send, recv, device=None):
        self.axis, self.place, self.count = axis, place, count
        self.source, self.target, self.send, self.recv = source, target, send, recv
        self.device = device or (lambda peer: peer)

    def copy(self, peer, lands):
        return pltpu.make_async_remote_copy(
            src_ref=self.source(peer),
            dst_ref=self.target(lands),
            send_sem=self.send.at[peer],
            recv_sem=self.recv.at[lands],
            device_id={self.axis: self.device(peer)},
            device_id_type=MESH,
        )

    def loop(self, act):
        def body(step, carry):
            act(lax.rem(self.place + step, self.count))
            return carry

        lax.fori_loop(1, self.count, body, 0)

    def start_one(self, peer):
        self.copy(peer, self.place).start()

    def start(self):
        self.loop(self.start_one)

    def arrive(self):
        self.loop(lambda peer: self.copy(peer, peer).wait_recv())

    def finish(self):
        self.loop(lambda peer: self.copy(peer, self.place).wait_send())


class Sums(Exchange):
    def __init__(self, place, count, source, target, relay, send, recv, relay_sem):
        super().__init__("head", place, count, source, target, send, recv)
        self.relay, self.relay_sem, self.joined = relay, relay_sem, count == 4
        self.end = (place == 0) | (place == 3)
        self.low = place < 2
        self.goal = jnp.where(self.low, 3, 0)

    def relayed(self):
        return pltpu.make_async_remote_copy(
            src_ref=self.source(self.goal),
            dst_ref=self.relay,
            send_sem=self.relay_sem.at[0],
            recv_sem=self.relay_sem.at[1],
            device_id={"head": jnp.where(self.low, 1, 2)},
            device_id_type=MESH,
        )

    def send_to(self, peer):
        if not self.joined:
            self.start_one(peer)
            return
        to_goal = peer == self.goal

        @pl.when(to_goal & self.end)
        def _():
            self.relayed().start()

        @pl.when(jnp.logical_not(to_goal))
        def _():
            self.start_one(peer)

    def loop(self, act):
        if not self.joined:
            super().loop(act)
            return
        for step in range(1, self.count):
            peer = lax.rem(self.place + step, self.count)

            @pl.when(jnp.logical_not(self.end & (peer == self.goal)))
            def _():
                act(peer)

    def start(self):
        for step in range(1, self.count):
            self.send_to(nearest(self.place, self.count - step, self.count))

    def pass_on(self):
        if self.joined:

            @pl.when(jnp.logical_not(self.end))
            def _():
                self.relayed().wait_recv()
                own = self.source(self.goal)
                own[...] = (own[...].astype(F32) + self.relay[...].astype(F32)).astype(BF)
                self.start_one(self.goal)

    def finish(self):
        super().finish()
        if self.joined:

            @pl.when(self.end)
            def _():
                self.relayed().wait_send()

    def total(self):
        self.arrive()
        if self.joined:

            @pl.when(self.end)
            def _():
                ref = self.target(self.goal)
                ref[...] = jnp.zeros(ref.shape, BF)

        total = self.target(0)[...].astype(F32)
        for j in range(1, self.count):
            total = total + self.target(j)[...].astype(F32)
        return total


def body(
    block_in,
    first_gain,
    first_bias,
    qkv_weight,
    out_weight,
    second_gain,
    second_bias,
    router,
    frozen_in,
    frozen_out,
    train_in,
    train_out,
    routes,
    seq,
    cotangent,
    block_out,
    input_grad,
    vec_out,
    weights_out,
    grad_in_out,
    grad_out_out,
    s,
    cfg,
):
    n, S, T, D, L = cfg["n"], cfg["S"], cfg["T"], cfg["D"], cfg["L"]
    E, R, W, HID, cap = cfg["E"], cfg["R"], cfg["W"], cfg["HID"], cfg["cap"]
    NF = D // FW
    M = E * R
    heads = W // HEAD_DIM
    SB = 4 if S % 4 == 0 else 1
    RB = SB * R
    half = L // 2
    group = cfg["group"]
    part = W // group
    quarters = group // 2
    crowds = S // group
    z = lax.axis_index("head")
    d = lax.axis_index("dp")

    loads = []
    for index, ref in enumerate((frozen_in, train_in, frozen_out, train_out)):
        loads.append(pltpu.make_async_copy(ref.at[0], s.experts.at[index], s.load_sem.at[index]))
        loads[-1].start()
    barrier = pltpu.get_barrier_semaphore()
    for step in range(1, n):
        pl.semaphore_signal(barrier, 1, device_id={"head": lax.rem(z + step, n)}, device_id_type=MESH)

    def greet(step, carry):
        pl.semaphore_signal(barrier, 1, device_id={"dp": lax.rem(d + step, S)}, device_id_type=MESH)
        return carry

    lax.fori_loop(1, S, greet, 0)

    normal_one, inverse_one = normalize(block_in[...])
    s.normal_one[...] = normal_one
    s.inverse_one[...] = jnp.broadcast_to(inverse_one, s.inverse_one.shape)
    s.normed[z] = (normal_one * first_gain[...].reshape(1, D) + first_bias[...].reshape(1, D)).astype(BF)
    for f in range(NF):
        s.cots[f, z] = cotangent[:, f * FW : (f + 1) * FW].astype(BF)
    s.routes[z] = routes[...]
    part_id = lax.rem(d, group)
    for q in range(group):
        s.outw[z, q] = out_weight[q * part : (q + 1) * part, :]
    pl.semaphore_wait(barrier, n - 1 + S - 1)

    def over_z(source, target, send, recv):
        return Exchange("head", z, n, source, target, send, recv)

    routes_x = over_z(lambda p: s.routes.at[z], lambda p: s.routes.at[p], s.routes_s, s.routes_r)
    routes_x.start()
    T2 = T // 2
    normed_lines = [
        Line(lambda b, h=h: s.normed.at[b, pl.ds(h * T2, T2), :], s.normed_s.at[h], s.normed_r.at[h], z, n)
        for h in range(2)
    ]
    cot_lines = [Line(lambda b, f=f: s.cots.at[f, b], s.cot_s.at[f], s.cot_r.at[f], z, n) for f in range(NF)]
    outw_x = over_z(
        lambda p: s.outw.at[z, part_id], lambda p: s.outw.at[p, part_id], s.outw_s, s.outw_r
    )
    outw_x.start()
    soon, later = cot_lines[: NF - 1], cot_lines[NF - 1]
    for line in soon + normed_lines:
        line.pass_on(z)

    def project(block):
        rows = pl.ds(pl.multiple_of(block * T, T), T)
        normed = s.normed[block]
        for index in range(3):
            value = mm_nt(normed, qkv_weight[index]).astype(BF)
            if index == 0:
                value = value * jnp.asarray(HEAD_DIM**-0.5, BF)
            s.qkv[index, rows, :] = value

    routes_x.arrive()

    expert_col = lax.broadcasted_iota(jnp.int32, (E, T), 0)
    earlier = (
        lax.broadcasted_iota(jnp.int32, (T, T), 0) < lax.broadcasted_iota(jnp.int32, (T, T), 1)
    ).astype(F32).astype(BF)
    row_ids = lax.broadcasted_iota(jnp.int32, (M, T), 0)
    for j in range(n):
        first, second = s.routes[j, 0:1, :], s.routes[j, 1:2, :]
        hot0, hot1 = expert_col == first, expert_col == second
        hot = jnp.where(hot0 | hot1, 1.0, 0.0)
        count = mm(hot.astype(BF), earlier)
        for k, (names, hit) in enumerate(((first, hot0), (second, hot1))):
            slot = jnp.sum(jnp.where(hit, count, 0.0), axis=0, keepdims=True).astype(jnp.int32)
            late = names >= S
            owner = jnp.where(late, names - S, names)
            row = (owner * 2 + jnp.where(late, 1, 0)) * R + j * cap + slot
            s.target[j, k : k + 1, :] = jnp.where(slot < cap, row, -1)
        s.place[:, j * T : (j + 1) * T] = jnp.where(
            (row_ids == s.target[j, 0:1, :]) | (row_ids == s.target[j, 1:2, :]), 1.0, 0.0
        ).astype(BF)

    base = d - part_id
    plane = []
    outw_x.arrive()
    for step in range(1, n):
        other = lax.rem(z + step, n)
        plane.append(
            Exchange(
                "dp",
                part_id,
                group,
                lambda p, other=other: s.outw.at[other, part_id],
                lambda p, other=other: s.outw.at[other, p],
                s.outw_ps.at[step],
                s.outw_pr.at[step],
                device=lambda p: base + p,
            )
        )
        plane[-1].start()

    def dispatch(rows_ref, out_ref, in_ref, send, recv, f):
        tokens = rows_ref[f].reshape(n * T, FW)
        for half_id in range(2):
            span = S // 2
            rows = slice(half_id * span * 2 * R, (half_id + 1) * span * 2 * R)
            value = mm(s.place[rows, :], tokens).astype(BF)
            out_ref[f, half_id * span : (half_id + 1) * span] = value.reshape(span, 2, R, FW)
        exchange = Exchange(
            "dp", d, S, lambda p: out_ref.at[f, p], lambda p: in_ref.at[f, :, p], send.at[f], recv.at[f]
        )
        exchange.start()
        in_ref[f, :, d] = out_ref[f, d]
        return exchange

    cot_x = []
    for step in range(1, n):
        block = nearest(z, step, n)
        for line in soon:
            line.arrive(block)
            line.pass_on(block)
        if step == 1:
            later.pass_on(z)
            project(z)
        if step == n - 1:
            for f in range(NF - 1):
                cot_x.append(dispatch(s.cots, s.cot_out, s.cot_in, s.cotx_s, s.cotx_r, f))
        for line in normed_lines:
            line.arrive(block)
            line.pass_on(block)
        project(block)

    def lanes_of(rows):
        return lax.broadcasted_iota(jnp.int32, (rows, W), 1) // HEAD_DIM

    two = seq[0:1, L - 1 : L] > 0
    lane_t = lanes_of(T)
    mixed_x = over_z(lambda p: s.mixed.at[p], lambda p: s.mixed_in.at[p], s.mixed_s, s.mixed_r)

    inner_place = (z > 0) & (z < n - 1)

    def cot_service(step):
        @pl.when(inner_place)
        def _():
            block = nearest(z, step, n)
            later.arrive(block)
            later.pass_on(block)

    for qi in range(n):
        keys = (qi + 1) * T
        query_pos = lax.broadcasted_iota(jnp.int32, (T, keys), 0) + qi * T
        key_pos = lax.broadcasted_iota(jnp.int32, (T, keys), 1)
        allowed = query_pos >= key_pos
        if (qi * T) // half > 0:
            allowed = allowed & ((key_pos >= half) | jnp.logical_not(two))
        queries = s.qkv[0, qi * T : (qi + 1) * T, :].astype(F32)
        out = jnp.zeros((T, W), F32)
        for h in range(heads):
            masked_q = jnp.where(lane_t == h, queries, 0.0).astype(BF)
            scores = jnp.where(allowed, mm_nt(masked_q, s.qkv[1, :keys, :]), NEG)
            exp_vals = jnp.exp(scores - jnp.max(scores, axis=1, keepdims=True))
            weights = (exp_vals / jnp.sum(exp_vals, axis=1, keepdims=True)).astype(BF)
            s.probs[h, qi * T : (qi + 1) * T, :keys] = weights
            out = jnp.where(lane_t == h, mm(weights, s.qkv[2, :keys, :]), out)
        s.mixed[qi] = out.astype(BF)

        @pl.when(z != qi)
        def _():
            mixed_x.start_one(qi)

        if qi == 0 and n > 2:
            cot_service(1)
        if qi == 1 and n > 2:
            cot_service(2)

    for step in range(3, n):
        cot_service(step)

    @pl.when(jnp.logical_not(inner_place))
    def _():
        for step in range(1, n):
            block = nearest(z, step, n)
            later.arrive(block)
            later.pass_on(block)

    cot_x.append(dispatch(s.cots, s.cot_out, s.cot_in, s.cotx_s, s.cotx_r, NF - 1))

    for exchange in plane:
        exchange.arrive()
    mixed_x.arrive()
    s.mixed_in[z] = s.mixed[z]
    branch = jnp.zeros((T, D), F32)
    for j in range(n):
        branch = branch + mm(s.mixed_in[j], s.outw[j].reshape(W, D))
    residual = block_in[...] + branch
    s.residual[...] = residual
    normal_two, inverse_two = normalize(residual)
    s.normal_two[...] = normal_two
    s.inverse_two[...] = jnp.broadcast_to(inverse_two, s.inverse_two.shape)
    second_b = (normal_two * second_gain[...].reshape(1, D) + second_bias[...].reshape(1, D)).astype(BF)
    for f in range(NF):
        s.second[f, z] = second_b[:, f * FW : (f + 1) * FW]
    second_lines = [
        Line(lambda b, f=f: s.second.at[f, b], s.second_s.at[f], s.second_r.at[f], z, n) for f in range(NF)
    ]
    for line in second_lines:
        line.pass_on(z)
    row_x = []
    for f in range(NF):
        for step in range(1, n):
            block = nearest(z, step, n)
            second_lines[f].arrive(block)
            second_lines[f].pass_on(block)
        row_x.append(dispatch(s.second, s.row_out, s.row_in, s.rowx_s, s.rowx_r, f))

    for j in range(n):
        logits = jnp.zeros((E, T), F32)
        for f in range(NF):
            logits = logits + mm_nt(router[:, f * FW : (f + 1) * FW], s.second[f, j])
        hot0, hot1 = expert_col == s.routes[j, 0:1, :], expert_col == s.routes[j, 1:2, :]
        pick0 = jnp.sum(jnp.where(hot0, logits, 0.0), axis=0, keepdims=True)
        pick1 = jnp.sum(jnp.where(hot1, logits, 0.0), axis=0, keepdims=True)
        top = jnp.maximum(pick0, pick1)
        exp0, exp1 = jnp.exp(pick0 - top), jnp.exp(pick1 - top)
        s.gates[j, 0:1, :] = exp0 / (exp0 + exp1)
        s.gates[j, 1:2, :] = exp1 / (exp0 + exp1)
        s.gates[j, 2:4, :] = s.target[j, 0:2, :].astype(F32)
        s.gates[j, 4:8, :] = jnp.zeros((4, T), F32)
        columns = jnp.transpose(s.gates[j])
        lane_ids = lax.broadcasted_iota(jnp.int32, (T, M), 1).astype(F32)
        s.combine[j * T : (j + 1) * T, :] = jnp.where(
            lane_ids == columns[:, 2:3],
            columns[:, 0:1],
            jnp.where(lane_ids == columns[:, 3:4], columns[:, 1:2], 0.0),
        ).astype(BF)
    slot_ids = lax.broadcasted_iota(jnp.int32, (R, T), 0)
    lane_128 = lax.broadcasted_iota(jnp.int32, (128, 128), 1)
    table = jnp.zeros((128, 128), F32)
    for owner in range(S):
        total = jnp.zeros((R, T), F32)
        ids = slot_ids + (owner * 2 + 1) * R
        for j in range(n):
            total = total + jnp.where(
                ids == s.target[j, 0:1, :],
                s.gates[j, 0:1, :],
                jnp.where(ids == s.target[j, 1:2, :], s.gates[j, 1:2, :], 0.0),
            )
        column = jnp.sum(total, axis=1, keepdims=True)
        if R < 128:
            column = jnp.concatenate([column, jnp.zeros((128 - R, 1), F32)], axis=0)
        table = jnp.where(lane_128 == owner, column, table)
    table = jnp.transpose(table)
    for owner in range(S):
        s.gate_out[owner] = jnp.broadcast_to(table[owner : owner + 1, :], (8, 128))
    gate_x = Exchange(
        "dp", d, S, lambda p: s.gate_out.at[p], lambda p: s.gate_in.at[p], s.gate_s, s.gate_r
    )
    gate_x.start()
    s.gate_in[d] = s.gate_out[d]

    for load in loads:
        load.wait()

    def row_blocks(act):
        def step(i, carry):
            act(i * SB, pl.multiple_of(i * RB, RB))
            return carry

        lax.fori_loop(0, S // SB, step, 0)

    def add_up(total_ref, rows_ref, f, transposed):
        for g in range(2):

            def act(block, row):
                value = rows_ref[f, g, pl.ds(block, SB)].reshape(RB, FW)
                if transposed:
                    piece = mm_nt(value, s.experts[2 + g, :, f * FW : (f + 1) * FW])
                else:
                    piece = mm(value, s.experts[g, f * FW : (f + 1) * FW, :])
                rows = pl.ds(g * S * R + row, RB)
                total_ref[rows, :] = piece if f == 0 else total_ref[rows, :] + piece

            row_blocks(act)

    for f in range(NF):
        cot_x[f].arrive()
        add_up(s.grad_active, s.cot_in, f, True)
    for f in range(NF):
        row_x[f].arrive()
        add_up(s.hidden, s.row_in, f, False)
    EB = 16 if R % 16 == 0 else 8

    for g in range(2):

        def activate(i, carry):
            rows = pl.ds(pl.multiple_of(i * EB, EB), EB)
            flat = pl.ds(pl.multiple_of(g * S * R + i * EB, EB), EB)
            value = s.hidden[flat, :]
            normal_cdf = 0.5 * (1.0 + lax.erf(value * 0.7071067811865476))
            s.active[g, rows, :] = (value * normal_cdf).astype(BF)
            s.hidden[flat, :] = normal_cdf + value * jnp.exp(-0.5 * value * value) * 0.3989422804014327
            return carry

        lax.fori_loop(0, S * R // EB, activate, 0)

    tables = []
    for g in range(2):
        table = jnp.zeros((128, 128), F32)
        for source in range(S):
            sums = []
            for i in range(R // EB):
                rows = slice(source * R + i * EB, source * R + (i + 1) * EB)
                flat = slice(g * S * R + rows.start, g * S * R + rows.stop)
                grad = s.grad_active[flat, :]
                s.grad_hidden[g, rows, :] = (grad * s.hidden[flat, :]).astype(BF)
                sums.append(
                    jnp.sum(grad * s.active[g, rows, :].astype(F32), axis=1, keepdims=True)
                )
            if R < 128:
                sums.append(jnp.zeros((128 - R, 1), F32))
            table = jnp.where(lane_128 == source, jnp.concatenate(sums, axis=0), table)
        tables.append(jnp.transpose(table))
    row_8 = lax.broadcasted_iota(jnp.int32, (8, 128), 0)
    for source in range(S):
        s.dot_out[source] = jnp.where(
            row_8 == 0, tables[0][source : source + 1, :], tables[1][source : source + 1, :]
        )
    dot_x = Exchange("dp", d, S, lambda p: s.dot_out.at[p], lambda p: s.dot_in.at[p], s.dot_s, s.dot_r)
    dot_x.start()
    s.dot_in[d] = s.dot_out[d]

    def give_back(f, rows_ref, first_weight, out_ref, in_ref, send, recv, transposed, go=True):
        for g in range(2):

            def act(block, row):
                value = rows_ref[g, pl.ds(row, RB), :]
                if transposed:
                    piece = mm_nt(value, s.experts[first_weight + g, f * FW : (f + 1) * FW, :])
                else:
                    piece = mm(value, s.experts[first_weight + g, :, f * FW : (f + 1) * FW])
                out_ref[f, pl.ds(block, SB), g] = piece.astype(BF).reshape(SB, R, FW)

            row_blocks(act)
        exchange = Exchange(
            "dp", d, S, lambda p: out_ref.at[f, p], lambda p: in_ref.at[f, p], send.at[f], recv.at[f]
        )
        if go:
            exchange.start()
        in_ref[f, d] = out_ref[f, d]
        return exchange

    if cfg["tight"]:
        for exchange in cot_x + row_x:
            exchange.finish()
        down_out, fore_out = s.cot_out, s.row_out
    else:
        down_out, fore_out = s.down_out, s.fore_out
    down_x = [
        give_back(f, s.grad_hidden, 0, down_out, s.down_in, s.down_s, s.down_r, True) for f in range(NF)
    ]
    fore_x = [
        give_back(f, s.active, 2, fore_out, s.fore_in, s.fore_s, s.fore_r, False, f < NF - 1)
        for f in range(NF)
    ]

    gate_x.arrive()
    columns = jnp.transpose(s.gate_in[:, 0, :])
    for source in range(S):
        column = columns[:R, source : source + 1]
        rows = slice(source * R, (source + 1) * R)
        s.active[1, rows, :] = (s.active[1, rows, :].astype(F32) * column).astype(BF)
        s.grad_hidden[1, rows, :] = (s.grad_hidden[1, rows, :].astype(F32) * column).astype(BF)
    for f in range(NF):
        s.hidden[f * FW : (f + 1) * FW, :] = mm_tn(
            s.row_in[f, 1].reshape(S * R, FW), s.grad_hidden[1]
        )
        s.grad_active[0:HID, f * FW : (f + 1) * FW] = mm_tn(
            s.active[1], s.cot_in[f, 1].reshape(S * R, FW)
        )
    stores = [
        pltpu.make_async_copy(s.hidden.at[0:D, :], grad_in_out.at[0], s.store_sem.at[0]),
        pltpu.make_async_copy(s.grad_active.at[0:HID, :], grad_out_out.at[0], s.store_sem.at[1]),
    ]
    for store in stores:
        store.start()

    def gather_rows(in_ref, f):
        return mm(s.combine[...], in_ref[f].reshape(M, FW)).astype(BF).reshape(n, T, FW)

    def token_sum(f, exchanges, in_ref, part_ref, sum_ref, send, recv, relay, relay_sem):
        exchanges[f].arrive()
        part_ref[f] = gather_rows(in_ref, f)
        sums_x = Sums(
            z,
            n,
            lambda p: part_ref.at[f, p],
            lambda p: sum_ref.at[f, p],
            relay.at[f],
            send.at[f],
            recv.at[f],
            relay_sem.at[f],
        )
        sums_x.start()
        sum_ref[f, z] = part_ref[f, z]
        return sums_x

    def add_sums(sums_x):
        return jnp.concatenate([exchange.total() for exchange in sums_x], axis=1)

    if cfg["tight"]:
        for line in cot_lines:
            line.finish()
        down_part = s.cots
    else:
        down_part = s.down_part
    down_sums = []
    for f in range(NF):
        down_sums.append(
            token_sum(
                f, down_x, s.down_in, down_part, s.down_sum, s.dsum_s, s.dsum_r, s.drelay, s.drelay_sem
            )
        )
        if f > 0:
            down_sums[f - 1].pass_on()

    dot_x.arrive()
    turned = [jnp.transpose(s.dot_in[:, g, :]) for g in range(2)]
    for j in range(n):
        total = jnp.zeros((R, T), F32)
        for owner in range(S):
            for g in range(2):
                ids = slot_ids + (owner * 2 + g) * R
                sign = jnp.where(
                    ids == s.target[j, 0:1, :], 1.0, jnp.where(ids == s.target[j, 1:2, :], -1.0, 0.0)
                )
                total = total + sign * turned[g][:R, owner : owner + 1]
        s.delta_out[j] = jnp.broadcast_to(jnp.sum(total, axis=0, keepdims=True), (8, T))
    delta_x = over_z(
        lambda p: s.delta_out.at[p], lambda p: s.delta_in.at[p], s.delta_s, s.delta_r
    )
    delta_x.start()
    down_sums[NF - 1].pass_on()
    s.delta_in[z] = s.delta_out[z]
    delta_x.arrive()
    delta = s.delta_in[0, 0:1, :]
    for j in range(1, n):
        delta = delta + s.delta_in[j, 0:1, :]

    grad_chosen = s.gates[z, 0:1, :] * s.gates[z, 1:2, :] * delta
    hot0, hot1 = expert_col == s.routes[z, 0:1, :], expert_col == s.routes[z, 1:2, :]
    grad_logits = jnp.where(hot0, grad_chosen, jnp.where(hot1, -grad_chosen, 0.0))
    router_part = contract(grad_logits, router[...].astype(F32), 0, 0, lax.Precision.HIGHEST)
    router_grads = [
        contract(grad_logits, s.second[f, z].astype(F32), 1, 0, lax.Precision.HIGHEST)
        for f in range(NF)
    ]
    grad_second = add_sums(down_sums) + router_part
    normal_two = s.normal_two[...]
    pair = jnp.concatenate(
        [
            jnp.sum(grad_second * normal_two, axis=0, keepdims=True),
            jnp.sum(grad_second, axis=0, keepdims=True),
            jnp.zeros((6, D), F32),
        ],
        axis=0,
    )
    sums_now = jnp.concatenate([jnp.concatenate(router_grads, axis=1), pair], axis=0)
    H = D // 2
    for side in range(2):
        s.early[side] = sums_now[:, side * H : (side + 1) * H]
    grad_residual = cotangent[...] + norm_back(
        grad_second, normal_two, s.inverse_two[:, 0:1], second_gain[...].reshape(1, D)
    )
    s.grad_residual[...] = grad_residual
    s.branch[...] = grad_residual.astype(BF)

    def mixed_back(heads_of):
        return mm_nt(s.branch[...], s.outw[heads_of].reshape(W, D)).astype(BF)

    mixed_x.finish()
    back_x = over_z(lambda p: s.mixed.at[p], lambda p: s.grad_mixed.at[p], s.back_s, s.back_r)
    for step in range(1, n):
        peer = nearest(z, n - step, n)
        s.mixed[peer] = mixed_back(peer)
        back_x.start_one(peer)
    s.grad_mixed[z] = mixed_back(z)
    core = lax.rem(d, 2)
    quarter = part_id // 2
    mate = d + 1 - 2 * core
    for j in range(n):
        value = mm_tn(s.mixed_in[j], s.branch[...])
        for piece in range(group):
            s.gsum[piece // quarters, piece % quarters, j] = value[piece * part : (piece + 1) * part, :].astype(BF)

    def to_mate(source, target, index):
        return pltpu.make_async_remote_copy(
            src_ref=source,
            dst_ref=target,
            send_sem=s.swap_s.at[index],
            recv_sem=s.swap_r.at[index],
            device_id={"dp": mate},
            device_id_type=MESH,
        )

    def over_chips(source, target, send, recv):
        return Exchange(
            "dp", quarter, quarters, source, target, send, recv, device=lambda p: base + 2 * p + core
        )

    early_swap = to_mate(s.early.at[1 - core], s.early_mate, 3)
    early_swap.start()
    out_swap = to_mate(s.gsum.at[1 - core], s.gswap, 0)
    out_swap.start()

    if cfg["tight"]:
        for exchange in down_sums:
            exchange.finish()
        fore_part = s.cots
    else:
        fore_part = s.fore_part
    fore_sums = []

    def fore_step(f):
        fore_sums.append(
            token_sum(
                f, fore_x, s.fore_in, fore_part, s.fore_sum, s.fsum_s, s.fsum_r, s.frelay, s.frelay_sem
            )
        )

    fore_step(0)
    early_swap.wait_recv()
    s.early_mate[...] = s.early[core] + s.early_mate[...]
    early_x = over_chips(lambda p: s.early_mate, lambda p: s.early_dp.at[p], s.early_s, s.early_r)
    early_x.start()
    s.early_dp[quarter] = s.early_mate[...]
    out_swap.wait_recv()
    s.gswap[...] = (s.gsum[core].astype(F32) + s.gswap[...].astype(F32)).astype(BF)
    out_x = over_chips(lambda p: s.gswap.at[p], lambda p: s.gparts.at[p], s.outp_s, s.outp_r)
    out_x.start()
    s.gparts[quarter] = s.gswap[quarter]
    fore_x[NF - 1].start()
    fore_sums[0].pass_on()
    back_x.arrive()
    fore_step(1)

    for qi in range(n):
        keys = (qi + 1) * T
        rows = slice(qi * T, (qi + 1) * T)
        grads = s.grad_mixed[qi]
        grads_f = grads.astype(F32)
        lane_k = lanes_of(keys)
        grad_q = jnp.zeros((T, W), F32)
        grad_k = jnp.zeros((keys, W), F32)
        grad_v = jnp.zeros((keys, W), F32)
        for h in range(heads):
            masked = jnp.where(lane_t == h, grads_f, 0.0).astype(BF)
            grad_w = mm_nt(masked, s.qkv[2, :keys, :])
            weights = s.probs[h, rows, :keys]
            probs = weights.astype(F32)
            inner = jnp.sum(probs * grad_w, axis=1, keepdims=True)
            grad_s = (probs * (grad_w - inner)).astype(BF)
            grad_q = jnp.where(lane_t == h, mm(grad_s, s.qkv[1, :keys, :]), grad_q)
            grad_k = jnp.where(lane_k == h, mm_tn(grad_s, s.qkv[0, rows, :]), grad_k)
            grad_v = jnp.where(lane_k == h, mm_tn(weights, grads), grad_v)
        s.grad_proj[0, rows, :] = (grad_q * HEAD_DIM**-0.5).astype(BF)
        if qi == 0:
            s.grad_kv[...] = jnp.zeros(s.grad_kv.shape, F32)
        s.grad_kv[0, :keys, :] = s.grad_kv[0, :keys, :] + grad_k
        s.grad_kv[1, :keys, :] = s.grad_kv[1, :keys, :] + grad_v
    for index in range(2):
        s.grad_proj[1 + index] = s.grad_kv[index].astype(BF)

    def first_part(block):
        rows = pl.ds(pl.multiple_of(block * T, T), T)
        total = mm(s.grad_proj[0, rows, :], qkv_weight[0])
        for index in range(1, 3):
            total = total + mm(s.grad_proj[index, rows, :], qkv_weight[index])
        s.first_out[block] = total.astype(BF)

    first_x = Sums(
        z,
        n,
        lambda p: s.first_out.at[p],
        lambda p: s.first_in.at[p],
        s.first_relay,
        s.first_s,
        s.first_r,
        s.first_relay_sem,
    )
    for step in range(1, n):
        peer = nearest(z, n - step, n)
        first_part(peer)
        first_x.send_to(peer)
    fore_sums[1].pass_on()
    first_part(z)
    s.first_in[z] = s.first_out[z]

    def add_chips(exchange, parts_ref):
        exchange.arrive()
        total = parts_ref[0].astype(F32)
        for peer in range(1, quarters):
            total = total + parts_ref[peer].astype(F32)
        return total

    crowd = d // group
    far_x = []

    def add_crowds(total, ref, send, recv):
        if crowds == 1:
            return total
        ref[crowd] = total.astype(ref.dtype)
        exchange = Exchange(
            "dp",
            crowd,
            crowds,
            lambda p: ref.at[crowd],
            lambda p: ref.at[p],
            send,
            recv,
            device=lambda p: p * group + part_id,
        )
        exchange.start()
        exchange.arrive()
        far_x.append(exchange)
        total = ref[0].astype(F32)
        for peer in range(1, crowds):
            total = total + ref[peer].astype(F32)
        return total

    out_swap.wait_send()
    normed_all = s.normed[...].reshape(L, D)
    for index in range(3):
        value = mm_tn(s.grad_proj[index], normed_all)
        for piece in range(group):
            s.gsum[piece // quarters, piece % quarters, index] = value[
                piece * part : (piece + 1) * part, :
            ].astype(BF)
    swap = to_mate(s.gsum.at[1 - core, :, 0:3], s.wswap, 1)
    swap.start()
    first_x.pass_on()
    swap.wait_recv()
    s.wswap[...] = (s.gsum[core, :, 0:3].astype(F32) + s.wswap[...].astype(F32)).astype(BF)
    pair_x = over_chips(lambda p: s.wswap.at[p], lambda p: s.wparts.at[p], s.pair_s, s.pair_r)
    pair_x.start()
    s.wparts[quarter] = s.wswap[quarter]
    total = add_chips(out_x, s.gparts)
    if crowds > 1:
        total = add_crowds(total, s.out_far, s.outf_s, s.outf_r)
    s.out_piece[...] = total.astype(BF)
    out_zx = over_z(lambda p: s.out_piece.at[p], lambda p: s.out_pieces.at[p], s.outz_s, s.outz_r)
    out_zx.start()
    s.out_pieces[z] = s.out_piece[z]
    for f in range(2, NF):
        fore_step(f)
    total = add_chips(early_x, s.early_dp)
    if crowds > 1:
        total = add_crowds(total, s.early_far, s.earlyf_s, s.earlyf_r)
    s.early_z[z] = total
    early_zx = over_z(lambda p: s.early_z.at[z], lambda p: s.early_z.at[p], s.earlyz_s, s.earlyz_r)
    early_zx.start()

    grad_first = first_x.total()
    normal_one = s.normal_one[...]
    s.late[...] = jnp.concatenate(
        [
            jnp.sum(grad_first * normal_one, axis=0, keepdims=True),
            jnp.sum(grad_first, axis=0, keepdims=True),
            jnp.zeros((6, D), F32),
        ],
        axis=0,
    )
    late_x = Exchange("dp", d, S, lambda p: s.late, lambda p: s.late_dp.at[p], s.late_s, s.late_r)
    late_x.start()
    s.late_dp[d] = s.late[...]
    total = add_chips(pair_x, s.wparts)
    if crowds > 1:
        total = add_crowds(total, s.w_far, s.wf_s, s.wf_r)
    s.wfull[core, quarter, 0:3] = total.astype(BF)
    out_zx.arrive()
    total = s.out_pieces[0].astype(F32)
    for j in range(1, n):
        total = total + s.out_pieces[j].astype(F32)
    s.wfull[core, quarter, 3] = total.astype(BF)
    full_x = over_chips(
        lambda p: s.wfull.at[core, quarter], lambda p: s.wfull.at[core, p], s.full_s, s.full_r
    )
    full_x.start()
    own_back = to_mate(s.wfull.at[core, quarter], s.wfull.at[core, quarter], 5)
    own_back.start()
    late_x.arrive()
    total = s.late_dp[0]
    for peer in range(1, S):
        total = total + s.late_dp[peer]
    s.late_z[z] = total
    late_zx = over_z(lambda p: s.late_z.at[z], lambda p: s.late_z.at[p], s.latez_s, s.latez_r)
    late_zx.start()
    for f in range(2, NF):
        fore_sums[f].pass_on()
    input_grad[...] = s.grad_residual[...] + norm_back(
        grad_first, normal_one, s.inverse_one[:, 0:1], first_gain[...].reshape(1, D)
    )
    early_zx.arrive()
    total = s.early_z[0]
    for j in range(1, n):
        total = total + s.early_z[j]
    s.early_all[core] = total
    early_back = to_mate(s.early_all.at[core], s.early_all.at[core], 4)
    early_back.start()
    backs = [own_back]
    for turn in range(1, quarters):
        peer = lax.rem(quarter + turn, quarters)
        full_x.copy(peer, peer).wait_recv()
        backs.append(to_mate(s.wfull.at[core, peer], s.wfull.at[core, peer], 5 + turn))
        backs[-1].start()

    block_out[...] = s.residual[...] + add_sums(fore_sums)
    to_mate(s.early_all.at[core], s.early_all.at[1 - core], 4).wait_recv()
    for side in range(2):
        vec_out[0 : E + 8, side * H : (side + 1) * H] = s.early_all[side]
    late_zx.arrive()
    total = s.late_z[0]
    for j in range(1, n):
        total = total + s.late_z[j]
    vec_out[E + 8 : E + 16, :] = total
    for turn in range(quarters):
        peer = lax.rem(quarter + turn, quarters)
        to_mate(s.wfull.at[core, peer], s.wfull.at[1 - core, peer], 5 + turn).wait_recv()
    sums_store = pltpu.make_async_copy(s.wfull, weights_out, s.store_sem.at[2])
    sums_store.start()
    stores.append(sums_store)

    for store in stores:
        store.wait()
    for copy in [swap, early_swap, early_back] + backs:
        copy.wait_send()
    for lines in (normed_lines, second_lines) if cfg["tight"] else (normed_lines, cot_lines, second_lines):
        for line in lines:
            line.finish()
    done = [routes_x, outw_x, gate_x, dot_x, delta_x, early_x, pair_x, early_zx, full_x, first_x, late_x]
    if not cfg["tight"]:
        done += cot_x + row_x + down_sums
    done += far_x + [late_zx, back_x, out_x, out_zx] + plane + down_x + fore_x + fore_sums
    for exchange in done:
        exchange.finish()


def hand_over(E, *refs):
    given, vecs = refs[:5], refs[5]
    large, small = refs[6:12], refs[12:17]
    held, narrow, wide, load_sem, store_sem = refs[17:21], refs[21], refs[22], refs[23], refs[24]
    loads = [
        pltpu.make_async_copy(given[index], (list(held) + [narrow])[index], load_sem.at[index])
        for index in range(5)
    ]
    for load in (loads[4], *loads[:4]):
        load.start()
    sources = [*held, wide.at[0:3], wide.at[3]]
    stores = [
        pltpu.make_async_copy(sources[index], large[index], store_sem.at[index]) for index in range(6)
    ]
    small[0][...] = vecs[0:E, :]
    D = vecs.shape[1]
    for index, row in enumerate((E + 8, E + 9, E, E + 1)):
        small[1 + index][...] = vecs[row : row + 1, :].reshape(D)
    loads[4].wait()
    part = narrow.shape[2]
    for piece in range(narrow.shape[0]):
        wide[:, piece * part : (piece + 1) * part, :] = narrow[piece].astype(F32)
    stores[4].start()
    stores[5].start()
    for index in range(4):
        loads[index].wait()
        stores[index].start()
    for store in stores:
        store.wait()


class Names:
    pass


def shards(
    block_in,
    first_gain,
    first_bias,
    qkv_weight,
    out_weight,
    second_gain,
    second_bias,
    router_weight,
    frozen_in,
    frozen_out,
    train_in,
    train_out,
    routes,
    seq_ids,
    cotangent,
):
    T, D = block_in.shape
    L = seq_ids.shape[0]
    E = router_weight.shape[1]
    S, n = lax.axis_size("dp"), lax.axis_size("head")
    W = qkv_weight.shape[2]
    HID = frozen_in.shape[2]
    cap = max(2, 5 * T // (2 * E))
    R = -(-(n * cap) // 8) * 8
    M = E * R
    NF = D // FW
    group = 8
    quarters = group // 2
    part = W // group
    crowds = S // group
    tight = S > group
    cfg = dict(tight=tight, n=n, S=S, T=T, D=D, L=L, E=E, R=R, W=W, HID=HID, cap=cap, group=group)
    DMA = pltpu.SemaphoreType.DMA
    scratch = dict(
        experts=VMEM((4, D, HID), BF),
        normal_one=VMEM((T, D), F32),
        inverse_one=VMEM((T, 128), F32),
        normed=VMEM((n, T, D), BF),
        cots=VMEM((NF, n, T, FW), BF),
        routes=VMEM((n, 2, T), jnp.int32),
        outw=VMEM((n, group, W // group, D), BF),
        qkv=VMEM((3, L, W), BF),
        target=VMEM((n, 8, T), jnp.int32),
        gates=VMEM((n, 8, T), F32),
        place=VMEM((M, L), BF),
        combine=VMEM((L, M), BF),
        probs=VMEM((W // HEAD_DIM, L, L), BF),
        mixed=VMEM((n, T, W), BF),
        mixed_in=VMEM((n, T, W), BF),
        residual=VMEM((T, D), F32),
        normal_two=VMEM((T, D), F32),
        inverse_two=VMEM((T, 128), F32),
        second=VMEM((NF, n, T, FW), BF),
        cot_out=VMEM((NF, S, 2, R, FW), BF),
        cot_in=VMEM((NF, 2, S, R, FW), BF),
        row_out=VMEM((NF, S, 2, R, FW), BF),
        row_in=VMEM((NF, 2, S, R, FW), BF),
        gate_out=VMEM((S, 8, 128), F32),
        gate_in=VMEM((S, 8, 128), F32),
        hidden=VMEM((2 * S * R, HID), F32),
        grad_active=VMEM((2 * S * R, HID), F32),
        active=VMEM((2, S * R, HID), BF),
        grad_hidden=VMEM((2, S * R, HID), BF),
        dot_out=VMEM((S, 8, 128), F32),
        dot_in=VMEM((S, 8, 128), F32),
        down_out=VMEM((NF, S, 2, R, FW), BF),
        down_in=VMEM((NF, S, 2, R, FW), BF),
        fore_out=VMEM((NF, S, 2, R, FW), BF),
        fore_in=VMEM((NF, S, 2, R, FW), BF),
        down_part=VMEM((NF, n, T, FW), BF),
        down_sum=VMEM((NF, n, T, FW), BF),
        fore_part=VMEM((NF, n, T, FW), BF),
        fore_sum=VMEM((NF, n, T, FW), BF),
        delta_out=VMEM((n, 8, T), F32),
        delta_in=VMEM((n, 8, T), F32),
        early=VMEM((2, E + 8, D // 2), F32),
        early_mate=VMEM((E + 8, D // 2), F32),
        early_dp=VMEM((quarters, E + 8, D // 2), F32),
        early_z=VMEM((n, E + 8, D // 2), F32),
        early_all=VMEM((2, E + 8, D // 2), F32),
        late=VMEM((8, D), F32),
        late_dp=VMEM((S, 8, D), F32),
        late_z=VMEM((n, 8, D), F32),
        grad_residual=VMEM((T, D), F32),
        branch=VMEM((T, D), BF),
        grad_mixed=VMEM((n, T, W), BF),
        grad_proj=VMEM((3, L, W), BF),
        grad_kv=VMEM((2, L, W), F32),
        first_out=VMEM((n, T, D), BF),
        first_relay=VMEM((T, D), BF),
        drelay=VMEM((NF, T, FW), BF),
        frelay=VMEM((NF, T, FW), BF),
        first_in=VMEM((n, T, D), BF),
        gsum=VMEM((2, quarters, n, part, D), BF),
        gswap=VMEM((quarters, n, part, D), BF),
        gparts=VMEM((quarters, n, part, D), BF),
        out_piece=VMEM((n, part, D), BF),
        out_pieces=VMEM((n, part, D), BF),
        wswap=VMEM((quarters, 3, part, D), BF),
        wparts=VMEM((quarters, 3, part, D), BF),
        wfull=VMEM((2, quarters, 4, part, D), BF),
        load_sem=DMA((4,)),
        store_sem=DMA((3,)),
        swap_s=DMA((5 + quarters,)),
        swap_r=DMA((5 + quarters,)),
        routes_s=DMA((n,)),
        routes_r=DMA((n,)),
        normed_s=DMA((2, 2, n)),
        normed_r=DMA((2, n)),
        cot_s=DMA((NF, 2, n)),
        cot_r=DMA((NF, n)),
        outw_s=DMA((n,)),
        outw_r=DMA((n,)),
        outw_ps=DMA((n, group)),
        outw_pr=DMA((n, group)),
        mixed_s=DMA((n,)),
        mixed_r=DMA((n,)),
        cotx_s=DMA((NF, S)),
        cotx_r=DMA((NF, S)),
        rowx_s=DMA((NF, S)),
        rowx_r=DMA((NF, S)),
        second_s=DMA((NF, 2, n)),
        second_r=DMA((NF, n)),
        gate_s=DMA((S,)),
        gate_r=DMA((S,)),
        dot_s=DMA((S,)),
        dot_r=DMA((S,)),
        down_s=DMA((NF, S)),
        down_r=DMA((NF, S)),
        fore_s=DMA((NF, S)),
        fore_r=DMA((NF, S)),
        dsum_s=DMA((NF, n)),
        dsum_r=DMA((NF, n)),
        fsum_s=DMA((NF, n)),
        fsum_r=DMA((NF, n)),
        delta_s=DMA((n,)),
        delta_r=DMA((n,)),
        back_s=DMA((n,)),
        back_r=DMA((n,)),
        outp_s=DMA((quarters,)),
        outp_r=DMA((quarters,)),
        outz_s=DMA((n,)),
        outz_r=DMA((n,)),
        early_s=DMA((quarters,)),
        early_r=DMA((quarters,)),
        earlyz_s=DMA((n,)),
        earlyz_r=DMA((n,)),
        first_relay_sem=DMA((2,)),
        drelay_sem=DMA((NF, 2)),
        frelay_sem=DMA((NF, 2)),
        first_s=DMA((n,)),
        first_r=DMA((n,)),
        pair_s=DMA((quarters,)),
        pair_r=DMA((quarters,)),
        full_s=DMA((quarters,)),
        full_r=DMA((quarters,)),
        late_s=DMA((S,)),
        late_r=DMA((S,)),
        latez_s=DMA((n,)),
        latez_r=DMA((n,)),
    )
    if crowds > 1:
        scratch.update(
            early_far=VMEM((crowds, E + 8, D // 2), F32),
            earlyf_s=DMA((crowds,)),
            earlyf_r=DMA((crowds,)),
            out_far=VMEM((crowds, n, part, D), BF),
            outf_s=DMA((crowds,)),
            outf_r=DMA((crowds,)),
            w_far=VMEM((crowds, 3, part, D), BF),
            wf_s=DMA((crowds,)),
            wf_r=DMA((crowds,)),
        )
    if tight:
        del scratch["down_out"], scratch["fore_out"], scratch["fore_part"], scratch["down_part"]
    names = list(scratch)

    def kernel(*refs):
        space = Names()
        for name, ref in zip(names, refs[21:]):
            setattr(space, name, ref)
        body(*refs[:21], space, cfg)

    whole = pl.BlockSpec(memory_space=VMEM)
    left = pl.BlockSpec(memory_space=pl.ANY)
    outs = pl.pallas_call(
        kernel,
        out_shape=(
            jax.ShapeDtypeStruct((T, D), F32),
            jax.ShapeDtypeStruct((T, D), F32),
            jax.ShapeDtypeStruct((E + 16, D), F32),
            jax.ShapeDtypeStruct((2, quarters, 4, part, D), BF),
            jax.ShapeDtypeStruct((1, D, HID), F32),
            jax.ShapeDtypeStruct((1, HID, D), F32),
        ),
        in_specs=[whole] * 8 + [left] * 4 + [whole] * 3,
        out_specs=(whole, whole, whole, left, left, left),
        scratch_shapes=list(scratch.values()),
        compiler_params=pltpu.CompilerParams(
            collective_id=0, has_side_effects=True, vmem_limit_bytes=67043328
        ),
    )(
        block_in,
        first_gain,
        first_bias,
        jnp.swapaxes(qkv_weight, 1, 2),
        out_weight,
        second_gain,
        second_bias,
        router_weight.T,
        frozen_in,
        frozen_out,
        train_in,
        train_out,
        routes.T,
        seq_ids.reshape(1, L),
        cotangent,
    )
    block_out, input_grad, vecs, sums, grad_train_in, grad_train_out = outs
    sums = sums.reshape(group, 4, part, D)
    big = [block_out, input_grad, grad_train_in, grad_train_out]
    vector = jax.ShapeDtypeStruct((D,), F32)
    done = pl.pallas_call(
        functools.partial(hand_over, E),
        out_shape=[jax.ShapeDtypeStruct(array.shape, F32) for array in big]
        + [
            jax.ShapeDtypeStruct((3, W, D), F32),
            jax.ShapeDtypeStruct((W, D), F32),
            jax.ShapeDtypeStruct((E, D), F32),
        ]
        + [vector] * 4,
        in_specs=[left] * 5 + [whole],
        out_specs=[left] * 6 + [whole] * 5,
        scratch_shapes=[VMEM(array.shape, F32) for array in big]
        + [VMEM((group, 4, part, D), BF), VMEM((4, W, D), F32), DMA((5,)), DMA((6,))],
        compiler_params=pltpu.CompilerParams(vmem_limit_bytes=67043328),
    )(*big, sums, vecs)
    block_out, input_grad, grad_train_in, grad_train_out, grad_qkv, grad_out, grad_router = done[:7]
    return (
        block_out,
        input_grad,
        done[7],
        done[8],
        jnp.swapaxes(grad_qkv, 1, 2),
        grad_out,
        done[9],
        done[10],
        grad_router.T,
        grad_train_in,
        grad_train_out,
    )


def solution(mesh):
    return jax.shard_map(
        shards,
        mesh=mesh,
        in_specs=(
            P(("dp", "head"), None),
            P(),
            P(),
            P(None, None, "head"),
            P("head", None),
            P(),
            P(),
            P(),
            P("dp", None, "head"),
            P("dp", "head", None),
            P("dp", None, "head"),
            P("dp", "head", None),
            P(("dp", "head"), None),
            P("dp"),
            P(("dp", "head"), None),
        ),
        out_specs=(
            P(("dp", "head"), None),
            P(("dp", "head"), None),
            P(),
            P(),
            P(None, None, "head"),
            P("head", None),
            P(),
            P(),
            P(),
            P("dp", None, "head"),
            P("dp", "head", None),
        ),
        check_vma=False,
    )
```
